256 devices in a mesh: grp: 8 (over y, core), shard: 32 (over z, x).
Axes of the slice: x: 4, y: 4, z: 8, core: 2. Of those that a mesh axis runs over, the one named last changes fastest.
Arguments:
- table: float32 [131072, 256], P('shard'), may hold values from -6 to 6
- accum: float32 [131072], P('shard'), may hold values from 0.05 to 2
- pooled_grad: bfloat16 [8, 32, 512, 256], P('grp', 'shard'), may hold values from -6 to 6
- row_ids: int32 [8, 32, 4096], P('grp', 'shard'), may hold values from 0 to 131071, as said below
- bag_ids: int32 [8, 32, 4096], P('grp', 'shard'), may hold values from 0 to 511, never falling along the last dimension, each value on 1 to 16 neighbouring positions
- touched: int32 [32, 1024], P('shard'), may hold values from 0 to 4095, as said below
Outputs:
- new_table: float32 [131072, 256], P('shard')
- new_accum: float32 [131072], P('shard')
The draws below stay inside these ranges and needn't reach their ends.
Inputs may be any that keep to these rules, and one draw needn't show every extreme that they name: `row_ids`: every id is s * 4096 + touched[s, k] for some shard s and some k: it lies in a listed row. At most 512 lookups of one device fall on one shard s (ids in s * 4096 to (s + 1) * 4096 - 1); in every draw some device sends exactly 512 to some shard, and in each replica one shard receives 512 from every device of that replica. Each row of touched holds 1024 distinct row numbers in increasing order.
All inputs are finite; a program needn't handle non-finite values.
Results may differ from the reference program's by a relative error of at most 0.0003.
Values may be sent and summed in bfloat16 or wider, within the bound.
No kernel may reach another device: no remote copies, remote signals or barrier semaphores. Data moves between devices by JAX's collectives and lax.ppermute only.
A program may use at most 128 MiB of HBM per device.

```python
import math
import jax
import jax.numpy as jnp
import numpy as np
from jax import lax

E = 256
ROWS_DEV = 4096
TOUCH = 1024
LOOK_DEV = 4096
POOL = 8
B_DEV = 512
CAP = 512
ROWS = 131072
N_GRP = 8
N_SHARD = 32


def listed_table(key):
    keys = jax.random.split(jax.random.fold_in(key, 11), N_SHARD)

    def one_shard(shard_key):
        return jnp.sort(jax.random.permutation(shard_key, ROWS_DEV)[:TOUCH]).astype(jnp.int32)
    return jax.vmap(one_shard)(keys)


def draw_touched(key, part):
    return listed_table(key)


def draw_row_ids(key, part):
    listed = listed_table(key)
    base_key = jax.random.fold_in(key, 23)
    hot = jax.random.randint(jax.random.fold_in(base_key, 1), (N_GRP,), 0, N_SHARD)
    offsets = jax.random.randint(jax.random.fold_in(base_key, 2), (N_GRP, N_SHARD), 0, N_SHARD - 1)
    position = jnp.arange(LOOK_DEV - CAP, dtype=jnp.int32)
    hot_full = hot[:, None, None]
    others = (hot_full + 1 + (position[None, None, :] + offsets[:, :, None]) % (N_SHARD - 1)) % N_SHARD
    hot_part = jnp.broadcast_to(hot_full, (N_GRP, N_SHARD, CAP))
    owners = jnp.concatenate([hot_part, others], axis=2).reshape(N_GRP * N_SHARD, LOOK_DEV)
    perm_keys = jax.random.split(jax.random.fold_in(base_key, 3), N_GRP * N_SHARD)
    orders = jax.vmap(lambda perm_key: jax.random.permutation(perm_key, LOOK_DEV))(perm_keys)
    owners = jnp.take_along_axis(owners, orders, axis=1).reshape(N_GRP, N_SHARD, LOOK_DEV)
    picks = jax.random.randint(jax.random.fold_in(base_key, 4), (N_GRP, N_SHARD, LOOK_DEV), 0, TOUCH)
    local_rows = listed[owners, picks]
    return (owners * ROWS_DEV + local_rows).astype(jnp.int32)


def levels(rng, shape, cuts, least, top_value):
    level = 1.0
    for axis_at, parts in cuts:
        draws = jax.random.uniform(jax.random.fold_in(jax.random.fold_in(rng, 6), axis_at), (parts,), jnp.float32, least / len(cuts), top_value / len(cuts))
        level = level * jnp.repeat(jnp.exp(draws), shape[axis_at] // parts).reshape((-1,) + (1,) * (len(shape) - 1 - axis_at))
    return level


def length_profile(amount, total, reach, lean):
    portions = [(1 << 20) // math.isqrt(rank ** lean) + 1 for rank in range(2, amount + 1)]
    spare, counts = total - reach - (amount - 1), [1] * (amount - 1)
    while spare > 0:
        free = [i for i in range(amount - 1) if counts[i] < reach]
        pool, remaining = sum([portions[i] for i in free]), spare
        for i in free:
            addition = min(reach - counts[i], max(1, remaining * portions[i] // pool), spare)
            counts[i] = counts[i] + addition
            spare = spare - addition
    return np.array([reach] + counts)


def uneven(key, count, total, limit, slope):
    if count == 2:
        one = jax.random.randint(key, (), max(1, total - limit), min(limit, total - 1) + 1)
        return jnp.stack([one, total - one])
    tallies = jnp.asarray(length_profile(count, total, limit, slope), jnp.int32)
    couples = (count - 1) // 2
    donor, sink = tallies[1:1 + 2 * couples:2], tallies[2:2 + 2 * couples:2]
    margin = jnp.minimum(donor - 1, limit - sink)
    passed = jax.random.randint(jax.random.fold_in(key, 1), (couples,), 0, 1 << 20) % (margin + 1)
    tallies = tallies.at[1:1 + 2 * couples:2].set(donor - passed).at[2:2 + 2 * couples:2].set(sink + passed)
    return tallies[jax.random.permutation(jax.random.fold_in(key, 2), count)]


def bell_draw(own_key, dims, width, reach, pieces=(), held_as=jnp.bfloat16):
    gain = levels(own_key, dims, pieces, -0.22, 0.18) if pieces else 1.0
    entries = jax.random.normal(own_key, dims, jnp.float32) * width * gain
    return jnp.minimum(jnp.maximum(entries, -reach), reach).astype(held_as)


def setup_inputs(seed: int = 0) -> dict:
    key_of = jax.random.split(jax.random.key(seed), 7)
    return {
        "table": bell_draw(key_of[0], (ROWS, E), 1.0, 6.0, ((0, 32),), jnp.float32),
        "accum": jnp.clip(jnp.exp(math.log(2.0) - 3.6888794 * jax.random.uniform(key_of[1], (ROWS,), jnp.float32) ** levels(key_of[1], (ROWS,), ((0, 32),), -0.2, 0.2)), 0.05, 2.0),
        "pooled_grad": bell_draw(key_of[2], (N_GRP, N_SHARD, B_DEV, E), 1.0, 6.0, ((0, 8), (1, 32))),
        "row_ids": draw_row_ids(jax.random.fold_in(key_of[6], 71), 0),
        "bag_ids": jax.vmap(lambda own: jnp.searchsorted(jnp.cumsum(uneven(own, B_DEV, LOOK_DEV, 2 * POOL, 0)), jnp.arange(LOOK_DEV), side="right"))(jax.random.split(key_of[4], N_GRP * N_SHARD)).reshape((N_GRP, N_SHARD, LOOK_DEV)).astype(jnp.int32),
        "touched": draw_touched(jax.random.fold_in(key_of[6], 71), 0),
    }


def reference(table, accum, pooled_grad, row_ids, bag_ids, touched):
    devices_all = N_GRP * N_SHARD
    grads = pooled_grad.reshape(devices_all, B_DEV, E)
    samples = bag_ids.reshape(devices_all, LOOK_DEV)
    values = jax.vmap(lambda grad_block, sample_ids: jnp.take(grad_block, sample_ids, axis=0))(grads, samples)
    values = values.reshape(-1, E).astype(jnp.float32)
    flat_ids = row_ids.reshape(-1)
    dense = jnp.zeros((ROWS, E), jnp.float32).at[flat_ids].add(values)
    shard_base = (jnp.arange(N_SHARD, dtype=jnp.int32) * ROWS_DEV)[:, None]
    listed_rows = (touched + shard_base).reshape(-1).astype(jnp.int32)
    keep = jnp.zeros((ROWS,), jnp.float32).at[listed_rows].set(1.0)
    grad_rows = dense * keep[:, None]
    new_accum = accum + lax.optimization_barrier(jnp.mean(grad_rows * grad_rows, axis=1))
    new_table = table - 0.5 * grad_rows / (jnp.sqrt(new_accum)[:, None] + 1e-08)
    return (new_table, new_accum)
```

```python
import jax
import jax.numpy as jnp
from jax import lax
from jax.experimental import pallas as pl
from jax.experimental.pallas import tpu as pltpu
from jax.sharding import PartitionSpec as P

E = 256
ROWS_DEV = 4096
TOUCH = 1024
HALF = TOUCH // 2
QUART = TOUCH // 8
LOOK = 4096
B_DEV = 512
LANES = 128
BLOCKS = 64
KEY_ROWS = 72
NZ, NX, NY, NC = 8, 4, 4, 2
F32 = jnp.float32
BF16 = jnp.bfloat16
I32 = jnp.int32
NT = (((1,), (1,)), ((), ()))
TN = (((0,), (0,)), ((), ()))


def iota(shape, dim):
    return lax.broadcasted_iota(I32, shape, dim)


def one_hot(mask):
    return jnp.where(mask, 1.0, 0.0).astype(BF16)


def pack_kernel(ids_ref, bags_ref, g_ref, keys_ref, gt_ref, a_ref, b_ref, o_ref):
    groups = LOOK // LANES
    ids = ids_ref[...]
    owner = ids >> 12
    owners = iota((32, LANES), 0)
    running = jnp.zeros((32, LANES), F32)
    for i in range(groups):
        hit = jnp.where(owner[i:i + 1, :] == owners, 1.0, 0.0)
        o_ref[i * 32:(i + 1) * 32, 0:LANES] = hit.astype(BF16)
        o_ref[i * 32:(i + 1) * 32, LANES:2 * LANES] = running.astype(BF16)
        running = running + hit
    before = one_hot(iota((LANES, LANES), 0) < iota((LANES, LANES), 1))
    weights = jnp.concatenate([before, jnp.ones((LANES, LANES), BF16)], axis=0)
    prefix = jnp.dot(o_ref[...], weights, preferred_element_type=F32)
    totals = jnp.concatenate([running, jnp.zeros((LANES - 32, LANES), F32)], axis=0)
    count_row = lax.dot_general(jnp.ones((8, LANES), BF16), totals.astype(BF16), NT,
                                preferred_element_type=F32).astype(I32)
    blocks_row = (count_row + (LANES - 1)) >> 7
    start_row = jnp.dot(blocks_row.astype(F32).astype(BF16), before, preferred_element_type=F32)
    start_col = jnp.sum(
        jnp.where(iota((32, LANES), 1) < iota((32, LANES), 0),
                  jnp.broadcast_to(blocks_row[0:1, :].astype(F32), (32, LANES)), 0.0),
        axis=1, keepdims=True) * float(LANES)
    start_all = jnp.broadcast_to(start_col, (32, LANES))
    for i in range(groups):
        hit = owner[i:i + 1, :] == owners
        pos = jnp.sum(jnp.where(hit, prefix[i * 32:(i + 1) * 32, :] + start_all, 0.0),
                      axis=0, keepdims=True).astype(I32)
        key = (((ids[i:i + 1, :] & (ROWS_DEV - 1)) << 9) | bags_ref[i:i + 1, :]) + 1
        at_hi = (pos >> 7) == iota((BLOCKS, LANES), 0)
        for piece in range(3):
            part = ((key >> (8 * piece)) & 255).astype(F32)
            a_ref[piece * BLOCKS:(piece + 1) * BLOCKS, i * LANES:(i + 1) * LANES] = jnp.where(
                at_hi, part, 0.0).astype(BF16)
        b_ref[:, i * LANES:(i + 1) * LANES] = one_hot((pos & (LANES - 1)) == iota((LANES, LANES), 0))
    placed = lax.dot_general(a_ref[...], b_ref[...], NT, preferred_element_type=F32).astype(I32)
    keys = (placed[0:BLOCKS] + (placed[BLOCKS:2 * BLOCKS] << 8)
            + (placed[2 * BLOCKS:3 * BLOCKS] << 16)) - 1
    keys_ref[0:BLOCKS, :] = keys
    keys_ref[BLOCKS:KEY_ROWS, :] = jnp.where(iota((8, LANES), 0) == 0, start_row.astype(I32), blocks_row)
    eye = one_hot(iota((E, E), 0) == iota((E, E), 1))
    gt_ref[...] = lax.dot_general(eye, g_ref[...], NT, preferred_element_type=F32).astype(BF16)


def pack(ids, bags, grads):
    return pl.pallas_call(
        pack_kernel,
        out_shape=(jax.ShapeDtypeStruct((KEY_ROWS, LANES), I32),
                   jax.ShapeDtypeStruct((E, B_DEV), BF16)),
        scratch_shapes=[pltpu.VMEM((3 * BLOCKS, LOOK), BF16),
                        pltpu.VMEM((LANES, LOOK), BF16),
                        pltpu.VMEM((TOUCH, 2 * LANES), BF16)],
        name="pack",
    )(ids, bags, grads)


def owner_kernel(*refs):
    meta_ref, shard_ref, rows_ref = refs[0:3]
    gts = refs[3:3 + NZ]
    keys = refs[3 + NZ:3 + 2 * NZ]
    send_ref, keep_ref, x_ref, k_ref = refs[3 + 2 * NZ:]
    shard = shard_ref[0]
    filled = jnp.int32(0)
    for d in range(NZ):
        first = meta_ref[2 * d, shard]
        many = meta_ref[2 * d + 1, shard]

        def gather(j, _, d=d, first=first, filled=filled):
            row = keys[d][pl.ds(first + j, 1), :]
            bag = row & (B_DEV - 1)
            picks = one_hot(bag == iota((B_DEV, LANES), 0))
            slot = filled + j
            x_ref[slot] = jnp.dot(gts[d][...], picks, preferred_element_type=F32).astype(BF16)
            k_ref[pl.ds(slot, 1), :] = row >> 9
            return 0

        lax.fori_loop(0, many, gather, 0)
        filled = filled + many
    rounds = (filled + 3) >> 2

    def blank(j, _):
        x_ref[j] = jnp.zeros((E, LANES), BF16)
        k_ref[pl.ds(j, 1), :] = jnp.full((1, LANES), -1, I32)
        return 0

    lax.fori_loop(filled, rounds * 4, blank, 0)
    send_ref[...] = jnp.zeros((HALF, E), F32)
    keep_ref[...] = jnp.zeros((HALF, E), F32)

    def accumulate(r, _):
        xs = jnp.concatenate([x_ref[4 * r + j] for j in range(4)], axis=1)
        rows4 = [k_ref[pl.ds(4 * r + j, 1), :] for j in range(4)]
        for out_ref, base in ((send_ref, 0), (keep_ref, HALF)):
            mine = rows_ref[base:base + HALF, :]
            hits = jnp.concatenate([one_hot(mine == row) for row in rows4], axis=1)
            out_ref[...] += lax.dot_general(hits, xs, NT, preferred_element_type=F32)
        return 0

    lax.fori_loop(0, rounds, accumulate, 0)


def owner_sums(meta, shard, rows, gts, keys):
    smem = pl.BlockSpec(memory_space=pltpu.SMEM)
    vmem = pl.BlockSpec(memory_space=pltpu.VMEM)
    return pl.pallas_call(
        owner_kernel,
        out_shape=(jax.ShapeDtypeStruct((HALF, E), F32), jax.ShapeDtypeStruct((HALF, E), F32)),
        in_specs=[smem, smem, vmem] + [vmem] * (2 * NZ),
        scratch_shapes=[pltpu.VMEM((4 * NZ, E, LANES), BF16), pltpu.VMEM((4 * NZ, LANES), I32)],
        name="owner_sums",
    )(meta, shard, rows, *gts, *keys)


def listed_accum_kernel(rows_ref, accum_ref, out_ref):
    rows = rows_ref[...]
    hi = jnp.where((rows >> 7) == iota((TOUCH, LANES), 1), 1.0, 0.0)
    padded = jnp.concatenate([accum_ref[...], jnp.zeros((LANES - 32, LANES), F32)], axis=0)
    line = jnp.dot(hi, padded, precision=lax.Precision.HIGHEST, preferred_element_type=F32)
    mine = jnp.where((rows & (LANES - 1)) == iota((TOUCH, LANES), 1), line, 0.0)
    out_ref[...] = jnp.broadcast_to(jnp.sum(mine, axis=1, keepdims=True), (TOUCH, LANES))


def listed_accum(rows, accum):
    return pl.pallas_call(
        listed_accum_kernel,
        out_shape=jax.ShapeDtypeStruct((TOUCH, LANES), F32),
        name="listed_accum",
    )(rows, accum)


def update_kernel(*refs):
    list_ref, table_ref, accum_ref, listed_ref, rows_ref = refs[0:5]
    chunks = refs[5:13]
    table_out, accum_out, u_ref, lhs_ref, rhs_ref = refs[13:]
    lane = iota((QUART, LANES), 1)
    for n in range(8):
        at = slice(n * QUART, (n + 1) * QUART)
        g = chunks[n][...]
        mean = jnp.sum(g * g, axis=1, keepdims=True) * (1.0 / E)
        now = listed_ref[at, 0:1] + mean
        u_ref[at, :] = 0.5 * g / (jnp.sqrt(now) + 1e-08)
        rows = rows_ref[at, :]
        lhs_ref[at, :] = jnp.where((rows >> 7) == lane, mean, 0.0)
        rhs_ref[at, :] = jnp.where((rows & (LANES - 1)) == lane, 1.0, 0.0)
    added = lax.dot_general(lhs_ref[...], rhs_ref[...], TN, precision=lax.Precision.HIGHEST,
                            preferred_element_type=F32)
    accum_out[...] = accum_ref[...] + added[0:32, :]
    table_out[...] = table_ref[...]

    def step(i, _):
        for j in range(8):
            p = i * 8 + j
            row = list_ref[i >> 4, (i & 15) * 8 + j]
            table_out[pl.ds(row, 1), :] = table_out[pl.ds(row, 1), :] - u_ref[pl.ds(p, 1), :]
        return 0

    lax.fori_loop(0, TOUCH // 8, step, 0)


def update(order, table, accum, listed, rows, chunks):
    vmem = pl.BlockSpec(memory_space=pltpu.VMEM)
    return pl.pallas_call(
        update_kernel,
        out_shape=(jax.ShapeDtypeStruct((ROWS_DEV, E), F32), jax.ShapeDtypeStruct((32, LANES), F32)),
        in_specs=[pl.BlockSpec(memory_space=pltpu.SMEM)] + [vmem] * 12,
        scratch_shapes=[pltpu.VMEM((TOUCH, E), F32), pltpu.VMEM((TOUCH, LANES), F32),
                        pltpu.VMEM((TOUCH, LANES), F32)],
        name="update",
    )(order, table, accum, listed, rows, *chunks)


def z_pairs(k):
    return [(z * NX + x, ((z + k) % NZ) * NX + x) for z in range(NZ) for x in range(NX)]


def x_pairs(k):
    return [(z * NX + x, z * NX + (x + k) % NX) for z in range(NZ) for x in range(NX)]


def y_pairs(k):
    return [(y * NC + c, ((y + k) % NY) * NC + c) for y in range(NY) for c in range(NC)]


C_PAIRS = [(y * NC + c, y * NC + 1 - c) for y in range(NY) for c in range(NC)]


def body(table, accum, pooled_grad, row_ids, bag_ids, touched):
    grp = lax.axis_index("grp")
    me = lax.axis_index("shard")
    y, c = grp // NC, grp % NC
    z, x = me // NX, me % NX
    keys, gt = pack(row_ids.reshape(32, LANES), bag_ids.reshape(32, LANES),
                    pooled_grad.reshape(B_DEV, E))
    gts, all_keys = [gt], [keys]
    for step in (1, -1):
        g_now, k_now = gt, keys
        for _ in range(NZ // 2 if step == 1 else NZ // 2 - 1):
            g_now = lax.ppermute(g_now, "shard", z_pairs(step))
            k_now = lax.ppermute(k_now, "shard", z_pairs(step))
            gts.append(g_now)
            all_keys.append(k_now)
    meta = jnp.concatenate([k[BLOCKS:BLOCKS + 2] for k in all_keys], axis=0)

    def ordered(listed):
        halves = listed.reshape(NC, NY, QUART)
        halves = jnp.where(c == 0, halves[::-1], halves)
        doubled = jnp.concatenate([halves, halves], axis=1)
        return lax.dynamic_slice(doubled, (0, y, 0), (NC, NY, QUART)).reshape(TOUCH)

    own_list = touched.reshape(TOUCH)
    lists = [ordered(own_list)]
    for k in range(1, NX):
        lists.append(ordered(lax.ppermute(own_list, "shard", x_pairs(-k))))
    rows = [jnp.broadcast_to(t[:, None], (TOUCH, LANES)) for t in lists]
    listed = listed_accum(rows[0], accum.reshape(32, LANES))

    arrived = []
    own = None
    for k in (2, 1, 3, 0):
        shard = (z * NX + (x + k) % NX).reshape(1)
        send, keep = owner_sums(meta, shard, rows[k], gts, all_keys)
        both = keep + lax.ppermute(send, "grp", C_PAIRS)
        if k:
            arrived.append(lax.ppermute(both, "shard", x_pairs(k)))
        else:
            own = both
    total = own + arrived[0] + arrived[1] + arrived[2]
    part = total[0:QUART]
    for j in range(1, NY):
        part = part + lax.ppermute(total[j * QUART:(j + 1) * QUART], "grp", y_pairs(j))
    mine = [part] + [lax.ppermute(part, "grp", y_pairs(-j)) for j in range(1, NY)]
    other = [lax.ppermute(m, "grp", C_PAIRS) for m in mine]
    new_table, new_accum = update(lists[0].reshape(8, LANES), table, accum.reshape(32, LANES),
                                  listed, rows[0], other + mine)
    return (new_table, new_accum.reshape(ROWS_DEV))


def solution(mesh):
    return jax.shard_map(
        body,
        mesh=mesh,
        in_specs=(
            P("shard", None),
            P("shard"),
            P("grp", "shard", None, None),
            P("grp", "shard", None),
            P("grp", "shard", None),
            P("shard", None),
        ),
        out_specs=(P("shard", None), P("shard")),
        check_vma=False,
    )
```

```python
import jax
import jax.numpy as jnp
from jax import lax
from jax.experimental import pallas as pl
from jax.experimental.pallas import tpu as pltpu
from jax.sharding import PartitionSpec as P


E = 256
ROWS_DEV = 4096
TOUCH = 1024
HALF = TOUCH // 2
QUART = TOUCH // 8
LOOK = 4096
B_DEV = 512
LANES = 128
BLOCKS = 128
KEY_ROWS = 24
NZ, NX, NY, NC = 8, 4, 4, 2
F32 = jnp.float32
BF16 = jnp.bfloat16
I32 = jnp.int32
NT = (((1,), (1,)), ((), ()))
TN = (((0,), (0,)), ((), ()))
FIRST_ROWS = pl.BlockSpec((1, TOUCH, LANES), lambda i: (0, 0, 0))


def iota(shape, dim):
    return lax.broadcasted_iota(I32, shape, dim)


def one_hot(mask):
    return jnp.where(mask, 1.0, 0.0).astype(BF16)


def pack_kernel(z_ref, ids_ref, bags_ref, keys_ref, a_ref, b_ref, o_ref):
    groups = LOOK // LANES
    ids = ids_ref[...]
    owner = ((ids >> 12) - NX * z_ref[0]) & (NZ * NX - 1)
    owners = iota((32, LANES), 0)
    running = jnp.zeros((32, LANES), F32)
    for i in range(groups):
        hit = jnp.where(owner[i:i + 1, :] == owners, 1.0, 0.0)
        o_ref[i * 32:(i + 1) * 32, 0:LANES] = hit.astype(BF16)
        o_ref[i * 32:(i + 1) * 32, LANES:2 * LANES] = running.astype(BF16)
        running = running + hit
    before = one_hot(iota((LANES, LANES), 0) < iota((LANES, LANES), 1))
    weights = jnp.concatenate([before, jnp.ones((LANES, LANES), BF16)], axis=0)
    prefix = jnp.dot(o_ref[...], weights, preferred_element_type=F32)
    counts = jnp.sum(running, axis=1, keepdims=True).astype(I32)
    blocks = jnp.broadcast_to((counts + (LANES - 1)) >> 7, (32, LANES))
    for i in range(groups):
        hit = owner[i:i + 1, :] == owners
        rank = jnp.sum(jnp.where(hit, prefix[i * 32:(i + 1) * 32, :], 0.0),
                       axis=0, keepdims=True).astype(I32)
        key = (((ids[i:i + 1, :] & (ROWS_DEV - 1)) << 9) | bags_ref[i:i + 1, :]) + 1
        at_hi = ((owner[i:i + 1, :] << 2) + (rank >> 7)) == iota((BLOCKS, LANES), 0)
        for piece in range(3):
            part = ((key >> (8 * piece)) & 255).astype(F32)
            a_ref[piece * BLOCKS:(piece + 1) * BLOCKS, i * LANES:(i + 1) * LANES] = jnp.where(
                at_hi, part, 0.0).astype(BF16)
        b_ref[:, i * LANES:(i + 1) * LANES] = one_hot((rank & (LANES - 1)) == iota((LANES, LANES), 0))
    placed = lax.dot_general(a_ref[...], b_ref[...], NT, preferred_element_type=F32).astype(I32)
    keys = (placed[0:BLOCKS] + (placed[BLOCKS:2 * BLOCKS] << 8)
            + (placed[2 * BLOCKS:3 * BLOCKS] << 16)) - 1
    for n in range(NZ):
        keys_ref[n, 0:16, :] = keys[16 * n:16 * (n + 1), :]
        keys_ref[n, 16:20, :] = blocks[4 * n:4 * (n + 1), :]
        keys_ref[n, 20:24, :] = blocks[4 * n:4 * (n + 1), :]


def pack(z, ids, bags):
    vmem = pl.BlockSpec(memory_space=pltpu.VMEM)
    return pl.pallas_call(
        pack_kernel,
        out_shape=jax.ShapeDtypeStruct((NZ, KEY_ROWS, LANES), I32),
        in_specs=[pl.BlockSpec(memory_space=pltpu.SMEM), vmem, vmem],
        scratch_shapes=[pltpu.VMEM((3 * BLOCKS, LOOK), BF16),
                        pltpu.VMEM((LANES, LOOK), BF16),
                        pltpu.VMEM((TOUCH, 2 * LANES), BF16)],
        cost_estimate=cost(4),
        name="pack",
    )(z, ids, bags)


def sums_kernel(*refs, sources, base, fresh):
    x_ref, refs = refs[0], list(refs[1:])
    take = lambda n: [refs.pop(0) for _ in range(n)]
    metas, grads, keys = take(sources), take(sources), take(sources)
    rows_ref = refs.pop(0)
    old_ref = None if fresh else refs.pop(0)
    gt_ref, xs_ref, k_ref = refs[-3:]
    outs = refs[:-3]
    if len(outs) == 1:
        outs = [outs[0].at[0, 0], outs[0].at[0, 1]]
    shard = pl.program_id(0)

    @pl.when(shard == 0)
    def _():
        eye = one_hot(iota((E, E), 0) == iota((E, E), 1))
        for d in range(sources):
            gt_ref[d] = lax.dot_general(eye, grads[d][...], NT, preferred_element_type=F32).astype(BF16)

    column = (x_ref[0] + base + shard) & (NX - 1)
    filled = jnp.int32(0)
    for d in range(sources):
        many = metas[d][column, 0]

        def gather(j, _, d=d, filled=filled):
            row = keys[d][pl.ds(4 * column + j, 1), :]
            picks = one_hot((row & (B_DEV - 1)) == iota((B_DEV, LANES), 0))
            slot = filled + j
            xs_ref[slot] = jnp.dot(gt_ref[d], picks, preferred_element_type=F32).astype(BF16)
            k_ref[pl.ds(slot, 1), :] = row >> 9
            return 0

        lax.fori_loop(0, many, gather, 0)
        filled = filled + many
    xs_ref[filled] = jnp.zeros((E, LANES), BF16)
    k_ref[pl.ds(filled, 1), :] = jnp.full((1, LANES), -1, I32)
    for h in range(2):
        outs[h][...] = jnp.zeros((HALF, E), F32) if fresh else old_ref[0, h]

    def accumulate(r, _):
        xs = jnp.concatenate([xs_ref[2 * r], xs_ref[2 * r + 1]], axis=1)
        pair = [k_ref[pl.ds(2 * r + j, 1), :] for j in range(2)]
        for h in range(2):
            mine = rows_ref[0, h * HALF:(h + 1) * HALF, :]
            hits = jnp.concatenate([one_hot(mine == row) for row in pair], axis=1)
            outs[h][...] += lax.dot_general(hits, xs, NT, preferred_element_type=F32)
        return 0

    lax.fori_loop(0, (filled + 1) >> 1, accumulate, 0)


def cost(us):
    return pl.CostEstimate(flops=int(us * 6e8), bytes_accessed=int(us * 3e6), transcendentals=0)


def sums(x, base, metas, grads, keys, rows, old, last):
    smem = pl.BlockSpec(memory_space=pltpu.SMEM)
    count = len(grads)
    whole = lambda shape: pl.BlockSpec(shape, lambda k: (0,) * len(shape))
    acc_spec = pl.BlockSpec((1, 2, HALF, E), lambda k: (base + k, 0, 0, 0))
    in_specs = ([smem] * (1 + count) + [whole((B_DEV, E))] * count + [whole((KEY_ROWS, LANES))] * count
                + [pl.BlockSpec((1, TOUCH, LANES), lambda k: (base + k, 0, 0))])
    if last:
        out_shape = [jax.ShapeDtypeStruct((HALF, E), F32)] * 2
        out_specs = [whole((HALF, E))] * 2
    else:
        out_shape = jax.ShapeDtypeStruct((NX, 2, HALF, E), F32)
        out_specs = acc_spec
    return pl.pallas_call(
        lambda *refs: sums_kernel(*refs, sources=count, base=base, fresh=old is None),
        grid=(1 if last else NX,),
        out_shape=out_shape,
        in_specs=in_specs + ([] if old is None else [acc_spec]),
        out_specs=out_specs,
        scratch_shapes=[pltpu.VMEM((count, E, B_DEV), BF16),
                        pltpu.VMEM((4 * count + 1, E, LANES), BF16),
                        pltpu.VMEM((4 * count + 8, LANES), I32)],
        cost_estimate=cost(3 if last else 6),
    )(x, *metas, *grads, *keys, rows, *([] if old is None else [old]))


def listed_kernel(list_ref, rows_ref, accum_ref, table_ref, accum_out, table_out):
    rows = rows_ref[0]
    hi = jnp.where((rows >> 7) == iota((TOUCH, LANES), 1), 1.0, 0.0)
    padded = jnp.concatenate([accum_ref[...], jnp.zeros((LANES - 32, LANES), F32)], axis=0)
    line = jnp.dot(hi, padded, precision=lax.Precision.HIGHEST, preferred_element_type=F32)
    mine = jnp.where((rows & (LANES - 1)) == iota((TOUCH, LANES), 1), line, 0.0)
    accum_out[...] = jnp.broadcast_to(jnp.sum(mine, axis=1, keepdims=True), (TOUCH, LANES))

    def step(i, _):
        for j in range(16):
            row = list_ref[i >> 3, (i & 7) * 16 + j]
            table_out[pl.ds(i * 16 + j, 1), :] = table_ref[pl.ds(row, 1), :]
        return 0

    lax.fori_loop(0, TOUCH // 16, step, 0)


def listed_values(order, rows, accum, table):
    vmem = pl.BlockSpec(memory_space=pltpu.VMEM)
    return pl.pallas_call(
        listed_kernel,
        out_shape=(jax.ShapeDtypeStruct((TOUCH, LANES), F32), jax.ShapeDtypeStruct((TOUCH, E), F32)),
        grid=(1,),
        in_specs=[pl.BlockSpec(memory_space=pltpu.SMEM), FIRST_ROWS, vmem, vmem],
        cost_estimate=cost(7),
        name="listed_values",
    )(order, rows, accum, table)


def update_kernel(*refs):
    list_ref, table_ref, accum_ref, listed_ref, old_ref, rows_ref = refs[0:6]
    chunks = refs[6:14]
    table_out, accum_out, new_ref, u_ref, lhs_ref, rhs_ref, sem = refs[14:]
    load = pltpu.make_async_copy(table_ref, new_ref, sem)
    load.start()
    lane = iota((QUART, LANES), 1)
    for n in range(8):
        at = slice(n * QUART, (n + 1) * QUART)
        g = chunks[n][...]
        mean = jnp.sum(g * g, axis=1, keepdims=True) * (1.0 / E)
        now = listed_ref[at, 0:1] + mean
        u_ref[at, :] = old_ref[at, :] - 0.5 * g / (jnp.sqrt(now) + 1e-08)
        rows = rows_ref[0, at, :]
        lhs_ref[at, :] = jnp.where((rows >> 7) == lane, mean, 0.0)
        rhs_ref[at, :] = jnp.where((rows & (LANES - 1)) == lane, 1.0, 0.0)
    added = lax.dot_general(lhs_ref[...], rhs_ref[...], TN, precision=lax.Precision.HIGHEST,
                            preferred_element_type=F32)
    accum_out[...] = accum_ref[...] + added[0:32, :]
    load.wait()

    def step(i, _):
        for j in range(16):
            row = list_ref[i >> 3, (i & 7) * 16 + j]
            new_ref[pl.ds(row, 1), :] = u_ref[pl.ds(i * 16 + j, 1), :]
        return 0

    lax.fori_loop(0, TOUCH // 16, step, 0)
    store = pltpu.make_async_copy(new_ref, table_out, sem)
    store.start()
    store.wait()


def update(order, table, accum, listed, old, rows, chunks):
    vmem = pl.BlockSpec(memory_space=pltpu.VMEM)
    hbm = pl.BlockSpec(memory_space=pl.ANY)
    return pl.pallas_call(
        update_kernel,
        out_shape=(jax.ShapeDtypeStruct((ROWS_DEV, E), F32), jax.ShapeDtypeStruct((32, LANES), F32)),
        grid=(1,),
        in_specs=[pl.BlockSpec(memory_space=pltpu.SMEM), hbm] + [vmem] * 3 + [FIRST_ROWS] + [vmem] * 8,
        out_specs=(hbm, vmem),
        scratch_shapes=[pltpu.VMEM((ROWS_DEV, E), F32), pltpu.VMEM((TOUCH, E), F32),
                        pltpu.VMEM((TOUCH, LANES), F32), pltpu.VMEM((TOUCH, LANES), F32),
                        pltpu.SemaphoreType.DMA],
        name="update",
    )(order, table, accum, listed, old, rows, *chunks)


def z_pairs(k):
    return [(z * NX + x, ((z + k) % NZ) * NX + x) for z in range(NZ) for x in range(NX)]


def x_pairs(k):
    return [(z * NX + x, z * NX + (x + k) % NX) for z in range(NZ) for x in range(NX)]


def y_pairs(k):
    return [(y * NC + c, ((y + k) % NY) * NC + c) for y in range(NY) for c in range(NC)]


C_PAIRS = [(y * NC + c, y * NC + 1 - c) for y in range(NY) for c in range(NC)]


def body(table, accum, pooled_grad, row_ids, bag_ids, touched):
    grp = lax.axis_index("grp")
    me = lax.axis_index("shard")
    y, c = grp // NC, grp % NC
    z, x = me // NX, me % NX
    grads = pooled_grad.reshape(B_DEV, E)

    def ordered(listed):
        halves = listed.reshape(NC, NY, QUART)
        halves = jnp.where(c == 0, halves[::-1], halves)
        doubled = jnp.concatenate([halves, halves], axis=1)
        return lax.dynamic_slice(doubled, (0, y, 0), (NC, NY, QUART)).reshape(TOUCH)

    own_list = touched.reshape(TOUCH)
    lists = [ordered(own_list)]
    for k in range(1, NX):
        lists.append(ordered(lax.ppermute(own_list, "shard", x_pairs(-k))))
    rows = jnp.broadcast_to(jnp.stack(lists)[:, :, None], (NX, TOUCH, LANES))

    keys = pack(z.reshape(1), row_ids.reshape(32, LANES), bag_ids.reshape(32, LANES))
    key_of = {0: keys[0]}
    for k in (1, -1, 2, -2, 3, -3, 4):
        key_of[-k] = lax.ppermute(keys[k % NZ], "shard", z_pairs(k))
    grad_of = {0: grads}
    for k in range(1, 5):
        grad_of[-k] = lax.ppermute(grad_of[1 - k], "shard", z_pairs(1))
        if k < 4:
            grad_of[k] = lax.ppermute(grad_of[k - 1], "shard", z_pairs(-1))

    order = lists[0].reshape(8, LANES)
    listed, old = listed_values(order, rows, accum.reshape(32, LANES), table)
    at = x.reshape(1)

    def add(sources, base, old, last):
        return sums(at, base, [key_of[d][16:24] for d in sources], [grad_of[d] for d in sources],
                    [key_of[d] for d in sources], rows, old, last)

    acc = add((0,), 0, None, False)
    acc = add((-1, 1), 0, acc, False)
    acc = add((-2, 2), 0, acc, False)
    acc = add((-3, 3), 0, acc, False)

    arrived = []
    own = None
    for k in (2, 1, 3, 0):
        send, keep = add((-4,), k, acc, True)
        both = keep + lax.ppermute(send, "grp", C_PAIRS)
        if k:
            arrived.append(lax.ppermute(both, "shard", x_pairs(k)))
        else:
            own = both
    total = own + arrived[0] + arrived[1] + arrived[2]
    part = total[0:QUART]
    for j in range(1, NY):
        part = part + lax.ppermute(total[j * QUART:(j + 1) * QUART], "grp", y_pairs(j))
    mine = [part] + [lax.ppermute(part, "grp", y_pairs(-j)) for j in range(1, NY)]
    other = [lax.ppermute(m, "grp", C_PAIRS) for m in mine]
    new_table, new_accum = update(order, table, accum.reshape(32, LANES),
                                  listed, old, rows, other + mine)
    return (new_table, new_accum.reshape(ROWS_DEV))


def solution(mesh):
    return jax.shard_map(
        body,
        mesh=mesh,
        in_specs=(
            P("shard", None),
            P("shard"),
            P("grp", "shard", None, None),
            P("grp", "shard", None),
            P("grp", "shard", None),
            P("shard", None),
        ),
        out_specs=(P("shard", None), P("shard")),
        check_vma=False,
    )
```

```python
import jax
import jax.numpy as jnp
from jax import lax
from jax.experimental import pallas as pl
from jax.experimental.pallas import tpu as pltpu
from jax.sharding import PartitionSpec as P


E = 256
ROWS_DEV = 4096
TOUCH = 1024
HALF = TOUCH // 2
QUART = TOUCH // 8
TILE = 512
LOOK = 4096
B_DEV = 512
LANES = 128
BLOCKS = 64
WIDTH = B_DEV + LANES
NZ, NX, NY, NC = 8, 4, 4, 2
F32 = jnp.float32
BF16 = jnp.bfloat16
I32 = jnp.int32
NT = (((1,), (1,)), ((), ()))
TN = (((0,), (0,)), ((), ()))
ORDER = (2, 1, 3, 0)
OWN_ROWS = pl.BlockSpec((1, TOUCH, LANES), lambda i: (3, 0, 0))


def iota(shape, dim):
    return lax.broadcasted_iota(I32, shape, dim)


def one_hot(mask):
    return jnp.where(mask, 1.0, 0.0).astype(BF16)


def pack_kernel(ids_ref, bags_ref, g_ref, out_ref, a_ref, b_ref, o_ref):
    groups = LOOK // LANES
    ids = ids_ref[...]
    owner = ids >> 12
    owners = iota((32, LANES), 0)
    running = jnp.zeros((32, LANES), F32)
    for i in range(groups):
        hit = jnp.where(owner[i:i + 1, :] == owners, 1.0, 0.0)
        o_ref[i * 32:(i + 1) * 32, 0:LANES] = hit.astype(BF16)
        o_ref[i * 32:(i + 1) * 32, LANES:2 * LANES] = running.astype(BF16)
        running = running + hit
    before = one_hot(iota((LANES, LANES), 0) < iota((LANES, LANES), 1))
    weights = jnp.concatenate([before, jnp.ones((LANES, LANES), BF16)], axis=0)
    prefix = jnp.dot(o_ref[...], weights, preferred_element_type=F32)
    totals = jnp.concatenate([running, jnp.zeros((LANES - 32, LANES), F32)], axis=0)
    count_row = lax.dot_general(jnp.ones((8, LANES), BF16), totals.astype(BF16), NT,
                                preferred_element_type=F32).astype(I32)
    blocks_row = (count_row + (LANES - 1)) >> 7
    start_row = jnp.dot(blocks_row.astype(F32).astype(BF16), before, preferred_element_type=F32)
    start_col = jnp.sum(
        jnp.where(iota((32, LANES), 1) < iota((32, LANES), 0),
                  jnp.broadcast_to(blocks_row[0:1, :].astype(F32), (32, LANES)), 0.0),
        axis=1, keepdims=True) * float(LANES)
    start_all = jnp.broadcast_to(start_col, (32, LANES))
    for i in range(groups):
        hit = owner[i:i + 1, :] == owners
        pos = jnp.sum(jnp.where(hit, prefix[i * 32:(i + 1) * 32, :] + start_all, 0.0),
                      axis=0, keepdims=True).astype(I32)
        key = (((ids[i:i + 1, :] & (ROWS_DEV - 1)) << 9) | bags_ref[i:i + 1, :]) + 1
        at_hi = (pos >> 7) == iota((BLOCKS, LANES), 0)
        for piece in range(3):
            part = ((key >> (8 * piece)) & 255).astype(F32)
            a_ref[piece * BLOCKS:(piece + 1) * BLOCKS, i * LANES:(i + 1) * LANES] = jnp.where(
                at_hi, part, 0.0).astype(BF16)
        b_ref[:, i * LANES:(i + 1) * LANES] = one_hot((pos & (LANES - 1)) == iota((LANES, LANES), 0))
    placed = lax.dot_general(a_ref[...], b_ref[...], NT, preferred_element_type=F32)
    out_ref[0:3 * BLOCKS, B_DEV:WIDTH] = placed.astype(BF16)
    meta = jnp.where(iota((16, LANES), 0) < 8,
                     jnp.concatenate([start_row, start_row], axis=0),
                     jnp.concatenate([blocks_row, blocks_row], axis=0).astype(F32))
    out_ref[3 * BLOCKS:3 * BLOCKS + 16, B_DEV:WIDTH] = meta.astype(BF16)
    out_ref[3 * BLOCKS + 16:E, B_DEV:WIDTH] = jnp.zeros((E - 3 * BLOCKS - 16, LANES), BF16)
    eye = one_hot(iota((E, E), 0) == iota((E, E), 1))
    out_ref[:, 0:B_DEV] = lax.dot_general(eye, g_ref[...], NT, preferred_element_type=F32).astype(BF16)


def pack(ids, bags, grads):
    return pl.pallas_call(
        pack_kernel,
        out_shape=jax.ShapeDtypeStruct((E, WIDTH), BF16),
        scratch_shapes=[pltpu.VMEM((3 * BLOCKS, LOOK), BF16),
                        pltpu.VMEM((LANES, LOOK), BF16),
                        pltpu.VMEM((TOUCH, 2 * LANES), BF16)],
        cost_estimate=cost(4),
        name="pack",
    )(ids, bags, grads)


def gather_kernel(z_ref, *refs, count):
    packets = refs[0:count]
    x_ref, k_ref, m_ref, all_ref, scalar_ref, sem = refs[count:]
    for d in range(count):
        side = packets[d][3 * BLOCKS:3 * BLOCKS + 16, B_DEV:WIDTH].astype(F32).astype(I32)
        m_ref[d] = jnp.where(iota((8, LANES), 0) == 0, side[0:8], side[8:16])
        copy = pltpu.make_async_copy(m_ref.at[d], scalar_ref.at[d], sem.at[d])
        copy.start()
        pieces = packets[d][0:3 * BLOCKS, B_DEV:WIDTH].astype(F32).astype(I32)
        all_ref[d] = (pieces[0:BLOCKS] + (pieces[BLOCKS:2 * BLOCKS] << 8)
                      + (pieces[2 * BLOCKS:3 * BLOCKS] << 16)) - 1
        copy.wait()

        def column(n, _, d=d):
            first = scalar_ref[d, 0, NX * z_ref[0] + n]

            def block(j, _):
                row = all_ref[d, pl.ds(first + j, 1), :]
                picks = one_hot((row & (B_DEV - 1)) == iota((B_DEV, LANES), 0))
                x_ref[d, 4 * n + j] = jnp.dot(packets[d][:, 0:B_DEV], picks,
                                              preferred_element_type=F32).astype(BF16)
                k_ref[d, pl.ds(4 * n + j, 1), :] = row >> 9
                return 0

            lax.fori_loop(0, scalar_ref[d, 1, NX * z_ref[0] + n], block, 0)
            return 0

        lax.fori_loop(0, NX, column, 0)


def gather(z, packets):
    count = len(packets)
    vmem = pl.BlockSpec(memory_space=pltpu.VMEM)
    return pl.pallas_call(
        lambda *refs: gather_kernel(*refs, count=count),
        out_shape=(jax.ShapeDtypeStruct((count, 16, E, LANES), BF16),
                   jax.ShapeDtypeStruct((count, 16, LANES), I32),
                   jax.ShapeDtypeStruct((count, 8, LANES), I32)),
        in_specs=[pl.BlockSpec(memory_space=pltpu.SMEM)] + [vmem] * count,
        scratch_shapes=[pltpu.VMEM((count, BLOCKS, LANES), I32), pltpu.SMEM((count, 8, LANES), I32),
                        pltpu.SemaphoreType.DMA((count,))],
        cost_estimate=cost(2 + 2 * count),
    )(z, *packets)


def sums_kernel(at_ref, *refs, counts, base):
    groups = len(counts)
    metas, xs, keys = refs[0:groups], refs[groups:2 * groups], refs[2 * groups:3 * groups]
    rows_ref, send_ref, keep_ref, all_ref, k_ref = refs[3 * groups:]
    column = at_ref[base + pl.program_id(0)]
    shard = at_ref[4] + column
    filled = jnp.int32(0)
    for n in range(groups):
        for d in range(counts[n]):
            many = metas[n][d, 1, shard]

            def move(j, _, n=n, d=d, filled=filled):
                all_ref[filled + j] = xs[n][d, j]
                k_ref[pl.ds(filled + j, 1), :] = keys[n][d, pl.ds(4 * column + j, 1), :]
                return 0

            lax.fori_loop(0, many, move, 0)
            filled = filled + many
    rounds = (filled + 7) >> 3

    def blank(j, _):
        all_ref[j] = jnp.zeros((E, LANES), BF16)
        k_ref[pl.ds(j, 1), :] = jnp.full((1, LANES), -1, I32)
        return 0

    lax.fori_loop(filled, rounds * 8, blank, 0)
    outs = (send_ref.at[0], keep_ref.at[0])
    for out in outs:
        out[...] = jnp.zeros((HALF, E), F32)

    def accumulate(r, _):
        wide = jnp.concatenate([all_ref[8 * r + j] for j in range(8)], axis=1)
        lines = [k_ref[pl.ds(8 * r + j, 1), :] for j in range(8)]
        for h in range(2):
            mine = rows_ref[0, h * HALF:(h + 1) * HALF, :]
            hits = jnp.concatenate([one_hot(mine == line) for line in lines], axis=1)
            outs[h][...] += lax.dot_general(hits, wide, NT, preferred_element_type=F32)
        return 0

    lax.fori_loop(0, rounds, accumulate, 0)


def cost(us):
    return pl.CostEstimate(flops=int(us * 6e8), bytes_accessed=int(us * 3e6), transcendentals=0)


def sums(at, base, many, gathered, rows):
    counts = tuple(g[0].shape[0] for g in gathered)
    total = sum(counts)
    smem = pl.BlockSpec(memory_space=pltpu.SMEM)
    out = pl.BlockSpec((1, HALF, E), lambda k, at: (k, 0, 0))
    in_specs = [smem] * len(counts)
    in_specs += [pl.BlockSpec((n, 4, E, LANES), lambda k, at: (0, at[base + k], 0, 0)) for n in counts]
    in_specs += [pl.BlockSpec((n, 16, LANES), lambda k, at: (0, 0, 0)) for n in counts]
    in_specs += [pl.BlockSpec((1, TOUCH, LANES), lambda k, at: (base + k, 0, 0))]
    return pl.pallas_call(
        lambda *refs: sums_kernel(*refs, counts=counts, base=base),
        grid_spec=pltpu.PrefetchScalarGridSpec(
            num_scalar_prefetch=1,
            grid=(many,),
            in_specs=in_specs,
            out_specs=[out, out],
            scratch_shapes=[pltpu.VMEM((4 * total, E, LANES), BF16), pltpu.VMEM((4 * total, LANES), I32)],
        ),
        out_shape=[jax.ShapeDtypeStruct((many, HALF, E), F32)] * 2,
        cost_estimate=cost(3 * many),
    )(at, *[g[2] for g in gathered], *[g[0] for g in gathered], *[g[1] for g in gathered], rows)


def listed_kernel(list_ref, rows_ref, accum_ref, table_ref, accum_out, table_out):
    rows = rows_ref[0]
    hi = jnp.where((rows >> 7) == iota((TOUCH, LANES), 1), 1.0, 0.0)
    padded = jnp.concatenate([accum_ref[...], jnp.zeros((LANES - 32, LANES), F32)], axis=0)
    line = jnp.dot(hi, padded, precision=lax.Precision.HIGHEST, preferred_element_type=F32)
    mine = jnp.where((rows & (LANES - 1)) == iota((TOUCH, LANES), 1), line, 0.0)
    accum_out[...] = jnp.broadcast_to(jnp.sum(mine, axis=1, keepdims=True), (TOUCH, LANES))

    def step(i, _):
        for j in range(16):
            row = list_ref[i >> 3, (i & 7) * 16 + j]
            table_out[pl.ds(i * 16 + j, 1), :] = table_ref[pl.ds(row, 1), :]
        return 0

    lax.fori_loop(0, TOUCH // 16, step, 0)


def listed_values(order, rows, accum, table):
    vmem = pl.BlockSpec(memory_space=pltpu.VMEM)
    return pl.pallas_call(
        listed_kernel,
        out_shape=(jax.ShapeDtypeStruct((TOUCH, LANES), F32), jax.ShapeDtypeStruct((TOUCH, E), F32)),
        grid=(1,),
        in_specs=[pl.BlockSpec(memory_space=pltpu.SMEM), OWN_ROWS, vmem, vmem],
        cost_estimate=cost(7),
        name="listed_values",
    )(order, rows, accum, table)


def update_kernel(*refs):
    plan_ref, list_ref, table_ref, accum_ref, listed_ref, old_ref, rows_ref = refs[0:7]
    chunks = refs[7:15]
    table_out, accum_out, u_ref, lhs_ref, rhs_ref = refs[15:]
    block = pl.program_id(0)

    @pl.when(block == 0)
    def _():
        lane = iota((QUART, LANES), 1)
        for n in range(8):
            at = slice(n * QUART, (n + 1) * QUART)
            g = chunks[n][...]
            mean = jnp.sum(g * g, axis=1, keepdims=True) * (1.0 / E)
            now = listed_ref[at, 0:1] + mean
            place = pl.multiple_of(plan_ref[16 + n] * QUART, QUART)
            u_ref[pl.ds(place, QUART), :] = old_ref[at, :] - 0.5 * g / (jnp.sqrt(now) + 1e-08)
            rows = rows_ref[0, at, :]
            lhs_ref[at, :] = jnp.where((rows >> 7) == lane, mean, 0.0)
            rhs_ref[at, :] = jnp.where((rows & (LANES - 1)) == lane, 1.0, 0.0)
        added = lax.dot_general(lhs_ref[...], rhs_ref[...], TN, precision=lax.Precision.HIGHEST,
                                preferred_element_type=F32)
        accum_out[...] = accum_ref[...] + added[0:32, :]

    table_out[...] = table_ref[...]
    first, last = plan_ref[block], plan_ref[block + 1]

    def put(n):
        row = list_ref[n >> 7, n & (LANES - 1)] - block * TILE
        table_out[pl.ds(row, 1), :] = u_ref[pl.ds(n, 1), :]

    def step(i, _):
        for j in range(8):
            put(first + i * 8 + j)
        return 0

    whole = (last - first) >> 3
    lax.fori_loop(0, whole, step, 0)
    lax.fori_loop(first + whole * 8, last, lambda n, _: (put(n), 0)[1], 0)


def update(plan, natural, table, accum, listed, old, rows, chunks):
    smem = pl.BlockSpec(memory_space=pltpu.SMEM)
    tile = pl.BlockSpec((TILE, E), lambda i: (i, 0))
    whole = lambda *shape: pl.BlockSpec(shape, lambda i: (0,) * len(shape))
    return pl.pallas_call(
        update_kernel,
        grid=(ROWS_DEV // TILE,),
        out_shape=(jax.ShapeDtypeStruct((ROWS_DEV, E), F32), jax.ShapeDtypeStruct((32, LANES), F32)),
        in_specs=[smem, smem, tile, whole(32, LANES), whole(TOUCH, LANES), whole(TOUCH, E), OWN_ROWS]
        + [whole(QUART, E)] * 8,
        out_specs=(tile, whole(32, LANES)),
        scratch_shapes=[pltpu.VMEM((TOUCH, E), F32), pltpu.VMEM((TOUCH, LANES), F32),
                        pltpu.VMEM((TOUCH, LANES), F32)],
        name="update",
    )(plan, natural, table, accum, listed, old, rows, *chunks)


def z_pairs(k):
    return [(z * NX + x, ((z + k) % NZ) * NX + x) for z in range(NZ) for x in range(NX)]


def x_pairs(k):
    return [(z * NX + x, z * NX + (x + k) % NX) for z in range(NZ) for x in range(NX)]


def y_pairs(k):
    return [(y * NC + c, ((y + k) % NY) * NC + c) for y in range(NY) for c in range(NC)]


C_PAIRS = [(y * NC + c, y * NC + 1 - c) for y in range(NY) for c in range(NC)]


def body(table, accum, pooled_grad, row_ids, bag_ids, touched):
    grp = lax.axis_index("grp")
    me = lax.axis_index("shard")
    y, c = grp // NC, grp % NC
    z, x = me // NX, me % NX

    def ordered(listed):
        halves = listed.reshape(NC, NY, QUART)
        halves = jnp.where(c == 0, halves[::-1], halves)
        doubled = jnp.concatenate([halves, halves], axis=1)
        return lax.dynamic_slice(doubled, (0, y, 0), (NC, NY, QUART)).reshape(TOUCH)

    own_list = touched.reshape(TOUCH)
    lists = {0: ordered(own_list)}
    for k in range(1, NX):
        lists[k] = ordered(lax.ppermute(own_list, "shard", x_pairs(-k)))
    stacked = jnp.stack([lists[k] for k in ORDER])[:, :, None]
    rows = jnp.broadcast_to(stacked, (NX, TOUCH, LANES))
    order = lists[0].reshape(8, LANES)
    bounds = jnp.sum((own_list[None, :] < TILE * jnp.arange(16, dtype=I32)[:, None]).astype(I32), axis=1)
    turn = (y + jnp.arange(NY, dtype=I32)) % NY
    plan = jnp.concatenate([bounds, (1 - c) * NY + turn, c * NY + turn])

    packet = pack(row_ids.reshape(32, LANES), bag_ids.reshape(32, LANES),
                  pooled_grad.reshape(B_DEV, E))
    got = {0: packet}
    for k in range(1, 5):
        got[-k] = lax.ppermute(got[1 - k], "shard", z_pairs(1))
        if k < 4:
            got[k] = lax.ppermute(got[k - 1], "shard", z_pairs(-1))
    gathered = []
    for sources in ((0,), (-1, 1), (-2, 2), (-3, 3), (-4,)):
        gathered.append(gather(z.reshape(1), [got[k] for k in sources]))

    listed, old = listed_values(order, rows, accum.reshape(32, LANES), table)
    at = jnp.concatenate([(x + jnp.array(ORDER, I32)) % NX, (NX * z).reshape(1)])
    both = {}
    for base, ks in ((0, (2,)), (1, (1, 3)), (3, (0,))):
        send, keep = sums(at, base, len(ks), gathered, rows)
        swapped = lax.ppermute(send, "grp", C_PAIRS)
        total = keep + swapped
        for n, k in enumerate(ks):
            both[k] = total[n]
    low = lax.ppermute(both[2][:HALF // 2], "shard", x_pairs(1))
    high = lax.ppermute(both[2][HALF // 2:], "shard", x_pairs(-1))
    up = jnp.concatenate([both[1][:HALF // 2] + low, both[1][HALF // 2:]], axis=0)
    down = jnp.concatenate([both[3][:HALF // 2], both[3][HALF // 2:] + high], axis=0)
    up = lax.ppermute(up, "shard", x_pairs(1))
    down = lax.ppermute(down, "shard", x_pairs(-1))
    total = both[0] + up + down
    part = total[0:QUART]
    for j in range(1, NY):
        part = part + lax.ppermute(total[j * QUART:(j + 1) * QUART], "grp", y_pairs(j))
    mine = [part] + [lax.ppermute(part, "grp", y_pairs(-j)) for j in range(1, NY)]
    other = [lax.ppermute(m, "grp", C_PAIRS) for m in mine]
    new_table, new_accum = update(plan, own_list.reshape(8, LANES), table, accum.reshape(32, LANES),
                                  listed, old, rows, other + mine)
    return (new_table, new_accum.reshape(ROWS_DEV))


def solution(mesh):
    return jax.shard_map(
        body,
        mesh=mesh,
        in_specs=(
            P("shard", None),
            P("shard"),
            P("grp", "shard", None, None),
            P("grp", "shard", None),
            P("grp", "shard", None),
            P("shard", None),
        ),
        out_specs=(P("shard", None), P("shard")),
        check_vma=False,
    )
```

```python
import jax
import jax.numpy as jnp
from jax import lax
from jax.experimental import pallas as pl
from jax.experimental.pallas import tpu as pltpu
from jax.sharding import PartitionSpec as P


E = 256
ROWS_DEV = 4096
TOUCH = 1024
HALF = TOUCH // 2
QUART = TOUCH // 8
TILE = 512
LOOK = 4096
B_DEV = 512
LANES = 128
BLOCKS = 64
WIDTH = B_DEV + LANES
NZ, NX, NY, NC = 8, 4, 4, 2
F32 = jnp.float32
BF16 = jnp.bfloat16
I32 = jnp.int32
NT = (((1,), (1,)), ((), ()))
TN = (((0,), (0,)), ((), ()))
ORDER = (2, 1, 3, 0)
SMEM = pl.BlockSpec(memory_space=pltpu.SMEM)
VMEM = pl.BlockSpec(memory_space=pltpu.VMEM)
PARAMS = pltpu.CompilerParams(vmem_limit_bytes=26 << 20)


def iota(shape, dim):
    return lax.broadcasted_iota(I32, shape, dim)


def one_hot(mask):
    return jnp.where(mask, 1.0, 0.0).astype(BF16)


def pack_kernel(ids_ref, bags_ref, g_ref, out_ref, a_ref, b_ref, o_ref):
    groups = LOOK // LANES
    ids = ids_ref[...]
    owner = ids >> 12
    owners = iota((32, LANES), 0)
    running = jnp.zeros((32, LANES), F32)
    for i in range(groups):
        hit = jnp.where(owner[i:i + 1, :] == owners, 1.0, 0.0)
        o_ref[i * 32:(i + 1) * 32, 0:LANES] = hit.astype(BF16)
        o_ref[i * 32:(i + 1) * 32, LANES:2 * LANES] = running.astype(BF16)
        running = running + hit
    before = one_hot(iota((LANES, LANES), 0) < iota((LANES, LANES), 1))
    weights = jnp.concatenate([before, jnp.ones((LANES, LANES), BF16)], axis=0)
    prefix = jnp.dot(o_ref[...], weights, preferred_element_type=F32)
    totals = jnp.concatenate([running, jnp.zeros((LANES - 32, LANES), F32)], axis=0)
    count_row = lax.dot_general(jnp.ones((8, LANES), BF16), totals.astype(BF16), NT,
                                preferred_element_type=F32).astype(I32)
    blocks_row = (count_row + (LANES - 1)) >> 7
    start_row = jnp.dot(blocks_row.astype(F32).astype(BF16), before, preferred_element_type=F32)
    start_col = jnp.sum(
        jnp.where(iota((32, LANES), 1) < iota((32, LANES), 0),
                  jnp.broadcast_to(blocks_row[0:1, :].astype(F32), (32, LANES)), 0.0),
        axis=1, keepdims=True) * float(LANES)
    start_all = jnp.broadcast_to(start_col, (32, LANES))
    for i in range(groups):
        hit = owner[i:i + 1, :] == owners
        pos = jnp.sum(jnp.where(hit, prefix[i * 32:(i + 1) * 32, :] + start_all, 0.0),
                      axis=0, keepdims=True).astype(I32)
        key = (((ids[i:i + 1, :] & (ROWS_DEV - 1)) << 9) | bags_ref[i:i + 1, :]) + 1
        at_hi = (pos >> 7) == iota((BLOCKS, LANES), 0)
        for piece in range(3):
            part = ((key >> (8 * piece)) & 255).astype(F32)
            a_ref[piece * BLOCKS:(piece + 1) * BLOCKS, i * LANES:(i + 1) * LANES] = jnp.where(
                at_hi, part, 0.0).astype(BF16)
        b_ref[:, i * LANES:(i + 1) * LANES] = one_hot((pos & (LANES - 1)) == iota((LANES, LANES), 0))
    placed = lax.dot_general(a_ref[...], b_ref[...], NT, preferred_element_type=F32)
    out_ref[0:3 * BLOCKS, B_DEV:WIDTH] = placed.astype(BF16)
    meta = jnp.where(iota((16, LANES), 0) < 8,
                     jnp.concatenate([start_row, start_row], axis=0),
                     jnp.concatenate([blocks_row, blocks_row], axis=0).astype(F32))
    out_ref[3 * BLOCKS:3 * BLOCKS + 16, B_DEV:WIDTH] = meta.astype(BF16)
    out_ref[3 * BLOCKS + 16:E, B_DEV:WIDTH] = jnp.zeros((E - 3 * BLOCKS - 16, LANES), BF16)
    eye = one_hot(iota((E, E), 0) == iota((E, E), 1))
    out_ref[:, 0:B_DEV] = lax.dot_general(eye, g_ref[...], NT, preferred_element_type=F32).astype(BF16)


def pack(ids, bags, grads):
    return pl.pallas_call(
        pack_kernel,
        out_shape=jax.ShapeDtypeStruct((E, WIDTH), BF16),
        scratch_shapes=[pltpu.VMEM((3 * BLOCKS, LOOK), BF16),
                        pltpu.VMEM((LANES, LOOK), BF16),
                        pltpu.VMEM((TOUCH, 2 * LANES), BF16)],
        cost_estimate=cost(4),
        compiler_params=PARAMS,
        name="pack",
    )(ids, bags, grads)


def gather_kernel(z_ref, *refs, count):
    packets = refs[0:count]
    x_ref, k_ref, m_ref, all_ref, scalar_ref, sem = refs[count:]
    for d in range(count):
        side = packets[d][3 * BLOCKS:3 * BLOCKS + 16, B_DEV:WIDTH].astype(F32).astype(I32)
        m_ref[d] = jnp.where(iota((8, LANES), 0) == 0, side[0:8], side[8:16])
        copy = pltpu.make_async_copy(m_ref.at[d], scalar_ref.at[d], sem.at[d])
        copy.start()
        pieces = packets[d][0:3 * BLOCKS, B_DEV:WIDTH].astype(F32).astype(I32)
        all_ref[d] = (pieces[0:BLOCKS] + (pieces[BLOCKS:2 * BLOCKS] << 8)
                      + (pieces[2 * BLOCKS:3 * BLOCKS] << 16)) - 1
        copy.wait()

        def column(n, _, d=d):
            first = scalar_ref[d, 0, NX * z_ref[0] + n]

            def block(j, _):
                row = all_ref[d, pl.ds(first + j, 1), :]
                picks = one_hot((row & (B_DEV - 1)) == iota((B_DEV, LANES), 0))
                x_ref[d, 4 * n + j] = jnp.dot(packets[d][:, 0:B_DEV], picks,
                                              preferred_element_type=F32).astype(BF16)
                k_ref[d, pl.ds(4 * n + j, 1), :] = row >> 9
                return 0

            lax.fori_loop(0, scalar_ref[d, 1, NX * z_ref[0] + n], block, 0)
            return 0

        lax.fori_loop(0, NX, column, 0)


def gather(z, packets):
    count = len(packets)
    return pl.pallas_call(
        lambda *refs: gather_kernel(*refs, count=count),
        out_shape=(jax.ShapeDtypeStruct((count, 16, E, LANES), BF16),
                   jax.ShapeDtypeStruct((count, 16, LANES), I32),
                   jax.ShapeDtypeStruct((count, 8, LANES), I32)),
        in_specs=[SMEM] + [VMEM] * count,
        scratch_shapes=[pltpu.VMEM((count, BLOCKS, LANES), I32), pltpu.SMEM((count, 8, LANES), I32),
                        pltpu.SemaphoreType.DMA((count,))],
        cost_estimate=cost(2 + count),
        compiler_params=PARAMS,
    )(z, *packets)


def sums_kernel(at_ref, *refs, counts, base, many):
    groups = len(counts)
    metas, xs, keys = refs[0:groups], refs[groups:2 * groups], refs[2 * groups:3 * groups]
    rows_ref, send_ref, keep_ref, all_ref, k_ref = refs[3 * groups:]
    for m in range(many):
        column = at_ref[base + m]
        filled = jnp.int32(0)
        for n in range(groups):
            for d in range(counts[n]):
                found = metas[n][d, 1, at_ref[4] + column]

                def move(j, _, n=n, d=d, filled=filled, column=column):
                    all_ref[filled + j] = xs[n][d, 4 * column + j]
                    k_ref[pl.ds(filled + j, 1), :] = keys[n][d, pl.ds(4 * column + j, 1), :]
                    return 0

                lax.fori_loop(0, found, move, 0)
                filled = filled + found
        rounds = (filled + 7) >> 3

        def blank(j, _):
            all_ref[j] = jnp.zeros((E, LANES), BF16)
            k_ref[pl.ds(j, 1), :] = jnp.full((1, LANES), -1, I32)
            return 0

        lax.fori_loop(filled, rounds * 8, blank, 0)
        send_ref[m] = jnp.zeros((HALF, E), F32)
        keep_ref[m] = jnp.zeros((HALF, E), F32)

        def accumulate(r, _, m=m):
            wide = jnp.concatenate([all_ref[8 * r + j] for j in range(8)], axis=1)
            lines = [k_ref[pl.ds(8 * r + j, 1), :] for j in range(8)]
            for h, out_ref in enumerate((send_ref, keep_ref)):
                mine = rows_ref[base + m, h * HALF:(h + 1) * HALF, :]
                hits = jnp.concatenate([one_hot(mine == line) for line in lines], axis=1)
                out_ref[m] += lax.dot_general(hits, wide, NT, preferred_element_type=F32)
            return 0

        lax.fori_loop(0, rounds, accumulate, 0)


def cost(us):
    return pl.CostEstimate(flops=int(us * 6e8), bytes_accessed=int(us * 3e6), transcendentals=0)


def sums(at, base, many, gathered, rows):
    counts = tuple(g[0].shape[0] for g in gathered)
    total = sum(counts)
    return pl.pallas_call(
        lambda *refs: sums_kernel(*refs, counts=counts, base=base, many=many),
        in_specs=[SMEM] * (1 + len(counts)) + [VMEM] * (2 * len(counts) + 1),
        scratch_shapes=[pltpu.VMEM((4 * total, E, LANES), BF16), pltpu.VMEM((4 * total, LANES), I32)],
        out_shape=[jax.ShapeDtypeStruct((many, HALF, E), F32)] * 2,
        cost_estimate=cost(2 * many),
        compiler_params=PARAMS,
    )(at, *[g[2] for g in gathered], *[g[0] for g in gathered], *[g[1] for g in gathered], rows)


def listed_kernel(list_ref, rows_ref, accum_ref, table_ref, accum_out, table_out):
    rows = rows_ref[NX - 1]
    hi = jnp.where((rows >> 7) == iota((TOUCH, LANES), 1), 1.0, 0.0)
    padded = jnp.concatenate([accum_ref[...], jnp.zeros((LANES - 32, LANES), F32)], axis=0)
    line = jnp.dot(hi, padded, precision=lax.Precision.HIGHEST, preferred_element_type=F32)
    mine = jnp.where((rows & (LANES - 1)) == iota((TOUCH, LANES), 1), line, 0.0)
    accum_out[...] = jnp.broadcast_to(jnp.sum(mine, axis=1, keepdims=True), (TOUCH, LANES))

    def step(i, _):
        for j in range(16):
            row = list_ref[i >> 3, (i & 7) * 16 + j]
            table_out[pl.ds(i * 16 + j, 1), :] = table_ref[pl.ds(row, 1), :]
        return 0

    lax.fori_loop(0, TOUCH // 16, step, 0)


def listed_values(order, rows, accum, table):
    return pl.pallas_call(
        listed_kernel,
        out_shape=(jax.ShapeDtypeStruct((TOUCH, LANES), F32), jax.ShapeDtypeStruct((TOUCH, E), F32)),
        in_specs=[SMEM, VMEM, VMEM, VMEM],
        cost_estimate=cost(6),
        compiler_params=PARAMS,
        name="listed_values",
    )(order, rows, accum, table)


def update_kernel(*refs):
    plan_ref, list_ref, table_ref, accum_ref, listed_ref, old_ref, rows_ref = refs[0:7]
    chunks = refs[7:15]
    table_out, accum_out, u_ref, lhs_ref, rhs_ref = refs[15:]
    block = pl.program_id(0)

    @pl.when(block == 0)
    def _():
        lane = iota((QUART, LANES), 1)
        for n in range(8):
            at = slice(n * QUART, (n + 1) * QUART)
            g = chunks[n][...]
            mean = jnp.sum(g * g, axis=1, keepdims=True) * (1.0 / E)
            now = listed_ref[at, 0:1] + mean
            place = pl.multiple_of(plan_ref[16 + n] * QUART, QUART)
            u_ref[pl.ds(place, QUART), :] = old_ref[at, :] - 0.5 * g / (jnp.sqrt(now) + 1e-08)
            rows = rows_ref[NX - 1, at, :]
            lhs_ref[at, :] = jnp.where((rows >> 7) == lane, mean, 0.0)
            rhs_ref[at, :] = jnp.where((rows & (LANES - 1)) == lane, 1.0, 0.0)
        added = lax.dot_general(lhs_ref[...], rhs_ref[...], TN, precision=lax.Precision.HIGHEST,
                                preferred_element_type=F32)
        accum_out[...] = accum_ref[...] + added[0:32, :]

    table_out[...] = table_ref[pl.ds(pl.multiple_of(block * TILE, TILE), TILE), :]
    first, last = plan_ref[block], plan_ref[block + 1]

    def put(n):
        row = list_ref[n >> 7, n & (LANES - 1)] - block * TILE
        table_out[pl.ds(row, 1), :] = u_ref[pl.ds(n, 1), :]

    def step(i, _):
        for j in range(8):
            put(first + i * 8 + j)
        return 0

    whole = (last - first) >> 3
    lax.fori_loop(0, whole, step, 0)
    lax.fori_loop(first + whole * 8, last, lambda n, _: (put(n), 0)[1], 0)


def update(plan, natural, table, accum, listed, old, rows, chunks):
    return pl.pallas_call(
        update_kernel,
        grid=(ROWS_DEV // TILE,),
        out_shape=(jax.ShapeDtypeStruct((ROWS_DEV, E), F32), jax.ShapeDtypeStruct((32, LANES), F32)),
        in_specs=[SMEM, SMEM] + [VMEM] * 13,
        out_specs=(pl.BlockSpec((TILE, E), lambda i: (i, 0)), pl.BlockSpec((32, LANES), lambda i: (0, 0))),
        scratch_shapes=[pltpu.VMEM((TOUCH, E), F32), pltpu.VMEM((TOUCH, LANES), F32),
                        pltpu.VMEM((TOUCH, LANES), F32)],
        compiler_params=PARAMS,
        name="update",
    )(plan, natural, table, accum, listed, old, rows, *chunks)


def z_pairs(k):
    return [(z * NX + x, ((z + k) % NZ) * NX + x) for z in range(NZ) for x in range(NX)]


def x_pairs(k):
    return [(z * NX + x, z * NX + (x + k) % NX) for z in range(NZ) for x in range(NX)]


def y_pairs(k):
    return [(y * NC + c, ((y + k) % NY) * NC + c) for y in range(NY) for c in range(NC)]


C_PAIRS = [(y * NC + c, y * NC + 1 - c) for y in range(NY) for c in range(NC)]


def body(table, accum, pooled_grad, row_ids, bag_ids, touched):
    grp = lax.axis_index("grp")
    me = lax.axis_index("shard")
    y, c = grp // NC, grp % NC
    z, x = me // NX, me % NX

    def ordered(listed):
        halves = listed.reshape(NC, NY, QUART)
        halves = jnp.where(c == 0, halves[::-1], halves)
        doubled = jnp.concatenate([halves, halves], axis=1)
        return lax.dynamic_slice(doubled, (0, y, 0), (NC, NY, QUART)).reshape(TOUCH)

    own_list = touched.reshape(TOUCH)
    lists = {0: ordered(own_list)}
    for k in range(1, NX):
        lists[k] = ordered(lax.ppermute(own_list, "shard", x_pairs(-k)))
    stacked = jnp.stack([lists[k] for k in ORDER])[:, :, None]
    rows = jnp.broadcast_to(stacked, (NX, TOUCH, LANES))
    order = lists[0].reshape(8, LANES)
    bounds = jnp.sum((own_list[None, :] < TILE * jnp.arange(16, dtype=I32)[:, None]).astype(I32), axis=1)
    turn = (y + jnp.arange(NY, dtype=I32)) % NY
    plan = jnp.concatenate([bounds, (1 - c) * NY + turn, c * NY + turn])

    packet = pack(row_ids.reshape(32, LANES), bag_ids.reshape(32, LANES),
                  pooled_grad.reshape(B_DEV, E))
    got = {0: packet}
    for k in range(1, 5):
        got[-k] = lax.ppermute(got[1 - k], "shard", z_pairs(1))
        if k < 4:
            got[k] = lax.ppermute(got[k - 1], "shard", z_pairs(-1))
    gathered = []
    for sources in ((0,), (-1, 1), (-2, 2), (-3, 3), (-4,)):
        gathered.append(gather(z.reshape(1), [got[k] for k in sources]))

    table = pltpu.with_memory_space_constraint(table, pltpu.VMEM)
    listed, old = listed_values(order, rows, accum.reshape(32, LANES), table)
    at = jnp.concatenate([(x + jnp.array(ORDER, I32)) % NX, (NX * z).reshape(1)])
    both = {}
    for base, ks in ((0, (2,)), (1, (1, 3)), (3, (0,))):
        send, keep = sums(at, base, len(ks), gathered, rows)
        swapped = lax.ppermute(send, "grp", C_PAIRS)
        total = keep + swapped
        for n, k in enumerate(ks):
            both[k] = total[n]
    low = lax.ppermute(both[2][:HALF // 2], "shard", x_pairs(1))
    high = lax.ppermute(both[2][HALF // 2:], "shard", x_pairs(-1))
    up = jnp.concatenate([both[1][:HALF // 2] + low, both[1][HALF // 2:]], axis=0)
    down = jnp.concatenate([both[3][:HALF // 2], both[3][HALF // 2:] + high], axis=0)
    up = lax.ppermute(up, "shard", x_pairs(1))
    down = lax.ppermute(down, "shard", x_pairs(-1))
    total = both[0] + up + down
    part = total[0:QUART]
    for j in range(1, NY):
        part = part + lax.ppermute(total[j * QUART:(j + 1) * QUART], "grp", y_pairs(j))
    mine = [part] + [lax.ppermute(part, "grp", y_pairs(-j)) for j in range(1, NY)]
    other = [lax.ppermute(m, "grp", C_PAIRS) for m in mine]
    new_table, new_accum = update(plan, own_list.reshape(8, LANES), table, accum.reshape(32, LANES),
                                  listed, old, rows, other + mine)
    return (new_table, new_accum.reshape(ROWS_DEV))


def solution(mesh):
    return jax.shard_map(
        body,
        mesh=mesh,
        in_specs=(
            P("shard", None),
            P("shard"),
            P("grp", "shard", None, None),
            P("grp", "shard", None),
            P("grp", "shard", None),
            P("shard", None),
        ),
        out_specs=(P("shard", None), P("shard")),
        check_vma=False,
    )
```

```python
import jax
import jax.numpy as jnp
from jax import lax
from jax.experimental import pallas as pl
from jax.experimental.pallas import tpu as pltpu
from jax.sharding import PartitionSpec as P


E = 256
ROWS_DEV = 4096
TOUCH = 1024
HALF = TOUCH // 2
QUART = TOUCH // 8
TILE = 512
LOOK = 4096
B_DEV = 512
LANES = 128
BLOCKS = 64
WIDTH = B_DEV + LANES
NZ, NX, NY, NC = 8, 4, 4, 2
F32 = jnp.float32
BF16 = jnp.bfloat16
I32 = jnp.int32
NT = (((1,), (1,)), ((), ()))
TN = (((0,), (0,)), ((), ()))
ORDER = (2, 1, 3, 0)
SMEM = pl.BlockSpec(memory_space=pltpu.SMEM)
VMEM = pl.BlockSpec(memory_space=pltpu.VMEM)
HBM = pl.BlockSpec(memory_space=pltpu.HBM)
PARAMS = pltpu.CompilerParams(vmem_limit_bytes=26 << 20)


def iota(shape, dim):
    return lax.broadcasted_iota(I32, shape, dim)


def one_hot(mask):
    return jnp.where(mask, 1.0, 0.0).astype(BF16)


def in_hbm(array):
    return pltpu.with_memory_space_constraint(array, pltpu.HBM)


def pack_kernel(ids_hbm, bags_hbm, g_hbm, out_ref, a_ref, b_ref, o_ref, ids_ref, bags_ref, g_ref, sem):
    loads = [pltpu.make_async_copy(src, dst, sem.at[n])
             for n, (src, dst) in enumerate(((ids_hbm, ids_ref), (bags_hbm, bags_ref), (g_hbm, g_ref)))]
    for load in loads:
        load.start()
    for load in loads:
        load.wait()
    groups = LOOK // LANES
    ids = ids_ref[...]
    owner = ids >> 12
    owners = iota((32, LANES), 0)
    running = jnp.zeros((32, LANES), F32)
    for i in range(groups):
        hit = jnp.where(owner[i:i + 1, :] == owners, 1.0, 0.0)
        o_ref[i * 32:(i + 1) * 32, 0:LANES] = hit.astype(BF16)
        o_ref[i * 32:(i + 1) * 32, LANES:2 * LANES] = running.astype(BF16)
        running = running + hit
    before = one_hot(iota((LANES, LANES), 0) < iota((LANES, LANES), 1))
    weights = jnp.concatenate([before, jnp.ones((LANES, LANES), BF16)], axis=0)
    prefix = jnp.dot(o_ref[...], weights, preferred_element_type=F32)
    totals = jnp.concatenate([running, jnp.zeros((LANES - 32, LANES), F32)], axis=0)
    count_row = lax.dot_general(jnp.ones((8, LANES), BF16), totals.astype(BF16), NT,
                                preferred_element_type=F32).astype(I32)
    blocks_row = (count_row + (LANES - 1)) >> 7
    start_row = jnp.dot(blocks_row.astype(F32).astype(BF16), before, preferred_element_type=F32)
    start_col = jnp.sum(
        jnp.where(iota((32, LANES), 1) < iota((32, LANES), 0),
                  jnp.broadcast_to(blocks_row[0:1, :].astype(F32), (32, LANES)), 0.0),
        axis=1, keepdims=True) * float(LANES)
    start_all = jnp.broadcast_to(start_col, (32, LANES))
    for i in range(groups):
        hit = owner[i:i + 1, :] == owners
        pos = jnp.sum(jnp.where(hit, prefix[i * 32:(i + 1) * 32, :] + start_all, 0.0),
                      axis=0, keepdims=True).astype(I32)
        key = (((ids[i:i + 1, :] & (ROWS_DEV - 1)) << 9) | bags_ref[i:i + 1, :]) + 1
        at_hi = (pos >> 7) == iota((BLOCKS, LANES), 0)
        for piece in range(3):
            part = ((key >> (8 * piece)) & 255).astype(F32)
            a_ref[piece * BLOCKS:(piece + 1) * BLOCKS, i * LANES:(i + 1) * LANES] = jnp.where(
                at_hi, part, 0.0).astype(BF16)
        b_ref[:, i * LANES:(i + 1) * LANES] = one_hot((pos & (LANES - 1)) == iota((LANES, LANES), 0))
    placed = lax.dot_general(a_ref[...], b_ref[...], NT, preferred_element_type=F32)
    out_ref[0:3 * BLOCKS, B_DEV:WIDTH] = placed.astype(BF16)
    meta = jnp.where(iota((16, LANES), 0) < 8,
                     jnp.concatenate([start_row, start_row], axis=0),
                     jnp.concatenate([blocks_row, blocks_row], axis=0).astype(F32))
    out_ref[3 * BLOCKS:3 * BLOCKS + 16, B_DEV:WIDTH] = meta.astype(BF16)
    out_ref[3 * BLOCKS + 16:E, B_DEV:WIDTH] = jnp.zeros((E - 3 * BLOCKS - 16, LANES), BF16)
    eye = one_hot(iota((E, E), 0) == iota((E, E), 1))
    out_ref[:, 0:B_DEV] = lax.dot_general(eye, g_ref[...], NT, preferred_element_type=F32).astype(BF16)


def pack(ids, bags, grads):
    return pl.pallas_call(
        pack_kernel,
        out_shape=jax.ShapeDtypeStruct((E, WIDTH), BF16),
        in_specs=[HBM] * 3,
        scratch_shapes=[pltpu.VMEM((3 * BLOCKS, LOOK), BF16),
                        pltpu.VMEM((LANES, LOOK), BF16),
                        pltpu.VMEM((TOUCH, 2 * LANES), BF16),
                        pltpu.VMEM((32, LANES), I32), pltpu.VMEM((32, LANES), I32),
                        pltpu.VMEM((B_DEV, E), BF16), pltpu.SemaphoreType.DMA((3,))],
        cost_estimate=cost(4),
        compiler_params=PARAMS,
        name="pack",
    )(*[in_hbm(a) for a in (ids, bags, grads)])


def gather_kernel(z_ref, *refs, count):
    packets = refs[0:count]
    x_ref, k_ref, m_ref, all_ref, scalar_ref, sem = refs[count:]
    for d in range(count):
        side = packets[d][3 * BLOCKS:3 * BLOCKS + 16, B_DEV:WIDTH].astype(F32).astype(I32)
        m_ref[d] = jnp.where(iota((8, LANES), 0) == 0, side[0:8], side[8:16])
        copy = pltpu.make_async_copy(m_ref.at[d], scalar_ref.at[d], sem.at[d])
        copy.start()
        pieces = packets[d][0:3 * BLOCKS, B_DEV:WIDTH].astype(F32).astype(I32)
        all_ref[d] = (pieces[0:BLOCKS] + (pieces[BLOCKS:2 * BLOCKS] << 8)
                      + (pieces[2 * BLOCKS:3 * BLOCKS] << 16)) - 1
        copy.wait()

        def column(n, _, d=d):
            first = scalar_ref[d, 0, NX * z_ref[0] + n]

            def block(j, _):
                row = all_ref[d, pl.ds(first + j, 1), :]
                picks = one_hot((row & (B_DEV - 1)) == iota((B_DEV, LANES), 0))
                x_ref[d, 4 * n + j] = jnp.dot(packets[d][:, 0:B_DEV], picks,
                                              preferred_element_type=F32).astype(BF16)
                k_ref[d, pl.ds(4 * n + j, 1), :] = row >> 9
                return 0

            lax.fori_loop(0, scalar_ref[d, 1, NX * z_ref[0] + n], block, 0)
            return 0

        lax.fori_loop(0, NX, column, 0)


def gather(z, packets):
    count = len(packets)
    return pl.pallas_call(
        lambda *refs: gather_kernel(*refs, count=count),
        out_shape=(jax.ShapeDtypeStruct((count, 16, E, LANES), BF16),
                   jax.ShapeDtypeStruct((count, 16, LANES), I32),
                   jax.ShapeDtypeStruct((count, 8, LANES), I32)),
        in_specs=[SMEM] + [VMEM] * count,
        scratch_shapes=[pltpu.VMEM((count, BLOCKS, LANES), I32), pltpu.SMEM((count, 8, LANES), I32),
                        pltpu.SemaphoreType.DMA((count,))],
        cost_estimate=cost(2 + count),
        compiler_params=PARAMS,
    )(z, *packets)


def sums_kernel(at_ref, *refs, counts, base, many):
    groups = len(counts)
    metas, xs, keys = refs[0:groups], refs[groups:2 * groups], refs[2 * groups:3 * groups]
    rows_ref, send_ref, keep_ref, all_ref, k_ref = refs[3 * groups:]
    for m in range(many):
        column = at_ref[base + m]
        filled = jnp.int32(0)
        for n in range(groups):
            for d in range(counts[n]):
                found = metas[n][d, 1, at_ref[4] + column]

                def move(j, _, n=n, d=d, filled=filled, column=column):
                    all_ref[filled + j] = xs[n][d, 4 * column + j]
                    k_ref[pl.ds(filled + j, 1), :] = keys[n][d, pl.ds(4 * column + j, 1), :]
                    return 0

                lax.fori_loop(0, found, move, 0)
                filled = filled + found
        rounds = (filled + 7) >> 3

        def blank(j, _):
            all_ref[j] = jnp.zeros((E, LANES), BF16)
            k_ref[pl.ds(j, 1), :] = jnp.full((1, LANES), -1, I32)
            return 0

        lax.fori_loop(filled, rounds * 8, blank, 0)
        send_ref[m] = jnp.zeros((HALF, E), F32)
        keep_ref[m] = jnp.zeros((HALF, E), F32)

        def accumulate(r, _, m=m):
            wide = jnp.concatenate([all_ref[8 * r + j] for j in range(8)], axis=1)
            lines = [k_ref[pl.ds(8 * r + j, 1), :] for j in range(8)]
            for h, out_ref in enumerate((send_ref, keep_ref)):
                mine = rows_ref[base + m, h * HALF:(h + 1) * HALF, :]
                hits = jnp.concatenate([one_hot(mine == line) for line in lines], axis=1)
                out_ref[m] += lax.dot_general(hits, wide, NT, preferred_element_type=F32)
            return 0

        lax.fori_loop(0, rounds, accumulate, 0)


def cost(us):
    return pl.CostEstimate(flops=int(us * 6e8), bytes_accessed=int(us * 3e6), transcendentals=0)


def sums(at, base, many, gathered, rows):
    counts = tuple(g[0].shape[0] for g in gathered)
    total = sum(counts)
    return pl.pallas_call(
        lambda *refs: sums_kernel(*refs, counts=counts, base=base, many=many),
        in_specs=[SMEM] * (1 + len(counts)) + [VMEM] * (2 * len(counts) + 1),
        scratch_shapes=[pltpu.VMEM((4 * total, E, LANES), BF16), pltpu.VMEM((4 * total, LANES), I32)],
        out_shape=[jax.ShapeDtypeStruct((many, HALF, E), F32)] * 2,
        cost_estimate=cost(2 * many),
        compiler_params=PARAMS,
    )(at, *[g[2] for g in gathered], *[g[0] for g in gathered], *[g[1] for g in gathered], rows)


def listed_kernel(list_ref, rows_ref, accum_ref, table_ref, out_ref):
    rows = rows_ref[NX - 1]
    hi = jnp.where((rows >> 7) == iota((TOUCH, LANES), 1), 1.0, 0.0)
    padded = jnp.concatenate([accum_ref[...], jnp.zeros((LANES - 32, LANES), F32)], axis=0)
    line = jnp.dot(hi, padded, precision=lax.Precision.HIGHEST, preferred_element_type=F32)
    mine = jnp.where((rows & (LANES - 1)) == iota((TOUCH, LANES), 1), line, 0.0)
    out_ref[0:TOUCH, E:] = jnp.broadcast_to(jnp.sum(mine, axis=1, keepdims=True), (TOUCH, LANES))
    out_ref[TOUCH:, E:] = accum_ref[...]
    out_ref[TOUCH:, 0:E] = jnp.zeros((32, E), F32)

    def step(i, _):
        for j in range(16):
            row = list_ref[i >> 3, (i & 7) * 16 + j]
            out_ref[pl.ds(i * 16 + j, 1), 0:E] = table_ref[pl.ds(row, 1), :]
        return 0

    lax.fori_loop(0, TOUCH // 16, step, 0)


def listed_values(order, rows, accum, table):
    return pl.pallas_call(
        listed_kernel,
        out_shape=jax.ShapeDtypeStruct((TOUCH + 32, E + LANES), F32),
        in_specs=[SMEM, VMEM, VMEM, VMEM],
        cost_estimate=cost(6),
        compiler_params=PARAMS,
        name="listed_values",
    )(order, rows, accum, table)


def update_kernel(*refs):
    plan_ref, list_ref, table_ref, listed_hbm, rows_ref = refs[0:5]
    chunks = refs[5:13]
    table_out, accum_out, new_ref, listed_ref, u_ref, lhs_ref, rhs_ref, load_sem, store_sem = refs[13:]
    loads = [pltpu.make_async_copy(src, dst, load_sem.at[n])
             for n, (src, dst) in enumerate(((listed_hbm, listed_ref), (table_ref, new_ref)))]
    for load in loads:
        load.start()
    lane = iota((QUART, LANES), 1)
    means = []
    for n in range(8):
        at = slice(n * QUART, (n + 1) * QUART)
        g = chunks[n][...]
        mean = jnp.sum(g * g, axis=1, keepdims=True) * (1.0 / E)
        means.append(mean)
        rows = rows_ref[NX - 1, at, :]
        lhs_ref[at, :] = jnp.where((rows >> 7) == lane, mean, 0.0)
        rhs_ref[at, :] = jnp.where((rows & (LANES - 1)) == lane, 1.0, 0.0)
    loads[0].wait()
    for n in range(8):
        at = slice(n * QUART, (n + 1) * QUART)
        now = listed_ref[at, E:E + 1] + means[n]
        place = pl.multiple_of(plan_ref[16 + n] * QUART, QUART)
        u_ref[pl.ds(place, QUART), :] = (
            listed_ref[at, 0:E] - 0.5 * chunks[n][...] / (jnp.sqrt(now) + 1e-08))
    loads[1].wait()

    def put(n):
        new_ref[pl.ds(list_ref[n], 1), :] = u_ref[pl.ds(n, 1), :]

    def store(b):
        tile = pl.ds(pl.multiple_of(b * TILE, TILE), TILE)
        return pltpu.make_async_copy(new_ref.at[tile], table_out.at[tile], store_sem.at[b])

    def tile(b, _):
        first, last = plan_ref[b], plan_ref[b + 1]
        whole = (last - first) >> 3

        def step(i, _):
            for j in range(8):
                put(first + i * 8 + j)
            return 0

        lax.fori_loop(0, whole, step, 0)
        lax.fori_loop(first + whole * 8, last, lambda n, _: (put(n), 0)[1], 0)
        store(b).start()
        return 0

    lax.fori_loop(0, ROWS_DEV // TILE, tile, 0)
    added = lax.dot_general(lhs_ref[...], rhs_ref[...], TN, precision=lax.Precision.HIGHEST,
                            preferred_element_type=F32)
    accum_out[...] = listed_ref[TOUCH:, E:] + added[0:32, :]
    for b in range(ROWS_DEV // TILE):
        store(b).wait()


def update(plan, natural, table, listed, rows, chunks):
    return pl.pallas_call(
        update_kernel,
        out_shape=(jax.ShapeDtypeStruct((ROWS_DEV, E), F32), jax.ShapeDtypeStruct((32, LANES), F32)),
        in_specs=[SMEM, SMEM, HBM, HBM] + [VMEM] * 9,
        out_specs=(HBM, VMEM),
        scratch_shapes=[pltpu.VMEM((ROWS_DEV, E), F32), pltpu.VMEM((TOUCH + 32, E + LANES), F32),
                        pltpu.VMEM((TOUCH, E), F32),
                        pltpu.VMEM((TOUCH, LANES), F32), pltpu.VMEM((TOUCH, LANES), F32),
                        pltpu.SemaphoreType.DMA((2,)), pltpu.SemaphoreType.DMA((ROWS_DEV // TILE,))],
        compiler_params=PARAMS,
        name="update",
    )(plan, natural, in_hbm(table), in_hbm(listed), rows, *chunks)


def z_pairs(k):
    return [(z * NX + x, ((z + k) % NZ) * NX + x) for z in range(NZ) for x in range(NX)]


def x_pairs(k):
    return [(z * NX + x, z * NX + (x + k) % NX) for z in range(NZ) for x in range(NX)]


def y_pairs(k):
    return [(y * NC + c, ((y + k) % NY) * NC + c) for y in range(NY) for c in range(NC)]


C_PAIRS = [(y * NC + c, y * NC + 1 - c) for y in range(NY) for c in range(NC)]


def body(table, accum, pooled_grad, row_ids, bag_ids, touched):
    grp = lax.axis_index("grp")
    me = lax.axis_index("shard")
    y, c = grp // NC, grp % NC
    z, x = me // NX, me % NX

    def ordered(listed):
        halves = listed.reshape(NC, NY, QUART)
        halves = jnp.where(c == 0, halves[::-1], halves)
        doubled = jnp.concatenate([halves, halves], axis=1)
        return lax.dynamic_slice(doubled, (0, y, 0), (NC, NY, QUART)).reshape(TOUCH)

    own_list = touched.reshape(TOUCH)
    lists = {0: ordered(own_list)}
    for k in range(1, NX):
        lists[k] = ordered(lax.ppermute(own_list, "shard", x_pairs(-k)))
    stacked = jnp.stack([lists[k] for k in ORDER])[:, :, None]
    rows = jnp.broadcast_to(stacked, (NX, TOUCH, LANES))
    order = lists[0].reshape(8, LANES)
    bounds = jnp.sum((own_list[None, :] < TILE * jnp.arange(16, dtype=I32)[:, None]).astype(I32), axis=1)
    turn = (y + jnp.arange(NY, dtype=I32)) % NY
    plan = jnp.concatenate([bounds, (1 - c) * NY + turn, c * NY + turn])

    packet = pack(row_ids.reshape(32, LANES), bag_ids.reshape(32, LANES),
                  pooled_grad.reshape(B_DEV, E))
    got = {0: packet}
    for k in range(1, 5):
        got[-k] = lax.ppermute(got[1 - k], "shard", z_pairs(1))
        if k < 4:
            got[k] = lax.ppermute(got[k - 1], "shard", z_pairs(-1))
    gathered = []
    for sources in ((0,), (-1, 1), (-2, 2), (-3, 3), (-4,)):
        gathered.append(gather(z.reshape(1), [got[k] for k in sources]))

    listed = listed_values(order, rows, accum.reshape(32, LANES), table)
    at = jnp.concatenate([(x + jnp.array(ORDER, I32)) % NX, (NX * z).reshape(1)])
    both = {}
    for base, ks in ((0, (2,)), (1, (1, 3)), (3, (0,))):
        send, keep = sums(at, base, len(ks), gathered, rows)
        swapped = lax.ppermute(send, "grp", C_PAIRS)
        total = keep + swapped
        for n, k in enumerate(ks):
            both[k] = total[n]
    total = both[0]
    for k in (2, 1, 3):
        total = total + lax.ppermute(both[k], "shard", x_pairs(k))
    part = total[0:QUART]
    for j in range(1, NY):
        part = part + lax.ppermute(total[j * QUART:(j + 1) * QUART], "grp", y_pairs(j))
    mine = [part] + [lax.ppermute(part, "grp", y_pairs(-j)) for j in range(1, NY)]
    other = [lax.ppermute(m, "grp", C_PAIRS) for m in mine]
    new_table, new_accum = update(plan, own_list, table, listed, rows, other + mine)
    return (new_table, new_accum.reshape(ROWS_DEV))


def solution(mesh):
    return jax.shard_map(
        body,
        mesh=mesh,
        in_specs=(
            P("shard", None),
            P("shard"),
            P("grp", "shard", None, None),
            P("grp", "shard", None),
            P("grp", "shard", None),
            P("shard", None),
        ),
        out_specs=(P("shard", None), P("shard")),
        check_vma=False,
    )
```

```python
import jax
import jax.numpy as jnp
from jax import lax
from jax.experimental import pallas as pl
from jax.experimental.pallas import tpu as pltpu
from jax.sharding import PartitionSpec as P


E = 256
ROWS_DEV = 4096
TOUCH = 1024
HALF = TOUCH // 2
QUART = TOUCH // 8
PIECE = QUART // 2
TILE = 512
LOOK = 4096
B_DEV = 512
LANES = 128
BLOCKS = 64
WIDTH = B_DEV + LANES
NZ, NX, NY, NC = 8, 4, 4, 2
F32 = jnp.float32
BF16 = jnp.bfloat16
I32 = jnp.int32
NT = (((1,), (1,)), ((), ()))
TN = (((0,), (0,)), ((), ()))
ORDER = (2, 1, 3, 0)
SMEM = pl.BlockSpec(memory_space=pltpu.SMEM)
VMEM = pl.BlockSpec(memory_space=pltpu.VMEM)
HBM = pl.BlockSpec(memory_space=pltpu.HBM)
PARAMS = pltpu.CompilerParams(vmem_limit_bytes=14 << 20)


def iota(shape, dim):
    return lax.broadcasted_iota(I32, shape, dim)


def one_hot(mask):
    return jnp.where(mask, 1.0, 0.0).astype(BF16)


def in_hbm(array):
    return pltpu.with_memory_space_constraint(array, pltpu.HBM)


def pack_kernel(ids_hbm, bags_hbm, g_hbm, out_ref, a_ref, b_ref, o_ref, ids_ref, bags_ref, g_ref, sem):
    loads = [pltpu.make_async_copy(src, dst, sem.at[n])
             for n, (src, dst) in enumerate(((ids_hbm, ids_ref), (bags_hbm, bags_ref), (g_hbm, g_ref)))]
    for load in loads:
        load.start()
    for load in loads:
        load.wait()
    groups = LOOK // LANES
    ids = ids_ref[...]
    owner = ids >> 12
    owners = iota((32, LANES), 0)
    running = jnp.zeros((32, LANES), F32)
    for i in range(groups):
        hit = jnp.where(owner[i:i + 1, :] == owners, 1.0, 0.0)
        o_ref[i * 32:(i + 1) * 32, 0:LANES] = hit.astype(BF16)
        o_ref[i * 32:(i + 1) * 32, LANES:2 * LANES] = running.astype(BF16)
        running = running + hit
    before = one_hot(iota((LANES, LANES), 0) < iota((LANES, LANES), 1))
    weights = jnp.concatenate([before, jnp.ones((LANES, LANES), BF16)], axis=0)
    prefix = jnp.dot(o_ref[...], weights, preferred_element_type=F32)
    totals = jnp.concatenate([running, jnp.zeros((LANES - 32, LANES), F32)], axis=0)
    count_row = lax.dot_general(jnp.ones((8, LANES), BF16), totals.astype(BF16), NT,
                                preferred_element_type=F32).astype(I32)
    blocks_row = (count_row + (LANES - 1)) >> 7
    start_row = jnp.dot(blocks_row.astype(F32).astype(BF16), before, preferred_element_type=F32)
    start_col = jnp.sum(
        jnp.where(iota((32, LANES), 1) < iota((32, LANES), 0),
                  jnp.broadcast_to(blocks_row[0:1, :].astype(F32), (32, LANES)), 0.0),
        axis=1, keepdims=True) * float(LANES)
    start_all = jnp.broadcast_to(start_col, (32, LANES))
    for i in range(groups):
        hit = owner[i:i + 1, :] == owners
        pos = jnp.sum(jnp.where(hit, prefix[i * 32:(i + 1) * 32, :] + start_all, 0.0),
                      axis=0, keepdims=True).astype(I32)
        key = (((ids[i:i + 1, :] & (ROWS_DEV - 1)) << 9) | bags_ref[i:i + 1, :]) + 1
        at_hi = (pos >> 7) == iota((BLOCKS, LANES), 0)
        for piece in range(3):
            part = ((key >> (8 * piece)) & 255).astype(F32)
            a_ref[piece * BLOCKS:(piece + 1) * BLOCKS, i * LANES:(i + 1) * LANES] = jnp.where(
                at_hi, part, 0.0).astype(BF16)
        b_ref[:, i * LANES:(i + 1) * LANES] = one_hot((pos & (LANES - 1)) == iota((LANES, LANES), 0))
    placed = lax.dot_general(a_ref[...], b_ref[...], NT, preferred_element_type=F32)
    out_ref[0:3 * BLOCKS, B_DEV:WIDTH] = placed.astype(BF16)
    meta = jnp.where(iota((16, LANES), 0) < 8,
                     jnp.concatenate([start_row, start_row], axis=0),
                     jnp.concatenate([blocks_row, blocks_row], axis=0).astype(F32))
    out_ref[3 * BLOCKS:3 * BLOCKS + 16, B_DEV:WIDTH] = meta.astype(BF16)
    out_ref[3 * BLOCKS + 16:E, B_DEV:WIDTH] = jnp.zeros((E - 3 * BLOCKS - 16, LANES), BF16)
    eye = one_hot(iota((E, E), 0) == iota((E, E), 1))
    out_ref[:, 0:B_DEV] = lax.dot_general(eye, g_ref[...], NT, preferred_element_type=F32).astype(BF16)


def pack(ids, bags, grads):
    return pl.pallas_call(
        pack_kernel,
        out_shape=jax.ShapeDtypeStruct((E, WIDTH), BF16),
        in_specs=[HBM] * 3,
        scratch_shapes=[pltpu.VMEM((3 * BLOCKS, LOOK), BF16),
                        pltpu.VMEM((LANES, LOOK), BF16),
                        pltpu.VMEM((TOUCH, 2 * LANES), BF16),
                        pltpu.VMEM((32, LANES), I32), pltpu.VMEM((32, LANES), I32),
                        pltpu.VMEM((B_DEV, E), BF16), pltpu.SemaphoreType.DMA((3,))],
        cost_estimate=cost(4),
        compiler_params=PARAMS,
        name="pack",
    )(*[in_hbm(a) for a in (ids, bags, grads)])


def gather_kernel(z_ref, *refs, count, split):
    packets = refs[0:count + split]
    x_ref, k_ref, m_ref, all_ref, scalar_ref, sem = refs[count + split:]
    copies = []
    for d in range(count):
        tail = packets[d + split][3 * BLOCKS - 128 * split:3 * BLOCKS + 16 - 128 * split, B_DEV:WIDTH]
        side = tail.astype(F32).astype(I32)
        m_ref[d] = jnp.where(iota((8, LANES), 0) == 0, side[0:8], side[8:16])
        copies.append(pltpu.make_async_copy(m_ref.at[d], scalar_ref.at[d], sem.at[d]))
        copies[d].start()
    for d in range(count):
        low = packets[d][0:2 * BLOCKS, B_DEV:WIDTH].astype(F32).astype(I32)
        top = packets[d + split][2 * BLOCKS - 128 * split:3 * BLOCKS - 128 * split, B_DEV:WIDTH]
        all_ref[d, 0:BLOCKS] = (low[0:BLOCKS] + (low[BLOCKS:2 * BLOCKS] << 8)
                                + (top.astype(F32).astype(I32) << 16)) - 1
        all_ref[d, BLOCKS:BLOCKS + 16] = jnp.zeros((16, LANES), I32)
    for copy in copies:
        copy.wait()
    for d in range(count):
        first = scalar_ref[d, 0, NX * z_ref[0]]
        last = scalar_ref[d, 0, NX * z_ref[0] + NX - 1] + scalar_ref[d, 1, NX * z_ref[0] + NX - 1]
        k_ref[d] = all_ref[d, pl.ds(first, 16), :] >> 9

        def pair(j, _, d=d, first=first):
            lines = [all_ref[d, pl.ds(first + 2 * j + i, 1), :] & (B_DEV - 1) for i in range(2)]
            picks = jnp.concatenate([one_hot(line == iota((B_DEV, LANES), 0)) for line in lines], axis=1)
            for part in range(1 + split):
                rows = E >> split
                got = jnp.dot(packets[d + part][:, 0:B_DEV], picks,
                              preferred_element_type=F32).astype(BF16)
                for i in range(2):
                    x_ref[d, 2 * j + i, part * rows:(part + 1) * rows] = got[:, i * LANES:(i + 1) * LANES]
            return 0

        lax.fori_loop(0, (last - first + 1) >> 1, pair, 0)


def gather(z, packets, split):
    count = len(packets) - split
    return pl.pallas_call(
        lambda *refs: gather_kernel(*refs, count=count, split=split),
        out_shape=(jax.ShapeDtypeStruct((count, 16, E, LANES), BF16),
                   jax.ShapeDtypeStruct((count, 16, LANES), I32),
                   jax.ShapeDtypeStruct((count, 8, LANES), I32)),
        in_specs=[SMEM] + [VMEM] * len(packets),
        scratch_shapes=[pltpu.VMEM((count, BLOCKS + 16, LANES), I32), pltpu.SMEM((count, 8, LANES), I32),
                        pltpu.SemaphoreType.DMA((count,))],
        cost_estimate=cost(2 + count),
        compiler_params=PARAMS,
    )(z, *packets)


def sums_kernel(at_ref, *refs, counts, base, many):
    groups = len(counts)
    metas, xs, keys = refs[0:groups], refs[groups:2 * groups], refs[2 * groups:3 * groups]
    rows_ref, send_ref, keep_ref, all_ref, k_ref = refs[3 * groups:]
    for m in range(many):
        column = at_ref[base + m]
        filled = jnp.int32(0)
        for n in range(groups):
            for d in range(counts[n]):
                found = metas[n][d, 1, at_ref[4] + column]
                first = metas[n][d, 0, at_ref[4] + column] - metas[n][d, 0, at_ref[4]]

                def move(j, _, n=n, d=d, filled=filled, first=first):
                    all_ref[filled + j] = xs[n][d, first + j]
                    k_ref[pl.ds(filled + j, 1), :] = keys[n][d, pl.ds(first + j, 1), :]
                    return 0

                lax.fori_loop(0, found, move, 0)
                filled = filled + found
        rounds = (filled + 7) >> 3

        def blank(j, _):
            all_ref[j] = jnp.zeros((E, LANES), BF16)
            k_ref[pl.ds(j, 1), :] = jnp.full((1, LANES), -1, I32)
            return 0

        lax.fori_loop(filled, rounds * 8, blank, 0)
        send_ref[m] = jnp.zeros((HALF, E), F32)
        keep_ref[m] = jnp.zeros((HALF, E), F32)

        def accumulate(r, _, m=m):
            wide = jnp.concatenate([all_ref[8 * r + j] for j in range(8)], axis=1)
            lines = [k_ref[pl.ds(8 * r + j, 1), :] for j in range(8)]
            for h, out_ref in enumerate((send_ref, keep_ref)):
                mine = rows_ref[base + m, h * HALF:(h + 1) * HALF, :]
                hits = jnp.concatenate([one_hot(mine == line) for line in lines], axis=1)
                out_ref[m] += lax.dot_general(hits, wide, NT, preferred_element_type=F32)
            return 0

        lax.fori_loop(0, rounds, accumulate, 0)


def cost(us):
    return pl.CostEstimate(flops=int(us * 6e8), bytes_accessed=int(us * 3e6), transcendentals=0)


def sums(at, base, many, gathered, rows):
    counts = tuple(g[0].shape[0] for g in gathered)
    total = sum(counts)
    return pl.pallas_call(
        lambda *refs: sums_kernel(*refs, counts=counts, base=base, many=many),
        in_specs=[SMEM] * (1 + len(counts)) + [VMEM] * (2 * len(counts) + 1),
        scratch_shapes=[pltpu.VMEM((4 * total, E, LANES), BF16), pltpu.VMEM((4 * total, LANES), I32)],
        out_shape=[jax.ShapeDtypeStruct((many, HALF, E), F32)] * 2,
        cost_estimate=cost(2 * many),
        compiler_params=PARAMS,
    )(at, *[g[2] for g in gathered], *[g[0] for g in gathered], *[g[1] for g in gathered], rows)


def listed_kernel(list_ref, rows_ref, accum_ref, table_ref, out_ref):
    rows = rows_ref[NX - 1]
    hi = jnp.where((rows >> 7) == iota((TOUCH, LANES), 1), 1.0, 0.0)
    padded = jnp.concatenate([accum_ref[...], jnp.zeros((LANES - 32, LANES), F32)], axis=0)
    line = jnp.dot(hi, padded, precision=lax.Precision.HIGHEST, preferred_element_type=F32)
    mine = jnp.where((rows & (LANES - 1)) == iota((TOUCH, LANES), 1), line, 0.0)
    out_ref[0:TOUCH, E:] = jnp.broadcast_to(jnp.sum(mine, axis=1, keepdims=True), (TOUCH, LANES))
    out_ref[TOUCH:, E:] = accum_ref[...]
    out_ref[TOUCH:, 0:E] = jnp.zeros((32, E), F32)

    def step(i, _):
        for j in range(16):
            row = list_ref[i >> 3, (i & 7) * 16 + j]
            out_ref[pl.ds(i * 16 + j, 1), 0:E] = table_ref[pl.ds(row, 1), :]
        return 0

    lax.fori_loop(0, TOUCH // 16, step, 0)


def listed_values(order, rows, accum, table):
    return pl.pallas_call(
        listed_kernel,
        out_shape=jax.ShapeDtypeStruct((TOUCH + 32, E + LANES), F32),
        in_specs=[SMEM, VMEM, VMEM, VMEM],
        cost_estimate=cost(6),
        compiler_params=PARAMS,
        name="listed_values",
    )(order, rows, accum, table)


def update_kernel(*refs):
    plan_ref, list_ref, table_ref, listed_hbm, rows_ref = refs[0:5]
    chunks = refs[5:13]
    table_out, accum_out, new_ref, listed_ref, u_ref, lhs_ref, rhs_ref, load_sem, store_sem = refs[13:]
    tiles = ROWS_DEV // TILE
    listed_load = pltpu.make_async_copy(listed_hbm, listed_ref, load_sem.at[tiles])
    listed_load.start()

    def load(b):
        at = pl.ds(b * TILE if isinstance(b, int) else pl.multiple_of(b * TILE, TILE), TILE)
        return pltpu.make_async_copy(table_ref.at[at], new_ref.at[at], load_sem.at[b])

    for b in range(tiles):
        load(b).start()
    lane = iota((PIECE, LANES), 1)
    pieces = []
    for n in range(8):
        for half in range(2):
            start = (n >> 2) * HALF + half * (HALF // 2) + (n & 3) * PIECE
            at = slice(start, start + PIECE)
            g = chunks[n][half * PIECE:(half + 1) * PIECE, :]
            mean = jnp.sum(g * g, axis=1, keepdims=True) * (1.0 / E)
            rows = rows_ref[NX - 1, at, :]
            lhs_ref[at, :] = jnp.where((rows >> 7) == lane, mean, 0.0)
            rhs_ref[at, :] = jnp.where((rows & (LANES - 1)) == lane, 1.0, 0.0)
            pieces.append((n, half, at, mean))
    listed_load.wait()
    for n, half, at, mean in pieces:
        now = listed_ref[at, E:E + 1] + mean
        place = plan_ref[16 + n]
        place = (place >> 2) * HALF + half * (HALF // 2) + (place & 3) * PIECE
        u_ref[pl.ds(pl.multiple_of(place, PIECE), PIECE), :] = (
            listed_ref[at, 0:E]
            - 0.5 * chunks[n][half * PIECE:(half + 1) * PIECE, :] / (jnp.sqrt(now) + 1e-08))

    def put(n):
        new_ref[pl.ds(list_ref[n], 1), :] = u_ref[pl.ds(n, 1), :]

    def store(b):
        at = pl.ds(b * TILE if isinstance(b, int) else pl.multiple_of(b * TILE, TILE), TILE)
        return pltpu.make_async_copy(new_ref.at[at], table_out.at[at], store_sem.at[b])

    def tile(b, _):
        first, last = plan_ref[b], plan_ref[b + 1]
        whole = (last - first) >> 3

        def step(i, _):
            for j in range(8):
                put(first + i * 8 + j)
            return 0

        load(b).wait()
        lax.fori_loop(0, whole, step, 0)
        lax.fori_loop(first + whole * 8, last, lambda n, _: (put(n), 0)[1], 0)
        store(b).start()
        return 0

    lax.fori_loop(0, ROWS_DEV // TILE, tile, 0)
    added = lax.dot_general(lhs_ref[...], rhs_ref[...], TN, precision=lax.Precision.HIGHEST,
                            preferred_element_type=F32)
    accum_out[...] = listed_ref[TOUCH:, E:] + added[0:32, :]
    for b in range(ROWS_DEV // TILE):
        store(b).wait()


def update(plan, natural, table, listed, rows, chunks):
    return pl.pallas_call(
        update_kernel,
        out_shape=(jax.ShapeDtypeStruct((ROWS_DEV, E), F32), jax.ShapeDtypeStruct((32, LANES), F32)),
        in_specs=[SMEM, SMEM, HBM, HBM] + [VMEM] * 9,
        out_specs=(HBM, VMEM),
        scratch_shapes=[pltpu.VMEM((ROWS_DEV, E), F32), pltpu.VMEM((TOUCH + 32, E + LANES), F32),
                        pltpu.VMEM((TOUCH, E), F32),
                        pltpu.VMEM((TOUCH, LANES), F32), pltpu.VMEM((TOUCH, LANES), F32),
                        pltpu.SemaphoreType.DMA((ROWS_DEV // TILE + 1,)),
                        pltpu.SemaphoreType.DMA((ROWS_DEV // TILE,))],
        compiler_params=PARAMS,
        name="update",
    )(plan, natural, in_hbm(table), in_hbm(listed), rows, *chunks)


def z_pairs(k):
    return [(z * NX + x, ((z + k) % NZ) * NX + x) for z in range(NZ) for x in range(NX)]


def x_pairs(k):
    return [(z * NX + x, z * NX + (x + k) % NX) for z in range(NZ) for x in range(NX)]


def y_pairs(k):
    return [(y * NC + c, ((y + k) % NY) * NC + c) for y in range(NY) for c in range(NC)]


C_PAIRS = [(y * NC + c, y * NC + 1 - c) for y in range(NY) for c in range(NC)]


def body(table, accum, pooled_grad, row_ids, bag_ids, touched):
    grp = lax.axis_index("grp")
    me = lax.axis_index("shard")
    y, c = grp // NC, grp % NC
    z, x = me // NX, me % NX

    def ordered(listed):
        halves = listed.reshape(NC, 2, NY, PIECE)
        halves = jnp.where(c == 0, halves[::-1], halves)
        doubled = jnp.concatenate([halves, halves], axis=2)
        return lax.dynamic_slice(doubled, (0, 0, y, 0), (NC, 2, NY, PIECE)).reshape(TOUCH)

    own_list = touched.reshape(TOUCH)
    lists = {0: ordered(own_list)}
    for k in range(1, NX):
        lists[k] = ordered(lax.ppermute(own_list, "shard", x_pairs(-k)))
    stacked = jnp.stack([lists[k] for k in ORDER])[:, :, None]
    rows = jnp.broadcast_to(stacked, (NX, TOUCH, LANES))
    order = lists[0].reshape(8, LANES)
    bounds = jnp.sum((own_list[None, :] < TILE * jnp.arange(16, dtype=I32)[:, None]).astype(I32), axis=1)
    turn = (y + jnp.arange(NY, dtype=I32)) % NY
    plan = jnp.concatenate([bounds, (1 - c) * NY + turn, c * NY + turn])

    packet = pack(row_ids.reshape(32, LANES), bag_ids.reshape(32, LANES),
                  pooled_grad.reshape(B_DEV, E))
    got = {0: packet}
    for k in range(1, 4):
        got[-k] = lax.ppermute(got[1 - k], "shard", z_pairs(1))
        got[k] = lax.ppermute(got[k - 1], "shard", z_pairs(-1))
    last = [lax.ppermute(got[-3][:E // 2], "shard", z_pairs(1))]
    last.append(lax.ppermute(got[3][E // 2:], "shard", z_pairs(-1)))
    gathered = []
    for sources in ((0,), (-1, 1), (-2, 2), (-3, 3), None):
        packets = [got[k] for k in sources] if sources else last
        gathered.append(gather(z.reshape(1), packets, int(sources is None)))

    listed = listed_values(order, rows, accum.reshape(32, LANES), table)
    at = jnp.concatenate([(x + jnp.array(ORDER, I32)) % NX, (NX * z).reshape(1)])
    first, second = {}, {}
    for base, ks in ((0, (2,)), (1, (1, 3)), (3, (0,))):
        send, keep = sums(at, base, len(ks), gathered, rows)
        swapped = lax.ppermute(send, "grp", C_PAIRS)
        for n, k in enumerate(ks):
            first[k] = keep[n, :HALF // 2] + swapped[n, :HALF // 2]
            if k:
                first[k] = lax.ppermute(first[k], "shard", x_pairs(k))
            second[k] = (keep[n, HALF // 2:] + swapped[n, HALF // 2:]).reshape(NY, PIECE, E)
    side = [jnp.stack([second[k][j] for k in range(NX)]) for j in range(NY)]
    for j in (2, 1, 3):
        side[j] = lax.ppermute(side[j], "grp", y_pairs(j))
    low = (first[0] + first[2] + first[1] + first[3]).reshape(NY, PIECE, E)
    part_low = low[0]
    for j in (2, 1, 3):
        part_low = part_low + lax.ppermute(low[j], "grp", y_pairs(j))
    high = side[0] + side[2] + side[1] + side[3]
    part_high = high[0]
    for k in (2, 1, 3):
        part_high = part_high + lax.ppermute(high[k], "shard", x_pairs(k))
    part = jnp.concatenate([part_low, part_high], axis=0)
    mine = [part] + [lax.ppermute(part, "grp", y_pairs(-j)) for j in range(1, NY)]
    other = [lax.ppermute(m, "grp", C_PAIRS) for m in mine]
    new_table, new_accum = update(plan, own_list, table, listed, rows, other + mine)
    return (new_table, new_accum.reshape(ROWS_DEV))


def solution(mesh):
    return jax.shard_map(
        body,
        mesh=mesh,
        in_specs=(
            P("shard", None),
            P("shard"),
            P("grp", "shard", None, None),
            P("grp", "shard", None),
            P("grp", "shard", None),
            P("shard", None),
        ),
        out_specs=(P("shard", None), P("shard")),
        check_vma=False,
    )
```

```python
import jax
import jax.numpy as jnp
from jax import lax
from jax.experimental import pallas as pl
from jax.experimental.pallas import tpu as pltpu
from jax.sharding import PartitionSpec as P


E = 256
ROWS_DEV = 4096
TOUCH = 1024
HALF = TOUCH // 2
QUART = TOUCH // 8
TILE = 512
LOOK = 4096
B_DEV = 512
LANES = 128
BLOCKS = 64
WIDTH = B_DEV + LANES
NZ, NX, NY, NC = 8, 4, 4, 2
F32 = jnp.float32
BF16 = jnp.bfloat16
I32 = jnp.int32
NT = (((1,), (1,)), ((), ()))
TN = (((0,), (0,)), ((), ()))
ORDER = (2, 1, 3, 0)
SMEM = pl.BlockSpec(memory_space=pltpu.SMEM)
VMEM = pl.BlockSpec(memory_space=pltpu.VMEM)
HBM = pl.BlockSpec(memory_space=pltpu.HBM)
PARAMS = pltpu.CompilerParams(vmem_limit_bytes=14 << 20)


def iota(shape, dim):
    return lax.broadcasted_iota(I32, shape, dim)


def one_hot(mask):
    return jnp.where(mask, 1.0, 0.0).astype(BF16)


def in_hbm(array):
    return pltpu.with_memory_space_constraint(array, pltpu.HBM)


def pack_kernel(ids_hbm, bags_hbm, g_hbm, out_ref, a_ref, b_ref, o_ref, ids_ref, bags_ref, g_ref, sem):
    loads = [pltpu.make_async_copy(src, dst, sem.at[n])
             for n, (src, dst) in enumerate(((ids_hbm, ids_ref), (bags_hbm, bags_ref), (g_hbm, g_ref)))]
    for load in loads:
        load.start()
    for load in loads:
        load.wait()
    groups = LOOK // LANES
    ids = ids_ref[...]
    owner = ids >> 12
    owners = iota((32, LANES), 0)
    running = jnp.zeros((32, LANES), F32)
    for i in range(groups):
        hit = jnp.where(owner[i:i + 1, :] == owners, 1.0, 0.0)
        o_ref[i * 32:(i + 1) * 32, 0:LANES] = hit.astype(BF16)
        o_ref[i * 32:(i + 1) * 32, LANES:2 * LANES] = running.astype(BF16)
        running = running + hit
    before = one_hot(iota((LANES, LANES), 0) < iota((LANES, LANES), 1))
    weights = jnp.concatenate([before, jnp.ones((LANES, LANES), BF16)], axis=0)
    prefix = jnp.dot(o_ref[...], weights, preferred_element_type=F32)
    totals = jnp.concatenate([running, jnp.zeros((LANES - 32, LANES), F32)], axis=0)
    count_row = lax.dot_general(jnp.ones((8, LANES), BF16), totals.astype(BF16), NT,
                                preferred_element_type=F32).astype(I32)
    blocks_row = (count_row + (LANES - 1)) >> 7
    start_row = jnp.dot(blocks_row.astype(F32).astype(BF16), before, preferred_element_type=F32)
    start_col = jnp.sum(
        jnp.where(iota((32, LANES), 1) < iota((32, LANES), 0),
                  jnp.broadcast_to(blocks_row[0:1, :].astype(F32), (32, LANES)), 0.0),
        axis=1, keepdims=True) * float(LANES)
    start_all = jnp.broadcast_to(start_col, (32, LANES))
    for i in range(groups):
        hit = owner[i:i + 1, :] == owners
        pos = jnp.sum(jnp.where(hit, prefix[i * 32:(i + 1) * 32, :] + start_all, 0.0),
                      axis=0, keepdims=True).astype(I32)
        key = (((ids[i:i + 1, :] & (ROWS_DEV - 1)) << 9) | bags_ref[i:i + 1, :]) + 1
        at_hi = (pos >> 7) == iota((BLOCKS, LANES), 0)
        for piece in range(3):
            part = ((key >> (8 * piece)) & 255).astype(F32)
            a_ref[piece * BLOCKS:(piece + 1) * BLOCKS, i * LANES:(i + 1) * LANES] = jnp.where(
                at_hi, part, 0.0).astype(BF16)
        b_ref[:, i * LANES:(i + 1) * LANES] = one_hot((pos & (LANES - 1)) == iota((LANES, LANES), 0))
    placed = lax.dot_general(a_ref[...], b_ref[...], NT, preferred_element_type=F32)
    out_ref[0:3 * BLOCKS, B_DEV:WIDTH] = placed.astype(BF16)
    meta = jnp.where(iota((16, LANES), 0) < 8,
                     jnp.concatenate([start_row, start_row], axis=0),
                     jnp.concatenate([blocks_row, blocks_row], axis=0).astype(F32))
    out_ref[3 * BLOCKS:3 * BLOCKS + 16, B_DEV:WIDTH] = meta.astype(BF16)
    out_ref[3 * BLOCKS + 16:E, B_DEV:WIDTH] = jnp.zeros((E - 3 * BLOCKS - 16, LANES), BF16)
    eye = one_hot(iota((E, E), 0) == iota((E, E), 1))
    out_ref[:, 0:B_DEV] = lax.dot_general(eye, g_ref[...], NT, preferred_element_type=F32).astype(BF16)


def pack(ids, bags, grads):
    return pl.pallas_call(
        pack_kernel,
        out_shape=jax.ShapeDtypeStruct((E, WIDTH), BF16),
        in_specs=[HBM] * 3,
        scratch_shapes=[pltpu.VMEM((3 * BLOCKS, LOOK), BF16),
                        pltpu.VMEM((LANES, LOOK), BF16),
                        pltpu.VMEM((TOUCH, 2 * LANES), BF16),
                        pltpu.VMEM((32, LANES), I32), pltpu.VMEM((32, LANES), I32),
                        pltpu.VMEM((B_DEV, E), BF16), pltpu.SemaphoreType.DMA((3,))],
        cost_estimate=cost(4),
        compiler_params=PARAMS,
        name="pack",
    )(*[in_hbm(a) for a in (ids, bags, grads)])


def gather_kernel(z_ref, *refs, count, split):
    packets = refs[0:count + split]
    x_ref, k_ref, m_ref, all_ref, scalar_ref, sem = refs[count + split:]
    copies = []
    for d in range(count):
        cut = 128 if split and d == count - 1 else 0
        tail = packets[-1] if cut else packets[d]
        side = tail[3 * BLOCKS - cut:3 * BLOCKS + 16 - cut, B_DEV:WIDTH].astype(F32).astype(I32)
        m_ref[d] = jnp.where(iota((8, LANES), 0) == 0, side[0:8], side[8:16])
        copies.append(pltpu.make_async_copy(m_ref.at[d], scalar_ref.at[d], sem.at[d]))
        copies[d].start()
    for d in range(count):
        cut = 128 if split and d == count - 1 else 0
        tail = packets[-1] if cut else packets[d]
        low = packets[d][0:2 * BLOCKS, B_DEV:WIDTH].astype(F32).astype(I32)
        top = tail[2 * BLOCKS - cut:3 * BLOCKS - cut, B_DEV:WIDTH].astype(F32).astype(I32)
        all_ref[d, 0:BLOCKS] = (low[0:BLOCKS] + (low[BLOCKS:2 * BLOCKS] << 8) + (top << 16)) - 1
        all_ref[d, BLOCKS:BLOCKS + 16] = jnp.zeros((16, LANES), I32)
    for copy in copies:
        copy.wait()
    for d in range(count):
        parts = packets[d:] if split and d == count - 1 else packets[d:d + 1]
        first = scalar_ref[d, 0, NX * z_ref[0]]
        last = scalar_ref[d, 0, NX * z_ref[0] + NX - 1] + scalar_ref[d, 1, NX * z_ref[0] + NX - 1]
        k_ref[d] = all_ref[d, pl.ds(first, 16), :] >> 9

        def pair(j, _, d=d, first=first, parts=parts):
            lines = [all_ref[d, pl.ds(first + 2 * j + i, 1), :] & (B_DEV - 1) for i in range(2)]
            picks = jnp.concatenate([one_hot(line == iota((B_DEV, LANES), 0)) for line in lines], axis=1)
            rows = E // len(parts)
            for n, part in enumerate(parts):
                got = jnp.dot(part[:, 0:B_DEV], picks, preferred_element_type=F32).astype(BF16)
                for i in range(2):
                    x_ref[d, 2 * j + i, n * rows:(n + 1) * rows] = got[:, i * LANES:(i + 1) * LANES]
            return 0

        lax.fori_loop(0, (last - first + 1) >> 1, pair, 0)


def gather(z, packets, split):
    count = len(packets) - split
    return pl.pallas_call(
        lambda *refs: gather_kernel(*refs, count=count, split=split),
        out_shape=(jax.ShapeDtypeStruct((count, 16, E, LANES), BF16),
                   jax.ShapeDtypeStruct((count, 16, LANES), I32),
                   jax.ShapeDtypeStruct((count, 8, LANES), I32)),
        in_specs=[SMEM] + [VMEM] * len(packets),
        scratch_shapes=[pltpu.VMEM((count, BLOCKS + 16, LANES), I32), pltpu.SMEM((count, 8, LANES), I32),
                        pltpu.SemaphoreType.DMA((count,))],
        cost_estimate=cost(2 + count),
        compiler_params=PARAMS,
    )(z, *packets)


def sums_kernel(at_ref, *refs, counts, base, many):
    groups = len(counts)
    metas, xs, keys = refs[0:groups], refs[groups:2 * groups], refs[2 * groups:3 * groups]
    rows_ref, out_ref, all_ref, k_ref = refs[3 * groups:]
    for m in range(many):
        column = at_ref[base + m]
        filled = jnp.int32(0)
        for n in range(groups):
            for d in range(counts[n]):
                found = metas[n][d, 1, at_ref[4] + column]
                first = metas[n][d, 0, at_ref[4] + column] - metas[n][d, 0, at_ref[4]]

                def move(j, _, n=n, d=d, filled=filled, first=first):
                    all_ref[filled + j] = xs[n][d, first + j]
                    k_ref[pl.ds(filled + j, 1), :] = keys[n][d, pl.ds(first + j, 1), :]
                    return 0

                lax.fori_loop(0, found, move, 0)
                filled = filled + found
        rounds = (filled + 7) >> 3

        def blank(j, _):
            all_ref[j] = jnp.zeros((E, LANES), BF16)
            k_ref[pl.ds(j, 1), :] = jnp.full((1, LANES), -1, I32)
            return 0

        lax.fori_loop(filled, rounds * 8, blank, 0)
        out_ref[m] = jnp.zeros((HALF, E), F32)

        def accumulate(r, _, m=m):
            wide = jnp.concatenate([all_ref[8 * r + j] for j in range(8)], axis=1)
            lines = [k_ref[pl.ds(8 * r + j, 1), :] for j in range(8)]
            mine = rows_ref[base + m]
            hits = jnp.concatenate([one_hot(mine == line) for line in lines], axis=1)
            out_ref[m] += lax.dot_general(hits, wide, NT, preferred_element_type=F32)
            return 0

        lax.fori_loop(0, rounds, accumulate, 0)


def cost(us):
    return pl.CostEstimate(flops=int(us * 6e8), bytes_accessed=int(us * 3e6), transcendentals=0)


def sums(at, base, many, gathered, rows):
    counts = tuple(g[0].shape[0] for g in gathered)
    total = sum(counts)
    return pl.pallas_call(
        lambda *refs: sums_kernel(*refs, counts=counts, base=base, many=many),
        in_specs=[SMEM] * (1 + len(counts)) + [VMEM] * (2 * len(counts) + 1),
        scratch_shapes=[pltpu.VMEM((4 * total, E, LANES), BF16), pltpu.VMEM((4 * total, LANES), I32)],
        out_shape=jax.ShapeDtypeStruct((many, HALF, E), F32),
        cost_estimate=cost(2 * many),
        compiler_params=PARAMS,
    )(at, *[g[2] for g in gathered], *[g[0] for g in gathered], *[g[1] for g in gathered], rows)


def listed_kernel(list_ref, rows_ref, accum_ref, table_ref, out_ref):
    rows = rows_ref[...]
    hi = jnp.where((rows >> 7) == iota((TOUCH, LANES), 1), 1.0, 0.0)
    padded = jnp.concatenate([accum_ref[...], jnp.zeros((LANES - 32, LANES), F32)], axis=0)
    line = jnp.dot(hi, padded, precision=lax.Precision.HIGHEST, preferred_element_type=F32)
    mine = jnp.where((rows & (LANES - 1)) == iota((TOUCH, LANES), 1), line, 0.0)
    out_ref[0:TOUCH, E:] = jnp.broadcast_to(jnp.sum(mine, axis=1, keepdims=True), (TOUCH, LANES))
    out_ref[TOUCH:, E:] = accum_ref[...]
    out_ref[TOUCH:, 0:E] = jnp.zeros((32, E), F32)

    def step(i, _):
        for j in range(16):
            row = list_ref[i >> 3, (i & 7) * 16 + j]
            out_ref[pl.ds(i * 16 + j, 1), 0:E] = table_ref[pl.ds(row, 1), :]
        return 0

    lax.fori_loop(0, TOUCH // 16, step, 0)


def listed_values(order, rows, accum, table):
    return pl.pallas_call(
        listed_kernel,
        out_shape=jax.ShapeDtypeStruct((TOUCH + 32, E + LANES), F32),
        in_specs=[SMEM, VMEM, VMEM, VMEM],
        cost_estimate=cost(6),
        compiler_params=PARAMS,
        name="listed_values",
    )(order, rows, accum, table)


def update_kernel(*refs):
    plan_ref, list_ref, table_ref, listed_hbm, rows_ref = refs[0:5]
    chunks = refs[5:13]
    table_out, accum_out, new_ref, listed_ref, u_ref, lhs_ref, rhs_ref, load_sem, store_sem = refs[13:]
    tiles = ROWS_DEV // TILE
    listed_load = pltpu.make_async_copy(listed_hbm, listed_ref, load_sem.at[tiles])
    listed_load.start()

    def load(b):
        at = pl.ds(b * TILE if isinstance(b, int) else pl.multiple_of(b * TILE, TILE), TILE)
        return pltpu.make_async_copy(table_ref.at[at], new_ref.at[at], load_sem.at[b])

    for b in range(tiles):
        load(b).start()
    lane = iota((QUART, LANES), 1)
    means = []
    for n in range(8):
        at = slice(n * QUART, (n + 1) * QUART)
        g = chunks[n][...]
        means.append(jnp.sum(g * g, axis=1, keepdims=True) * (1.0 / E))
        rows = rows_ref[at, :]
        lhs_ref[at, :] = jnp.where((rows >> 7) == lane, means[n], 0.0)
        rhs_ref[at, :] = jnp.where((rows & (LANES - 1)) == lane, 1.0, 0.0)
    listed_load.wait()
    for n in range(8):
        at = slice(n * QUART, (n + 1) * QUART)
        now = listed_ref[at, E:E + 1] + means[n]
        u_ref[pl.ds(pl.multiple_of(plan_ref[16 + n] * QUART, QUART), QUART), :] = (
            listed_ref[at, 0:E] - 0.5 * chunks[n][...] / (jnp.sqrt(now) + 1e-08))

    def put(n):
        new_ref[pl.ds(list_ref[n], 1), :] = u_ref[pl.ds(n, 1), :]

    def store(b):
        at = pl.ds(b * TILE if isinstance(b, int) else pl.multiple_of(b * TILE, TILE), TILE)
        return pltpu.make_async_copy(new_ref.at[at], table_out.at[at], store_sem.at[b])

    def tile(b, _):
        first, last = plan_ref[b], plan_ref[b + 1]
        whole = (last - first) >> 3

        def step(i, _):
            for j in range(8):
                put(first + i * 8 + j)
            return 0

        load(b).wait()
        lax.fori_loop(0, whole, step, 0)
        lax.fori_loop(first + whole * 8, last, lambda n, _: (put(n), 0)[1], 0)
        store(b).start()
        return 0

    lax.fori_loop(0, ROWS_DEV // TILE, tile, 0)
    added = lax.dot_general(lhs_ref[...], rhs_ref[...], TN, precision=lax.Precision.HIGHEST,
                            preferred_element_type=F32)
    accum_out[...] = listed_ref[TOUCH:, E:] + added[0:32, :]
    for b in range(ROWS_DEV // TILE):
        store(b).wait()


def update(plan, natural, table, listed, rows, chunks):
    return pl.pallas_call(
        update_kernel,
        out_shape=(jax.ShapeDtypeStruct((ROWS_DEV, E), F32), jax.ShapeDtypeStruct((32, LANES), F32)),
        in_specs=[SMEM, SMEM, HBM, HBM] + [VMEM] * 9,
        out_specs=(HBM, VMEM),
        scratch_shapes=[pltpu.VMEM((ROWS_DEV, E), F32), pltpu.VMEM((TOUCH + 32, E + LANES), F32),
                        pltpu.VMEM((TOUCH, E), F32),
                        pltpu.VMEM((TOUCH, LANES), F32), pltpu.VMEM((TOUCH, LANES), F32),
                        pltpu.SemaphoreType.DMA((ROWS_DEV // TILE + 1,)),
                        pltpu.SemaphoreType.DMA((ROWS_DEV // TILE,))],
        compiler_params=PARAMS,
        name="update",
    )(plan, natural, in_hbm(table), in_hbm(listed), rows, *chunks)


def z_pairs(k):
    return [(z * NX + x, ((z + k) % NZ) * NX + x) for z in range(NZ) for x in range(NX)]


def x_pairs(k):
    return [(z * NX + x, z * NX + (x + k) % NX) for z in range(NZ) for x in range(NX)]


def y_pairs(k):
    return [(y * NC + c, ((y + k) % NY) * NC + c) for y in range(NY) for c in range(NC)]


C_PAIRS = [(y * NC + c, y * NC + 1 - c) for y in range(NY) for c in range(NC)]


def body(table, accum, pooled_grad, row_ids, bag_ids, touched):
    grp = lax.axis_index("grp")
    me = lax.axis_index("shard")
    y, c = grp // NC, grp % NC
    z, x = me // NX, me % NX

    def ordered(listed):
        halves = listed.reshape(NC, NY, QUART)
        halves = jnp.where(c == 0, halves[::-1], halves)
        doubled = jnp.concatenate([halves, halves], axis=1)
        return lax.dynamic_slice(doubled, (0, y, 0), (NC, NY, QUART)).reshape(TOUCH)

    own_list = touched.reshape(TOUCH)
    lists = {0: ordered(own_list)}
    for k in range(1, NX):
        lists[k] = ordered(lax.ppermute(own_list, "shard", x_pairs(-k)))
    stacked = jnp.stack([lists[k][HALF:] for k in ORDER])[:, :, None]
    rows = jnp.broadcast_to(stacked, (NX, HALF, LANES))
    all_rows = jnp.broadcast_to(lists[0][:, None], (TOUCH, LANES))
    order = lists[0].reshape(8, LANES)
    bounds = jnp.sum((own_list[None, :] < TILE * jnp.arange(16, dtype=I32)[:, None]).astype(I32), axis=1)
    turn = (y + jnp.arange(NY, dtype=I32)) % NY
    plan = jnp.concatenate([bounds, (1 - c) * NY + turn, c * NY + turn])

    packet = pack(row_ids.reshape(32, LANES), bag_ids.reshape(32, LANES),
                  pooled_grad.reshape(B_DEV, E))

    def swap(packets):
        return [lax.ppermute(p, "grp", C_PAIRS) for p in packets]

    def gather_of(packets, split):
        return gather(z.reshape(1), packets, split)

    up = down = packet
    other = swap([packet])
    gathered = [gather_of([packet], 0)]
    for _ in range(1, 4):
        up = lax.ppermute(up, "shard", z_pairs(1))
        down = lax.ppermute(down, "shard", z_pairs(-1))
        gathered.append(gather_of([up, down] + other, 0))
        other = swap([up, down])
    up = lax.ppermute(up[:E // 2], "shard", z_pairs(1))
    down = lax.ppermute(down[E // 2:], "shard", z_pairs(-1))
    gathered.append(gather_of(other + [up, down], 1))
    gathered.append(gather_of(swap([up, down]), 1))

    listed = listed_values(order, all_rows, accum.reshape(32, LANES), table)
    at = jnp.concatenate([(x + jnp.array(ORDER, I32)) % NX, (NX * z).reshape(1)])
    both = {}
    for base, ks in ((0, (2,)), (1, (1, 3)), (3, (0,))):
        found = sums(at, base, len(ks), gathered, rows)
        for n, k in enumerate(ks):
            both[k] = found[n]
            if k:
                both[k] = lax.ppermute(both[k], "shard", x_pairs(k))
    total = both[0] + both[2] + both[1] + both[3]
    part = total[0:QUART]
    for j in (2, 1, 3):
        part = part + lax.ppermute(total[j * QUART:(j + 1) * QUART], "grp", y_pairs(j))
    mine = [part] + [lax.ppermute(part, "grp", y_pairs(-j)) for j in range(1, NY)]
    other = [lax.ppermute(m, "grp", C_PAIRS) for m in mine]
    new_table, new_accum = update(plan, own_list, table, listed, all_rows, other + mine)
    return (new_table, new_accum.reshape(ROWS_DEV))


def solution(mesh):
    return jax.shard_map(
        body,
        mesh=mesh,
        in_specs=(
            P("shard", None),
            P("shard"),
            P("grp", "shard", None, None),
            P("grp", "shard", None),
            P("grp", "shard", None),
            P("shard", None),
        ),
        out_specs=(P("shard", None), P("shard")),
        check_vma=False,
    )
```

```python
import jax
import jax.numpy as jnp
from jax import lax
from jax.experimental import pallas as pl
from jax.experimental.pallas import tpu as pltpu
from jax.sharding import PartitionSpec as P


E = 256
ROWS_DEV = 4096
TOUCH = 1024
HALF = TOUCH // 2
QUART = TOUCH // 8
TILE = 512
LOOK = 4096
B_DEV = 512
LANES = 128
BLOCKS = 64
WIDTH = B_DEV + LANES
NZ, NX, NY, NC = 8, 4, 4, 2
F32 = jnp.float32
BF16 = jnp.bfloat16
I32 = jnp.int32
NT = (((1,), (1,)), ((), ()))
TN = (((0,), (0,)), ((), ()))
ORDER = (2, 1, 3, 0)
SMEM = pl.BlockSpec(memory_space=pltpu.SMEM)
VMEM = pl.BlockSpec(memory_space=pltpu.VMEM)
HBM = pl.BlockSpec(memory_space=pltpu.HBM)
PARAMS = pltpu.CompilerParams(vmem_limit_bytes=14 << 20)


def iota(shape, dim):
    return lax.broadcasted_iota(I32, shape, dim)


def one_hot(mask):
    return jnp.where(mask, 1.0, 0.0).astype(BF16)


def in_hbm(array):
    return pltpu.with_memory_space_constraint(array, pltpu.HBM)


def pack_kernel(ids_hbm, bags_hbm, g_hbm, out_ref, a_ref, b_ref, o_ref, ids_ref, bags_ref, g_ref, sem):
    loads = [pltpu.make_async_copy(src, dst, sem.at[n])
             for n, (src, dst) in enumerate(((ids_hbm, ids_ref), (bags_hbm, bags_ref), (g_hbm, g_ref)))]
    for load in loads:
        load.start()
    for load in loads:
        load.wait()
    groups = LOOK // LANES
    ids = ids_ref[...]
    owner = ids >> 12
    owners = iota((32, LANES), 0)
    running = jnp.zeros((32, LANES), F32)
    for i in range(groups):
        hit = jnp.where(owner[i:i + 1, :] == owners, 1.0, 0.0)
        o_ref[i * 32:(i + 1) * 32, 0:LANES] = hit.astype(BF16)
        o_ref[i * 32:(i + 1) * 32, LANES:2 * LANES] = running.astype(BF16)
        running = running + hit
    before = one_hot(iota((LANES, LANES), 0) < iota((LANES, LANES), 1))
    weights = jnp.concatenate([before, jnp.ones((LANES, LANES), BF16)], axis=0)
    prefix = jnp.dot(o_ref[...], weights, preferred_element_type=F32)
    totals = jnp.concatenate([running, jnp.zeros((LANES - 32, LANES), F32)], axis=0)
    count_row = lax.dot_general(jnp.ones((8, LANES), BF16), totals.astype(BF16), NT,
                                preferred_element_type=F32).astype(I32)
    blocks_row = (count_row + (LANES - 1)) >> 7
    start_row = jnp.dot(blocks_row.astype(F32).astype(BF16), before, preferred_element_type=F32)
    start_col = jnp.sum(
        jnp.where(iota((32, LANES), 1) < iota((32, LANES), 0),
                  jnp.broadcast_to(blocks_row[0:1, :].astype(F32), (32, LANES)), 0.0),
        axis=1, keepdims=True) * float(LANES)
    start_all = jnp.broadcast_to(start_col, (32, LANES))
    for i in range(groups):
        hit = owner[i:i + 1, :] == owners
        pos = jnp.sum(jnp.where(hit, prefix[i * 32:(i + 1) * 32, :] + start_all, 0.0),
                      axis=0, keepdims=True).astype(I32)
        key = (((ids[i:i + 1, :] & (ROWS_DEV - 1)) << 9) | bags_ref[i:i + 1, :]) + 1
        at_hi = (pos >> 7) == iota((BLOCKS, LANES), 0)
        for piece in range(3):
            part = ((key >> (8 * piece)) & 255).astype(F32)
            a_ref[piece * BLOCKS:(piece + 1) * BLOCKS, i * LANES:(i + 1) * LANES] = jnp.where(
                at_hi, part, 0.0).astype(BF16)
        b_ref[:, i * LANES:(i + 1) * LANES] = one_hot((pos & (LANES - 1)) == iota((LANES, LANES), 0))
    placed = lax.dot_general(a_ref[...], b_ref[...], NT, preferred_element_type=F32)
    out_ref[0:3 * BLOCKS, B_DEV:WIDTH] = placed.astype(BF16)
    meta = jnp.where(iota((16, LANES), 0) < 8,
                     jnp.concatenate([start_row, start_row], axis=0),
                     jnp.concatenate([blocks_row, blocks_row], axis=0).astype(F32))
    out_ref[3 * BLOCKS:3 * BLOCKS + 16, B_DEV:WIDTH] = meta.astype(BF16)
    out_ref[3 * BLOCKS + 16:E, B_DEV:WIDTH] = jnp.zeros((E - 3 * BLOCKS - 16, LANES), BF16)
    eye = one_hot(iota((E, E), 0) == iota((E, E), 1))
    out_ref[:, 0:B_DEV] = lax.dot_general(eye, g_ref[...], NT, preferred_element_type=F32).astype(BF16)


def pack(ids, bags, grads):
    return pl.pallas_call(
        pack_kernel,
        out_shape=jax.ShapeDtypeStruct((E, WIDTH), BF16),
        in_specs=[HBM] * 3,
        scratch_shapes=[pltpu.VMEM((3 * BLOCKS, LOOK), BF16),
                        pltpu.VMEM((LANES, LOOK), BF16),
                        pltpu.VMEM((TOUCH, 2 * LANES), BF16),
                        pltpu.VMEM((32, LANES), I32), pltpu.VMEM((32, LANES), I32),
                        pltpu.VMEM((B_DEV, E), BF16), pltpu.SemaphoreType.DMA((3,))],
        cost_estimate=cost(4),
        compiler_params=PARAMS,
        name="pack",
    )(*[in_hbm(a) for a in (ids, bags, grads)])


def gather_kernel(z_ref, *refs, count, split):
    packets = refs[0:count + split]
    x_ref, k_ref, m_ref, all_ref, scalar_ref, sem = refs[count + split:]
    copies = []
    for d in range(count):
        cut = 128 if split and d == count - 1 else 0
        tail = packets[-1] if cut else packets[d]
        side = tail[3 * BLOCKS - cut:3 * BLOCKS + 16 - cut, B_DEV:WIDTH].astype(F32).astype(I32)
        m_ref[d] = jnp.where(iota((8, LANES), 0) == 0, side[0:8], side[8:16])
        copies.append(pltpu.make_async_copy(m_ref.at[d], scalar_ref.at[d], sem.at[d]))
        copies[d].start()
    for d in range(count):
        cut = 128 if split and d == count - 1 else 0
        tail = packets[-1] if cut else packets[d]
        low = packets[d][0:2 * BLOCKS, B_DEV:WIDTH].astype(F32).astype(I32)
        top = tail[2 * BLOCKS - cut:3 * BLOCKS - cut, B_DEV:WIDTH].astype(F32).astype(I32)
        all_ref[d, 0:BLOCKS] = (low[0:BLOCKS] + (low[BLOCKS:2 * BLOCKS] << 8) + (top << 16)) - 1
        all_ref[d, BLOCKS:BLOCKS + 16] = jnp.zeros((16, LANES), I32)
    for copy in copies:
        copy.wait()
    for d in range(count):
        parts = packets[d:] if split and d == count - 1 else packets[d:d + 1]
        first = scalar_ref[d, 0, NX * z_ref[0]]
        last = scalar_ref[d, 0, NX * z_ref[0] + NX - 1] + scalar_ref[d, 1, NX * z_ref[0] + NX - 1]
        k_ref[d] = all_ref[d, pl.ds(first, 16), :] >> 9

        def pair(j, _, d=d, first=first, parts=parts):
            lines = [all_ref[d, pl.ds(first + 2 * j + i, 1), :] & (B_DEV - 1) for i in range(2)]
            picks = jnp.concatenate([one_hot(line == iota((B_DEV, LANES), 0)) for line in lines], axis=1)
            rows = E // len(parts)
            for n, part in enumerate(parts):
                got = jnp.dot(part[:, 0:B_DEV], picks, preferred_element_type=F32).astype(BF16)
                for i in range(2):
                    x_ref[d, 2 * j + i, n * rows:(n + 1) * rows] = got[:, i * LANES:(i + 1) * LANES]
            return 0

        lax.fori_loop(0, (last - first + 1) >> 1, pair, 0)


def gather(z, packets, split):
    count = len(packets) - split
    return pl.pallas_call(
        lambda *refs: gather_kernel(*refs, count=count, split=split),
        out_shape=(jax.ShapeDtypeStruct((count, 16, E, LANES), BF16),
                   jax.ShapeDtypeStruct((count, 16, LANES), I32),
                   jax.ShapeDtypeStruct((count, 8, LANES), I32)),
        in_specs=[SMEM] + [VMEM] * len(packets),
        scratch_shapes=[pltpu.VMEM((count, BLOCKS + 16, LANES), I32), pltpu.SMEM((count, 8, LANES), I32),
                        pltpu.SemaphoreType.DMA((count,))],
        cost_estimate=cost(2 + count),
        compiler_params=PARAMS,
    )(z, *packets)


def sums_kernel(at_ref, *refs, counts, base, many, fresh):
    groups = len(counts)
    metas, xs, keys = refs[0:groups], refs[groups:2 * groups], refs[2 * groups:3 * groups]
    rows_ref = refs[3 * groups]
    out_ref, all_ref, k_ref = refs[-3:]
    for m in range(many):
        column = at_ref[base + m]
        filled = jnp.int32(0)
        for n in range(groups):
            for d in range(counts[n]):
                found = metas[n][d, 1, at_ref[4] + column]
                first = metas[n][d, 0, at_ref[4] + column] - metas[n][d, 0, at_ref[4]]

                def move(j, _, n=n, d=d, filled=filled, first=first):
                    all_ref[filled + j] = xs[n][d, first + j]
                    k_ref[pl.ds(filled + j, 1), :] = keys[n][d, pl.ds(first + j, 1), :]
                    return 0

                lax.fori_loop(0, found, move, 0)
                filled = filled + found
        rounds = (filled + 7) >> 3

        def blank(j, _):
            all_ref[j] = jnp.zeros((E, LANES), BF16)
            k_ref[pl.ds(j, 1), :] = jnp.full((1, LANES), -1, I32)
            return 0

        lax.fori_loop(filled, rounds * 8, blank, 0)
        out_ref[m] = jnp.zeros((HALF, E), F32) if fresh else refs[3 * groups + 1][m]

        def accumulate(r, _, m=m):
            wide = jnp.concatenate([all_ref[8 * r + j] for j in range(8)], axis=1)
            lines = [k_ref[pl.ds(8 * r + j, 1), :] for j in range(8)]
            mine = rows_ref[base + m]
            hits = jnp.concatenate([one_hot(mine == line) for line in lines], axis=1)
            out_ref[m] += lax.dot_general(hits, wide, NT, preferred_element_type=F32)
            return 0

        lax.fori_loop(0, rounds, accumulate, 0)


def cost(us):
    return pl.CostEstimate(flops=int(us * 6e8), bytes_accessed=int(us * 3e6), transcendentals=0)


def sums(at, base, many, gathered, rows, old):
    counts = tuple(g[0].shape[0] for g in gathered)
    total = sum(counts)
    return pl.pallas_call(
        lambda *refs: sums_kernel(*refs, counts=counts, base=base, many=many, fresh=not old),
        in_specs=[SMEM] * (1 + len(counts)) + [VMEM] * (2 * len(counts) + 1 + len(old)),
        scratch_shapes=[pltpu.VMEM((4 * total, E, LANES), BF16), pltpu.VMEM((4 * total, LANES), I32)],
        out_shape=jax.ShapeDtypeStruct((many, HALF, E), F32),
        cost_estimate=cost(2 * many),
        compiler_params=PARAMS,
    )(at, *[g[2] for g in gathered], *[g[0] for g in gathered], *[g[1] for g in gathered], rows, *old)


def listed_kernel(list_ref, rows_ref, accum_ref, table_ref, out_ref):
    rows = rows_ref[...]
    hi = jnp.where((rows >> 7) == iota((TOUCH, LANES), 1), 1.0, 0.0)
    padded = jnp.concatenate([accum_ref[...], jnp.zeros((LANES - 32, LANES), F32)], axis=0)
    line = jnp.dot(hi, padded, precision=lax.Precision.HIGHEST, preferred_element_type=F32)
    mine = jnp.where((rows & (LANES - 1)) == iota((TOUCH, LANES), 1), line, 0.0)
    out_ref[0:TOUCH, E:] = jnp.broadcast_to(jnp.sum(mine, axis=1, keepdims=True), (TOUCH, LANES))
    out_ref[TOUCH:, E:] = accum_ref[...]
    out_ref[TOUCH:, 0:E] = jnp.zeros((32, E), F32)

    def step(i, _):
        for j in range(16):
            row = list_ref[i >> 3, (i & 7) * 16 + j]
            out_ref[pl.ds(i * 16 + j, 1), 0:E] = table_ref[pl.ds(row, 1), :]
        return 0

    lax.fori_loop(0, TOUCH // 16, step, 0)


def listed_values(order, rows, accum, table):
    return pl.pallas_call(
        listed_kernel,
        out_shape=jax.ShapeDtypeStruct((TOUCH + 32, E + LANES), F32),
        in_specs=[SMEM, VMEM, VMEM, VMEM],
        cost_estimate=cost(6),
        compiler_params=PARAMS,
        name="listed_values",
    )(order, rows, accum, table)


def update_kernel(*refs):
    plan_ref, list_ref, table_ref, listed_hbm, rows_ref = refs[0:5]
    chunks = refs[5:13]
    table_out, accum_out, new_ref, listed_ref, u_ref, lhs_ref, rhs_ref, load_sem, store_sem = refs[13:]
    tiles = ROWS_DEV // TILE
    listed_load = pltpu.make_async_copy(listed_hbm, listed_ref, load_sem.at[tiles])
    listed_load.start()

    def load(b):
        at = pl.ds(b * TILE if isinstance(b, int) else pl.multiple_of(b * TILE, TILE), TILE)
        return pltpu.make_async_copy(table_ref.at[at], new_ref.at[at], load_sem.at[b])

    for b in range(tiles):
        load(b).start()
    lane = iota((QUART, LANES), 1)
    means = []
    for n in range(8):
        at = slice(n * QUART, (n + 1) * QUART)
        g = chunks[n][...]
        means.append(jnp.sum(g * g, axis=1, keepdims=True) * (1.0 / E))
        rows = rows_ref[at, :]
        lhs_ref[at, :] = jnp.where((rows >> 7) == lane, means[n], 0.0)
        rhs_ref[at, :] = jnp.where((rows & (LANES - 1)) == lane, 1.0, 0.0)
    listed_load.wait()
    for n in range(8):
        at = slice(n * QUART, (n + 1) * QUART)
        now = listed_ref[at, E:E + 1] + means[n]
        u_ref[pl.ds(pl.multiple_of(plan_ref[16 + n] * QUART, QUART), QUART), :] = (
            listed_ref[at, 0:E] - 0.5 * chunks[n][...] / (jnp.sqrt(now) + 1e-08))

    def put(n):
        new_ref[pl.ds(list_ref[n], 1), :] = u_ref[pl.ds(n, 1), :]

    def store(b):
        at = pl.ds(b * TILE if isinstance(b, int) else pl.multiple_of(b * TILE, TILE), TILE)
        return pltpu.make_async_copy(new_ref.at[at], table_out.at[at], store_sem.at[b])

    def tile(b, _):
        first, last = plan_ref[b], plan_ref[b + 1]
        whole = (last - first) >> 3

        def step(i, _):
            for j in range(8):
                put(first + i * 8 + j)
            return 0

        load(b).wait()
        lax.fori_loop(0, whole, step, 0)
        lax.fori_loop(first + whole * 8, last, lambda n, _: (put(n), 0)[1], 0)
        store(b).start()
        return 0

    lax.fori_loop(0, ROWS_DEV // TILE, tile, 0)
    added = lax.dot_general(lhs_ref[...], rhs_ref[...], TN, precision=lax.Precision.HIGHEST,
                            preferred_element_type=F32)
    accum_out[...] = listed_ref[TOUCH:, E:] + added[0:32, :]
    for b in range(ROWS_DEV // TILE):
        store(b).wait()


def update(plan, natural, table, listed, rows, chunks):
    return pl.pallas_call(
        update_kernel,
        out_shape=(jax.ShapeDtypeStruct((ROWS_DEV, E), F32), jax.ShapeDtypeStruct((32, LANES), F32)),
        in_specs=[SMEM, SMEM, HBM, HBM] + [VMEM] * 9,
        out_specs=(HBM, VMEM),
        scratch_shapes=[pltpu.VMEM((ROWS_DEV, E), F32), pltpu.VMEM((TOUCH + 32, E + LANES), F32),
                        pltpu.VMEM((TOUCH, E), F32),
                        pltpu.VMEM((TOUCH, LANES), F32), pltpu.VMEM((TOUCH, LANES), F32),
                        pltpu.SemaphoreType.DMA((ROWS_DEV // TILE + 1,)),
                        pltpu.SemaphoreType.DMA((ROWS_DEV // TILE,))],
        compiler_params=PARAMS,
        name="update",
    )(plan, natural, in_hbm(table), in_hbm(listed), rows, *chunks)


def z_pairs(k):
    return [(z * NX + x, ((z + k) % NZ) * NX + x) for z in range(NZ) for x in range(NX)]


def x_pairs(k):
    return [(z * NX + x, z * NX + (x + k) % NX) for z in range(NZ) for x in range(NX)]


def y_pairs(k):
    return [(y * NC + c, ((y + k) % NY) * NC + c) for y in range(NY) for c in range(NC)]


C_PAIRS = [(y * NC + c, y * NC + 1 - c) for y in range(NY) for c in range(NC)]


def body(table, accum, pooled_grad, row_ids, bag_ids, touched):
    grp = lax.axis_index("grp")
    me = lax.axis_index("shard")
    y, c = grp // NC, grp % NC
    z, x = me // NX, me % NX

    def ordered(listed):
        halves = listed.reshape(NC, NY, QUART)
        halves = jnp.where(c == 0, halves[::-1], halves)
        doubled = jnp.concatenate([halves, halves], axis=1)
        return lax.dynamic_slice(doubled, (0, y, 0), (NC, NY, QUART)).reshape(TOUCH)

    own_list = touched.reshape(TOUCH)
    lists = {0: ordered(own_list)}
    for k in range(1, NX):
        lists[k] = ordered(lax.ppermute(own_list, "shard", x_pairs(-k)))
    stacked = jnp.stack([lists[k][HALF:] for k in ORDER])[:, :, None]
    rows = jnp.broadcast_to(stacked, (NX, HALF, LANES))
    all_rows = jnp.broadcast_to(lists[0][:, None], (TOUCH, LANES))
    order = lists[0].reshape(8, LANES)
    bounds = jnp.sum((own_list[None, :] < TILE * jnp.arange(16, dtype=I32)[:, None]).astype(I32), axis=1)
    turn = (y + jnp.arange(NY, dtype=I32)) % NY
    plan = jnp.concatenate([bounds, (1 - c) * NY + turn, c * NY + turn])

    packet = pack(row_ids.reshape(32, LANES), bag_ids.reshape(32, LANES),
                  pooled_grad.reshape(B_DEV, E))

    def swap(packets):
        return [lax.ppermute(p, "grp", C_PAIRS) for p in packets]

    def gather_of(packets, split):
        return gather(z.reshape(1), packets, split)

    up = down = packet
    other = swap([packet])
    gathered = [gather_of([packet], 0)]
    for _ in range(1, 4):
        up = lax.ppermute(up, "shard", z_pairs(1))
        down = lax.ppermute(down, "shard", z_pairs(-1))
        gathered.append(gather_of([up, down] + other, 0))
        other = swap([up, down])
    up = lax.ppermute(up, "shard", z_pairs(1))
    gathered.append(gather_of(other, 0))
    at = jnp.concatenate([(x + jnp.array(ORDER, I32)) % NX, (NX * z).reshape(1)])
    most = sums(at, 0, 1, gathered, rows, [])
    gathered.append(gather_of([up], 0))
    gathered.append(gather_of(swap([up]), 0))

    listed = listed_values(order, all_rows, accum.reshape(32, LANES), table)
    both = {}
    for base, ks in ((0, (2,)), (1, (1, 3)), (3, (0,))):
        found = sums(at, base, len(ks), gathered[5:] if base == 0 else gathered, rows,
                     [most] if base == 0 else [])
        for n, k in enumerate(ks):
            both[k] = found[n]
            if k:
                both[k] = lax.ppermute(both[k], "shard", x_pairs(k))
    total = both[0] + both[2] + both[1] + both[3]
    part = total[0:QUART]
    for j in (2, 1, 3):
        part = part + lax.ppermute(total[j * QUART:(j + 1) * QUART], "grp", y_pairs(j))
    mine = [part] + [lax.ppermute(part, "grp", y_pairs(-j)) for j in range(1, NY)]
    other = [lax.ppermute(m, "grp", C_PAIRS) for m in mine]
    new_table, new_accum = update(plan, own_list, table, listed, all_rows, other + mine)
    return (new_table, new_accum.reshape(ROWS_DEV))


def solution(mesh):
    return jax.shard_map(
        body,
        mesh=mesh,
        in_specs=(
            P("shard", None),
            P("shard"),
            P("grp", "shard", None, None),
            P("grp", "shard", None),
            P("grp", "shard", None),
            P("shard", None),
        ),
        out_specs=(P("shard", None), P("shard")),
        check_vma=False,
    )
```

```python
import jax
import jax.numpy as jnp
from jax import lax
from jax.experimental import pallas as pl
from jax.experimental.pallas import tpu as pltpu
from jax.sharding import PartitionSpec as P


E = 256
ROWS_DEV = 4096
TOUCH = 1024
HALF = TOUCH // 2
QUART = TOUCH // 8
TILE = 512
LOOK = 4096
B_DEV = 512
LANES = 128
BLOCKS = 64
WIDTH = B_DEV + LANES
NZ, NX, NY, NC = 8, 4, 4, 2
F32 = jnp.float32
BF16 = jnp.bfloat16
I32 = jnp.int32
NT = (((1,), (1,)), ((), ()))
TN = (((0,), (0,)), ((), ()))
ORDER = (2, 1, 3, 0)
SMEM = pl.BlockSpec(memory_space=pltpu.SMEM)
VMEM = pl.BlockSpec(memory_space=pltpu.VMEM)
HBM = pl.BlockSpec(memory_space=pltpu.HBM)
PARAMS = pltpu.CompilerParams(vmem_limit_bytes=14 << 20)


def iota(shape, dim):
    return lax.broadcasted_iota(I32, shape, dim)


def one_hot(mask):
    return jnp.where(mask, 1.0, 0.0).astype(BF16)


def in_hbm(array):
    return pltpu.with_memory_space_constraint(array, pltpu.HBM)


def pack_kernel(ids_hbm, bags_hbm, g_hbm, out_ref, a_ref, b_ref, o_ref, ids_ref, bags_ref, g_ref, sem):
    loads = [pltpu.make_async_copy(src, dst, sem.at[n])
             for n, (src, dst) in enumerate(((ids_hbm, ids_ref), (bags_hbm, bags_ref), (g_hbm, g_ref)))]
    for load in loads:
        load.start()
    for load in loads:
        load.wait()
    groups = LOOK // LANES
    ids = ids_ref[...]
    owner = ids >> 12
    owners = iota((32, LANES), 0)
    running = jnp.zeros((32, LANES), F32)
    for i in range(groups):
        hit = jnp.where(owner[i:i + 1, :] == owners, 1.0, 0.0)
        o_ref[i * 32:(i + 1) * 32, 0:LANES] = hit.astype(BF16)
        o_ref[i * 32:(i + 1) * 32, LANES:2 * LANES] = running.astype(BF16)
        running = running + hit
    before = one_hot(iota((LANES, LANES), 0) < iota((LANES, LANES), 1))
    weights = jnp.concatenate([before, jnp.ones((LANES, LANES), BF16)], axis=0)
    prefix = jnp.dot(o_ref[...], weights, preferred_element_type=F32)
    totals = jnp.concatenate([running, jnp.zeros((LANES - 32, LANES), F32)], axis=0)
    count_row = lax.dot_general(jnp.ones((8, LANES), BF16), totals.astype(BF16), NT,
                                preferred_element_type=F32).astype(I32)
    blocks_row = (count_row + (LANES - 1)) >> 7
    start_row = jnp.dot(blocks_row.astype(F32).astype(BF16), before, preferred_element_type=F32)
    start_col = jnp.sum(
        jnp.where(iota((32, LANES), 1) < iota((32, LANES), 0),
                  jnp.broadcast_to(blocks_row[0:1, :].astype(F32), (32, LANES)), 0.0),
        axis=1, keepdims=True) * float(LANES)
    start_all = jnp.broadcast_to(start_col, (32, LANES))
    for i in range(groups):
        hit = owner[i:i + 1, :] == owners
        pos = jnp.sum(jnp.where(hit, prefix[i * 32:(i + 1) * 32, :] + start_all, 0.0),
                      axis=0, keepdims=True).astype(I32)
        key = (((ids[i:i + 1, :] & (ROWS_DEV - 1)) << 9) | bags_ref[i:i + 1, :]) + 1
        at_hi = (pos >> 7) == iota((BLOCKS, LANES), 0)
        for piece in range(3):
            part = ((key >> (8 * piece)) & 255).astype(F32)
            a_ref[piece * BLOCKS:(piece + 1) * BLOCKS, i * LANES:(i + 1) * LANES] = jnp.where(
                at_hi, part, 0.0).astype(BF16)
        b_ref[:, i * LANES:(i + 1) * LANES] = one_hot((pos & (LANES - 1)) == iota((LANES, LANES), 0))
    placed = lax.dot_general(a_ref[...], b_ref[...], NT, preferred_element_type=F32)
    out_ref[0:3 * BLOCKS, B_DEV:WIDTH] = placed.astype(BF16)
    meta = jnp.where(iota((16, LANES), 0) < 8,
                     jnp.concatenate([start_row, start_row], axis=0),
                     jnp.concatenate([blocks_row, blocks_row], axis=0).astype(F32))
    out_ref[3 * BLOCKS:3 * BLOCKS + 16, B_DEV:WIDTH] = meta.astype(BF16)
    out_ref[3 * BLOCKS + 16:E, B_DEV:WIDTH] = jnp.zeros((E - 3 * BLOCKS - 16, LANES), BF16)
    eye = one_hot(iota((E, E), 0) == iota((E, E), 1))
    out_ref[:, 0:B_DEV] = lax.dot_general(eye, g_ref[...], NT, preferred_element_type=F32).astype(BF16)


def pack(ids, bags, grads):
    return pl.pallas_call(
        pack_kernel,
        out_shape=jax.ShapeDtypeStruct((E, WIDTH), BF16),
        in_specs=[HBM] * 3,
        scratch_shapes=[pltpu.VMEM((3 * BLOCKS, LOOK), BF16),
                        pltpu.VMEM((LANES, LOOK), BF16),
                        pltpu.VMEM((TOUCH, 2 * LANES), BF16),
                        pltpu.VMEM((32, LANES), I32), pltpu.VMEM((32, LANES), I32),
                        pltpu.VMEM((B_DEV, E), BF16), pltpu.SemaphoreType.DMA((3,))],
        cost_estimate=cost(4),
        compiler_params=PARAMS,
        name="pack",
    )(*[in_hbm(a) for a in (ids, bags, grads)])


def gather_kernel(z_ref, *refs, counts):
    groups, total = len(counts), sum(counts)
    packets = [refs[n].at[i] for n in range(groups) for i in range(counts[n])]
    x_ref, k_ref, m_ref, all_ref, scalar_ref, sem = refs[groups:]
    copies = []
    for d in range(total):
        side = packets[d][3 * BLOCKS:3 * BLOCKS + 16, B_DEV:WIDTH].astype(F32).astype(I32)
        m_ref[d] = jnp.where(iota((8, LANES), 0) == 0, side[0:8], side[8:16])
        copies.append(pltpu.make_async_copy(m_ref.at[d], scalar_ref.at[d], sem.at[d]))
        copies[d].start()
    for d in range(total):
        pieces = packets[d][0:3 * BLOCKS, B_DEV:WIDTH].astype(F32).astype(I32)
        all_ref[d, 0:BLOCKS] = (pieces[0:BLOCKS] + (pieces[BLOCKS:2 * BLOCKS] << 8)
                                + (pieces[2 * BLOCKS:3 * BLOCKS] << 16)) - 1
        all_ref[d, BLOCKS:BLOCKS + 16] = jnp.zeros((16, LANES), I32)
    for copy in copies:
        copy.wait()
    for d in range(total):
        first = scalar_ref[d, 0, NX * z_ref[0]]
        last = scalar_ref[d, 0, NX * z_ref[0] + NX - 1] + scalar_ref[d, 1, NX * z_ref[0] + NX - 1]
        k_ref[d] = all_ref[d, pl.ds(first, 16), :] >> 9

        def pair(j, _, d=d, first=first):
            lines = [all_ref[d, pl.ds(first + 2 * j + i, 1), :] & (B_DEV - 1) for i in range(2)]
            picks = jnp.concatenate([one_hot(line == iota((B_DEV, LANES), 0)) for line in lines], axis=1)
            got = jnp.dot(packets[d][:, 0:B_DEV], picks, preferred_element_type=F32).astype(BF16)
            for i in range(2):
                x_ref[d, 2 * j + i] = got[:, i * LANES:(i + 1) * LANES]
            return 0

        lax.fori_loop(0, (last - first + 1) >> 1, pair, 0)


def gather(z, packets):
    counts = tuple(p.shape[0] for p in packets)
    count = sum(counts)
    return pl.pallas_call(
        lambda *refs: gather_kernel(*refs, counts=counts),
        out_shape=(jax.ShapeDtypeStruct((count, 16, E, LANES), BF16),
                   jax.ShapeDtypeStruct((count, 16, LANES), I32),
                   jax.ShapeDtypeStruct((count, 8, LANES), I32)),
        in_specs=[SMEM] + [VMEM] * len(packets),
        scratch_shapes=[pltpu.VMEM((count, BLOCKS + 16, LANES), I32), pltpu.SMEM((count, 8, LANES), I32),
                        pltpu.SemaphoreType.DMA((count,))],
        cost_estimate=cost(2 + count),
        compiler_params=PARAMS,
    )(z, *packets)


def sums_kernel(at_ref, *refs, counts, base, many, fresh):
    groups = len(counts)
    metas, xs, keys = refs[0:groups], refs[groups:2 * groups], refs[2 * groups:3 * groups]
    rows_ref = refs[3 * groups]
    out_ref, all_ref, k_ref = refs[-3:]
    for m in range(many):
        column = at_ref[base + m]
        filled = jnp.int32(0)
        for n in range(groups):
            for d in range(counts[n]):
                found = metas[n][d, 1, at_ref[4] + column]
                first = metas[n][d, 0, at_ref[4] + column] - metas[n][d, 0, at_ref[4]]

                def move(j, _, n=n, d=d, filled=filled, first=first):
                    all_ref[filled + j] = xs[n][d, first + j]
                    k_ref[pl.ds(filled + j, 1), :] = keys[n][d, pl.ds(first + j, 1), :]
                    return 0

                lax.fori_loop(0, found, move, 0)
                filled = filled + found
        rounds = (filled + 7) >> 3

        def blank(j, _):
            all_ref[j] = jnp.zeros((E, LANES), BF16)
            k_ref[pl.ds(j, 1), :] = jnp.full((1, LANES), -1, I32)
            return 0

        lax.fori_loop(filled, rounds * 8, blank, 0)
        out_ref[m] = jnp.zeros((HALF, E), F32) if fresh else refs[3 * groups + 1][m]

        def accumulate(r, _, m=m):
            wide = jnp.concatenate([all_ref[8 * r + j] for j in range(8)], axis=1)
            lines = [k_ref[pl.ds(8 * r + j, 1), :] for j in range(8)]
            mine = rows_ref[base + m]
            hits = jnp.concatenate([one_hot(mine == line) for line in lines], axis=1)
            out_ref[m] += lax.dot_general(hits, wide, NT, preferred_element_type=F32)
            return 0

        lax.fori_loop(0, rounds, accumulate, 0)


def cost(us):
    return pl.CostEstimate(flops=int(us * 6e8), bytes_accessed=int(us * 3e6), transcendentals=0)


def sums(at, base, many, gathered, rows, old):
    counts = tuple(g[0].shape[0] for g in gathered)
    total = sum(counts)
    return pl.pallas_call(
        lambda *refs: sums_kernel(*refs, counts=counts, base=base, many=many, fresh=not old),
        in_specs=[SMEM] * (1 + len(counts)) + [VMEM] * (2 * len(counts) + 1 + len(old)),
        scratch_shapes=[pltpu.VMEM((4 * total, E, LANES), BF16), pltpu.VMEM((4 * total, LANES), I32)],
        out_shape=jax.ShapeDtypeStruct((many, HALF, E), F32),
        cost_estimate=cost(2 * many),
        compiler_params=PARAMS,
    )(at, *[g[2] for g in gathered], *[g[0] for g in gathered], *[g[1] for g in gathered], rows, *old)


def listed_kernel(list_ref, rows_ref, accum_ref, table_ref, out_ref):
    rows = rows_ref[...]
    hi = jnp.where((rows >> 7) == iota((TOUCH, LANES), 1), 1.0, 0.0)
    padded = jnp.concatenate([accum_ref[...], jnp.zeros((LANES - 32, LANES), F32)], axis=0)
    line = jnp.dot(hi, padded, precision=lax.Precision.HIGHEST, preferred_element_type=F32)
    mine = jnp.where((rows & (LANES - 1)) == iota((TOUCH, LANES), 1), line, 0.0)
    out_ref[0:TOUCH, E:] = jnp.broadcast_to(jnp.sum(mine, axis=1, keepdims=True), (TOUCH, LANES))
    out_ref[TOUCH:, E:] = accum_ref[...]
    out_ref[TOUCH:, 0:E] = jnp.zeros((32, E), F32)

    def step(i, _):
        for j in range(16):
            row = list_ref[i >> 3, (i & 7) * 16 + j]
            out_ref[pl.ds(i * 16 + j, 1), 0:E] = table_ref[pl.ds(row, 1), :]
        return 0

    lax.fori_loop(0, TOUCH // 16, step, 0)


def listed_values(order, rows, accum, table):
    return pl.pallas_call(
        listed_kernel,
        out_shape=jax.ShapeDtypeStruct((TOUCH + 32, E + LANES), F32),
        in_specs=[SMEM, VMEM, VMEM, VMEM],
        cost_estimate=cost(6),
        compiler_params=PARAMS,
        name="listed_values",
    )(order, rows, accum, table)


def update_kernel(*refs):
    plan_ref, list_ref, table_ref, listed_hbm, rows_ref = refs[0:5]
    chunks = [refs[5]] + [refs[6].at[n * QUART:(n + 1) * QUART] for n in range(NY - 1)] + list(refs[7:11])
    table_out, accum_out, new_ref, listed_ref, u_ref, lhs_ref, rhs_ref, load_sem, store_sem = refs[11:]
    tiles = ROWS_DEV // TILE
    listed_load = pltpu.make_async_copy(listed_hbm, listed_ref, load_sem.at[tiles])
    listed_load.start()

    def load(b):
        at = pl.ds(b * TILE if isinstance(b, int) else pl.multiple_of(b * TILE, TILE), TILE)
        return pltpu.make_async_copy(table_ref.at[at], new_ref.at[at], load_sem.at[b])

    for b in range(tiles):
        load(b).start()
    lane = iota((QUART, LANES), 1)
    means = []
    for n in range(8):
        at = slice(n * QUART, (n + 1) * QUART)
        g = chunks[n][...]
        means.append(jnp.sum(g * g, axis=1, keepdims=True) * (1.0 / E))
        rows = rows_ref[at, :]
        lhs_ref[at, :] = jnp.where((rows >> 7) == lane, means[n], 0.0)
        rhs_ref[at, :] = jnp.where((rows & (LANES - 1)) == lane, 1.0, 0.0)
    listed_load.wait()
    for n in range(8):
        at = slice(n * QUART, (n + 1) * QUART)
        now = listed_ref[at, E:E + 1] + means[n]
        u_ref[pl.ds(pl.multiple_of(plan_ref[16 + n] * QUART, QUART), QUART), :] = (
            listed_ref[at, 0:E] - 0.5 * chunks[n][...] / (jnp.sqrt(now) + 1e-08))

    def put(n):
        new_ref[pl.ds(list_ref[n], 1), :] = u_ref[pl.ds(n, 1), :]

    def store(b):
        at = pl.ds(b * TILE if isinstance(b, int) else pl.multiple_of(b * TILE, TILE), TILE)
        return pltpu.make_async_copy(new_ref.at[at], table_out.at[at], store_sem.at[b])

    def tile(b, _):
        first, last = plan_ref[b], plan_ref[b + 1]
        whole = (last - first) >> 3

        def step(i, _):
            for j in range(8):
                put(first + i * 8 + j)
            return 0

        load(b).wait()
        lax.fori_loop(0, whole, step, 0)
        lax.fori_loop(first + whole * 8, last, lambda n, _: (put(n), 0)[1], 0)
        store(b).start()
        return 0

    lax.fori_loop(0, ROWS_DEV // TILE, tile, 0)
    added = lax.dot_general(lhs_ref[...], rhs_ref[...], TN, precision=lax.Precision.HIGHEST,
                            preferred_element_type=F32)
    accum_out[...] = listed_ref[TOUCH:, E:] + added[0:32, :]
    for b in range(ROWS_DEV // TILE):
        store(b).wait()


def update(plan, natural, table, listed, rows, chunks):
    return pl.pallas_call(
        update_kernel,
        out_shape=(jax.ShapeDtypeStruct((ROWS_DEV, E), F32), jax.ShapeDtypeStruct((32, LANES), F32)),
        in_specs=[SMEM, SMEM, HBM, HBM] + [VMEM] * 7,
        out_specs=(HBM, VMEM),
        scratch_shapes=[pltpu.VMEM((ROWS_DEV, E), F32), pltpu.VMEM((TOUCH + 32, E + LANES), F32),
                        pltpu.VMEM((TOUCH, E), F32),
                        pltpu.VMEM((TOUCH, LANES), F32), pltpu.VMEM((TOUCH, LANES), F32),
                        pltpu.SemaphoreType.DMA((ROWS_DEV // TILE + 1,)),
                        pltpu.SemaphoreType.DMA((ROWS_DEV // TILE,))],
        compiler_params=PARAMS,
        name="update",
    )(plan, natural, in_hbm(table), in_hbm(listed), rows, *chunks)


def x_pairs(k):
    return [(z * NX + x, z * NX + (x + k) % NX) for z in range(NZ) for x in range(NX)]


def y_pairs(k):
    return [(y * NC + c, ((y + k) % NY) * NC + c) for y in range(NY) for c in range(NC)]


HOPS = [((y * NC + c) * NZ * NX + z * NX + x,
         (y * NC + c) * NZ * NX + (z + 1 - 2 * c) % NZ * NX + x)
        for y in range(NY) for c in range(NC) for z in range(NZ) for x in range(NX)]
C_PAIRS = [(y * NC + c, y * NC + 1 - c) for y in range(NY) for c in range(NC)]


def body(table, accum, pooled_grad, row_ids, bag_ids, touched):
    grp = lax.axis_index("grp")
    me = lax.axis_index("shard")
    y, c = grp // NC, grp % NC
    z, x = me // NX, me % NX

    def ordered(listed):
        halves = listed.reshape(NC, NY, QUART)
        halves = jnp.where(c == 0, halves[::-1], halves)
        doubled = jnp.concatenate([halves, halves], axis=1)
        return lax.dynamic_slice(doubled, (0, y, 0), (NC, NY, QUART)).reshape(TOUCH)

    own_list = touched.reshape(TOUCH)
    lists = {0: ordered(own_list)}
    for k in range(1, NX):
        lists[k] = ordered(lax.ppermute(own_list, "shard", x_pairs(-k)))
    stacked = jnp.stack([lists[k][HALF:] for k in ORDER])[:, :, None]
    rows = jnp.broadcast_to(stacked, (NX, HALF, LANES))
    all_rows = jnp.broadcast_to(lists[0][:, None], (TOUCH, LANES))
    order = lists[0].reshape(8, LANES)
    bounds = jnp.sum((own_list[None, :] < TILE * jnp.arange(16, dtype=I32)[:, None]).astype(I32), axis=1)
    turn = (y + jnp.arange(NY, dtype=I32)) % NY
    plan = jnp.concatenate([bounds, (1 - c) * NY + turn, c * NY + turn])

    packet = pack(row_ids.reshape(32, LANES), bag_ids.reshape(32, LANES),
                  pooled_grad.reshape(B_DEV, E))

    def swap(array):
        return lax.ppermute(array, "grp", C_PAIRS)

    def hop(array):
        return lax.ppermute(array, ("grp", "shard"), HOPS)

    def gather_of(packets):
        return gather(z.reshape(1), packets)

    at = jnp.concatenate([(x + jnp.array(ORDER, I32)) % NX, (NX * z).reshape(1)])
    pool = jnp.stack([packet, swap(packet)])
    one = hop(pool)
    gathered = [gather_of([pool])]
    two = hop(one)
    one_other = swap(one)
    gathered.append(gather_of([one]))
    three = hop(two)
    two_other = swap(two)
    gathered.append(gather_of([two, one_other]))
    four = hop(three[0:1])
    three_other = swap(three)
    gathered.append(gather_of([three, two_other]))
    gathered.append(gather_of([three_other]))
    most = sums(at, 0, 1, gathered, rows, [])
    four_other = swap(four)
    gathered.append(gather_of([four]))
    gathered.append(gather_of([four_other]))

    listed = listed_values(order, all_rows, accum.reshape(32, LANES), table)
    both = {}
    for base, ks in ((0, (2,)), (1, (1, 3)), (3, (0,))):
        found = sums(at, base, len(ks), gathered[5:] if base == 0 else gathered, rows,
                     [most] if base == 0 else [])
        for n, k in enumerate(ks):
            both[k] = found[n]
            if k:
                both[k] = lax.ppermute(both[k], "shard", x_pairs(k))
    total = both[0] + both[2] + both[1] + both[3]
    part = total[0:QUART]
    for j in (2, 1, 3):
        part = part + lax.ppermute(total[j * QUART:(j + 1) * QUART], "grp", y_pairs(j))
    mine = [part] + [lax.ppermute(part, "grp", y_pairs(-j)) for j in range(1, NY)]
    other = [swap(part), swap(jnp.concatenate(mine[1:], axis=0))]
    new_table, new_accum = update(plan, own_list, table, listed, all_rows, other + mine)
    return (new_table, new_accum.reshape(ROWS_DEV))


def solution(mesh):
    return jax.shard_map(
        body,
        mesh=mesh,
        in_specs=(
            P("shard", None),
            P("shard"),
            P("grp", "shard", None, None),
            P("grp", "shard", None),
            P("grp", "shard", None),
            P("shard", None),
        ),
        out_specs=(P("shard", None), P("shard")),
        check_vma=False,
    )
```

```python
import jax
import jax.numpy as jnp
from jax import lax
from jax.experimental import pallas as pl
from jax.experimental.pallas import tpu as pltpu
from jax.sharding import PartitionSpec as P


E = 256
ROWS_DEV = 4096
TOUCH = 1024
HALF = TOUCH // 2
QUART = TOUCH // 8
TILE = 512
LOOK = 4096
B_DEV = 512
LANES = 128
BLOCKS = 64
WIDTH = B_DEV + LANES
NZ, NX, NY, NC = 8, 4, 4, 2
F32 = jnp.float32
BF16 = jnp.bfloat16
I32 = jnp.int32
NT = (((1,), (1,)), ((), ()))
TN = (((0,), (0,)), ((), ()))
ORDER = (2, 1, 3, 0)
SMEM = pl.BlockSpec(memory_space=pltpu.SMEM)
VMEM = pl.BlockSpec(memory_space=pltpu.VMEM)
HBM = pl.BlockSpec(memory_space=pltpu.HBM)
PARAMS = pltpu.CompilerParams(vmem_limit_bytes=14 << 20)


def iota(shape, dim):
    return lax.broadcasted_iota(I32, shape, dim)


def one_hot(mask):
    return jnp.where(mask, 1.0, 0.0).astype(BF16)


def in_hbm(array):
    return pltpu.with_memory_space_constraint(array, pltpu.HBM)


def pack_kernel(ids_hbm, bags_hbm, g_hbm, out_ref, a_ref, b_ref, o_ref, ids_ref, bags_ref, g_ref, sem):
    loads = [pltpu.make_async_copy(src, dst, sem.at[n])
             for n, (src, dst) in enumerate(((ids_hbm, ids_ref), (bags_hbm, bags_ref), (g_hbm, g_ref)))]
    for load in loads:
        load.start()
    for load in loads:
        load.wait()
    groups = LOOK // LANES
    ids = ids_ref[...]
    owner = ids >> 12
    owners = iota((32, LANES), 0)
    running = jnp.zeros((32, LANES), F32)
    for i in range(groups):
        hit = jnp.where(owner[i:i + 1, :] == owners, 1.0, 0.0)
        o_ref[i * 32:(i + 1) * 32, 0:LANES] = hit.astype(BF16)
        o_ref[i * 32:(i + 1) * 32, LANES:2 * LANES] = running.astype(BF16)
        running = running + hit
    before = one_hot(iota((LANES, LANES), 0) < iota((LANES, LANES), 1))
    weights = jnp.concatenate([before, jnp.ones((LANES, LANES), BF16)], axis=0)
    prefix = jnp.dot(o_ref[...], weights, preferred_element_type=F32)
    totals = jnp.concatenate([running, jnp.zeros((LANES - 32, LANES), F32)], axis=0)
    count_row = lax.dot_general(jnp.ones((8, LANES), BF16), totals.astype(BF16), NT,
                                preferred_element_type=F32).astype(I32)
    blocks_row = (count_row + (LANES - 1)) >> 7
    start_row = jnp.dot(blocks_row.astype(F32).astype(BF16), before, preferred_element_type=F32)
    start_col = jnp.sum(
        jnp.where(iota((32, LANES), 1) < iota((32, LANES), 0),
                  jnp.broadcast_to(blocks_row[0:1, :].astype(F32), (32, LANES)), 0.0),
        axis=1, keepdims=True) * float(LANES)
    start_all = jnp.broadcast_to(start_col, (32, LANES))
    for i in range(groups):
        hit = owner[i:i + 1, :] == owners
        pos = jnp.sum(jnp.where(hit, prefix[i * 32:(i + 1) * 32, :] + start_all, 0.0),
                      axis=0, keepdims=True).astype(I32)
        key = (((ids[i:i + 1, :] & (ROWS_DEV - 1)) << 9) | bags_ref[i:i + 1, :]) + 1
        at_hi = (pos >> 7) == iota((BLOCKS, LANES), 0)
        for piece in range(3):
            part = ((key >> (8 * piece)) & 255).astype(F32)
            a_ref[piece * BLOCKS:(piece + 1) * BLOCKS, i * LANES:(i + 1) * LANES] = jnp.where(
                at_hi, part, 0.0).astype(BF16)
        b_ref[:, i * LANES:(i + 1) * LANES] = one_hot((pos & (LANES - 1)) == iota((LANES, LANES), 0))
    placed = lax.dot_general(a_ref[...], b_ref[...], NT, preferred_element_type=F32)
    out_ref[0:3 * BLOCKS, B_DEV:WIDTH] = placed.astype(BF16)
    meta = jnp.where(iota((16, LANES), 0) < 8,
                     jnp.concatenate([start_row, start_row], axis=0),
                     jnp.concatenate([blocks_row, blocks_row], axis=0).astype(F32))
    out_ref[3 * BLOCKS:3 * BLOCKS + 16, B_DEV:WIDTH] = meta.astype(BF16)
    out_ref[3 * BLOCKS + 16:E, B_DEV:WIDTH] = jnp.zeros((E - 3 * BLOCKS - 16, LANES), BF16)
    eye = one_hot(iota((E, E), 0) == iota((E, E), 1))
    out_ref[:, 0:B_DEV] = lax.dot_general(eye, g_ref[...], NT, preferred_element_type=F32).astype(BF16)


def pack(ids, bags, grads):
    return pl.pallas_call(
        pack_kernel,
        out_shape=jax.ShapeDtypeStruct((E, WIDTH), BF16),
        in_specs=[HBM] * 3,
        scratch_shapes=[pltpu.VMEM((3 * BLOCKS, LOOK), BF16),
                        pltpu.VMEM((LANES, LOOK), BF16),
                        pltpu.VMEM((TOUCH, 2 * LANES), BF16),
                        pltpu.VMEM((32, LANES), I32), pltpu.VMEM((32, LANES), I32),
                        pltpu.VMEM((B_DEV, E), BF16), pltpu.SemaphoreType.DMA((3,))],
        cost_estimate=cost(4),
        compiler_params=PARAMS,
        name="pack",
    )(*[in_hbm(a) for a in (ids, bags, grads)])


def gather_kernel(z_ref, *refs, count, split):
    packets = refs[0:count + split]
    x_ref, k_ref, m_ref, all_ref, scalar_ref, sem = refs[count + split:]
    copies = []
    for d in range(count):
        cut = 128 if split and d == count - 1 else 0
        tail = packets[-1] if cut else packets[d]
        side = tail[3 * BLOCKS - cut:3 * BLOCKS + 16 - cut, B_DEV:WIDTH].astype(F32).astype(I32)
        m_ref[d] = jnp.where(iota((8, LANES), 0) == 0, side[0:8], side[8:16])
        copies.append(pltpu.make_async_copy(m_ref.at[d], scalar_ref.at[d], sem.at[d]))
        copies[d].start()
    for d in range(count):
        cut = 128 if split and d == count - 1 else 0
        tail = packets[-1] if cut else packets[d]
        low = packets[d][0:2 * BLOCKS, B_DEV:WIDTH].astype(F32).astype(I32)
        top = tail[2 * BLOCKS - cut:3 * BLOCKS - cut, B_DEV:WIDTH].astype(F32).astype(I32)
        all_ref[d, 0:BLOCKS] = (low[0:BLOCKS] + (low[BLOCKS:2 * BLOCKS] << 8) + (top << 16)) - 1
        all_ref[d, BLOCKS:BLOCKS + 16] = jnp.zeros((16, LANES), I32)
    for copy in copies:
        copy.wait()
    for d in range(count):
        parts = packets[d:] if split and d == count - 1 else packets[d:d + 1]
        first = scalar_ref[d, 0, NX * z_ref[0]]
        last = scalar_ref[d, 0, NX * z_ref[0] + NX - 1] + scalar_ref[d, 1, NX * z_ref[0] + NX - 1]
        k_ref[d] = all_ref[d, pl.ds(first, 16), :] >> 9

        def pair(j, _, d=d, first=first, parts=parts):
            lines = [all_ref[d, pl.ds(first + 2 * j + i, 1), :] & (B_DEV - 1) for i in range(2)]
            picks = jnp.concatenate([one_hot(line == iota((B_DEV, LANES), 0)) for line in lines], axis=1)
            rows = E // len(parts)
            for n, part in enumerate(parts):
                got = jnp.dot(part[:, 0:B_DEV], picks, preferred_element_type=F32).astype(BF16)
                for i in range(2):
                    x_ref[d, 2 * j + i, n * rows:(n + 1) * rows] = got[:, i * LANES:(i + 1) * LANES]
            return 0

        lax.fori_loop(0, (last - first + 1) >> 1, pair, 0)


def gather(z, packets, split):
    count = len(packets) - split
    return pl.pallas_call(
        lambda *refs: gather_kernel(*refs, count=count, split=split),
        out_shape=(jax.ShapeDtypeStruct((count, 16, E, LANES), BF16),
                   jax.ShapeDtypeStruct((count, 16, LANES), I32),
                   jax.ShapeDtypeStruct((count, 8, LANES), I32)),
        in_specs=[SMEM] + [VMEM] * len(packets),
        scratch_shapes=[pltpu.VMEM((count, BLOCKS + 16, LANES), I32), pltpu.SMEM((count, 8, LANES), I32),
                        pltpu.SemaphoreType.DMA((count,))],
        cost_estimate=cost(2 + count),
        compiler_params=PARAMS,
    )(z, *packets)


def sums_kernel(at_ref, *refs, counts, base, many, fresh):
    groups = len(counts)
    metas, xs, keys = refs[0:groups], refs[groups:2 * groups], refs[2 * groups:3 * groups]
    rows_ref = refs[3 * groups]
    out_ref, all_ref, k_ref = refs[-3:]
    for m in range(many):
        column = at_ref[base + m]
        filled = jnp.int32(0)
        for n in range(groups):
            for d in range(counts[n]):
                found = metas[n][d, 1, at_ref[4] + column]
                first = metas[n][d, 0, at_ref[4] + column] - metas[n][d, 0, at_ref[4]]

                def move(j, _, n=n, d=d, filled=filled, first=first):
                    all_ref[filled + j] = xs[n][d, first + j]
                    k_ref[pl.ds(filled + j, 1), :] = keys[n][d, pl.ds(first + j, 1), :]
                    return 0

                lax.fori_loop(0, found, move, 0)
                filled = filled + found
        rounds = (filled + 7) >> 3

        def blank(j, _):
            all_ref[j] = jnp.zeros((E, LANES), BF16)
            k_ref[pl.ds(j, 1), :] = jnp.full((1, LANES), -1, I32)
            return 0

        lax.fori_loop(filled, rounds * 8, blank, 0)
        out_ref[m] = jnp.zeros((HALF, E), F32) if fresh else refs[3 * groups + 1][m]

        def accumulate(r, _, m=m):
            wide = jnp.concatenate([all_ref[8 * r + j] for j in range(8)], axis=1)
            lines = [k_ref[pl.ds(8 * r + j, 1), :] for j in range(8)]
            mine = rows_ref[base + m]
            hits = jnp.concatenate([one_hot(mine == line) for line in lines], axis=1)
            out_ref[m] += lax.dot_general(hits, wide, NT, preferred_element_type=F32)
            return 0

        lax.fori_loop(0, rounds, accumulate, 0)


def cost(us):
    return pl.CostEstimate(flops=int(us * 6e8), bytes_accessed=int(us * 3e6), transcendentals=0)


def sums(at, base, many, gathered, rows, old):
    counts = tuple(g[0].shape[0] for g in gathered)
    total = sum(counts)
    return pl.pallas_call(
        lambda *refs: sums_kernel(*refs, counts=counts, base=base, many=many, fresh=not old),
        in_specs=[SMEM] * (1 + len(counts)) + [VMEM] * (2 * len(counts) + 1 + len(old)),
        scratch_shapes=[pltpu.VMEM((4 * total, E, LANES), BF16), pltpu.VMEM((4 * total, LANES), I32)],
        out_shape=jax.ShapeDtypeStruct((many, HALF, E), F32),
        cost_estimate=cost(2 * many),
        compiler_params=PARAMS,
    )(at, *[g[2] for g in gathered], *[g[0] for g in gathered], *[g[1] for g in gathered], rows, *old)


def listed_kernel(list_ref, rows_ref, accum_ref, table_ref, out_ref):
    rows = rows_ref[...]
    hi = jnp.where((rows >> 7) == iota((TOUCH, LANES), 1), 1.0, 0.0)
    padded = jnp.concatenate([accum_ref[...], jnp.zeros((LANES - 32, LANES), F32)], axis=0)
    line = jnp.dot(hi, padded, precision=lax.Precision.HIGHEST, preferred_element_type=F32)
    mine = jnp.where((rows & (LANES - 1)) == iota((TOUCH, LANES), 1), line, 0.0)
    out_ref[0:TOUCH, E:] = jnp.broadcast_to(jnp.sum(mine, axis=1, keepdims=True), (TOUCH, LANES))
    out_ref[TOUCH:, E:] = accum_ref[...]
    out_ref[TOUCH:, 0:E] = jnp.zeros((32, E), F32)

    def step(i, _):
        for j in range(16):
            row = list_ref[i >> 3, (i & 7) * 16 + j]
            out_ref[pl.ds(i * 16 + j, 1), 0:E] = table_ref[pl.ds(row, 1), :]
        return 0

    lax.fori_loop(0, TOUCH // 16, step, 0)


def listed_values(order, rows, accum, table):
    return pl.pallas_call(
        listed_kernel,
        out_shape=jax.ShapeDtypeStruct((TOUCH + 32, E + LANES), F32),
        in_specs=[SMEM, VMEM, VMEM, VMEM],
        cost_estimate=cost(6),
        compiler_params=PARAMS,
        name="listed_values",
    )(order, rows, accum, table)


def update_kernel(*refs):
    plan_ref, list_ref, table_ref, listed_hbm, rows_ref = refs[0:5]
    chunks = refs[5:13]
    table_out, accum_out, new_ref, listed_ref, u_ref, lhs_ref, rhs_ref, load_sem, store_sem = refs[13:]
    tiles = ROWS_DEV // TILE
    listed_load = pltpu.make_async_copy(listed_hbm, listed_ref, load_sem.at[tiles])
    listed_load.start()

    def load(b):
        at = pl.ds(b * TILE if isinstance(b, int) else pl.multiple_of(b * TILE, TILE), TILE)
        return pltpu.make_async_copy(table_ref.at[at], new_ref.at[at], load_sem.at[b])

    for b in range(tiles):
        load(b).start()
    lane = iota((QUART, LANES), 1)
    means = []
    for n in range(8):
        at = slice(n * QUART, (n + 1) * QUART)
        g = chunks[n][...]
        means.append(jnp.sum(g * g, axis=1, keepdims=True) * (1.0 / E))
        rows = rows_ref[at, :]
        lhs_ref[at, :] = jnp.where((rows >> 7) == lane, means[n], 0.0)
        rhs_ref[at, :] = jnp.where((rows & (LANES - 1)) == lane, 1.0, 0.0)
    listed_load.wait()
    for n in range(8):
        at = slice(n * QUART, (n + 1) * QUART)
        now = listed_ref[at, E:E + 1] + means[n]
        u_ref[pl.ds(pl.multiple_of(plan_ref[16 + n] * QUART, QUART), QUART), :] = (
            listed_ref[at, 0:E] - 0.5 * chunks[n][...] / (jnp.sqrt(now) + 1e-08))

    def put(n):
        new_ref[pl.ds(list_ref[n], 1), :] = u_ref[pl.ds(n, 1), :]

    def store(b):
        at = pl.ds(b * TILE if isinstance(b, int) else pl.multiple_of(b * TILE, TILE), TILE)
        return pltpu.make_async_copy(new_ref.at[at], table_out.at[at], store_sem.at[b])

    def tile(b, _):
        first, last = plan_ref[b], plan_ref[b + 1]
        low, high = (first + 7) >> 3, last >> 3

        def step(i, _):
            block = u_ref[pl.ds(pl.multiple_of(i * 8, 8), 8), :]
            for j in range(8):
                new_ref[pl.ds(list_ref[i * 8 + j], 1), :] = block[j:j + 1, :]
            return 0

        load(b).wait()
        lax.fori_loop(first, jnp.minimum(low * 8, last), lambda n, _: (put(n), 0)[1], 0)
        lax.fori_loop(low, high, step, 0)
        lax.fori_loop(jnp.maximum(high, low) * 8, last, lambda n, _: (put(n), 0)[1], 0)
        store(b).start()
        return 0

    lax.fori_loop(0, ROWS_DEV // TILE, tile, 0)
    added = lax.dot_general(lhs_ref[...], rhs_ref[...], TN, precision=lax.Precision.HIGHEST,
                            preferred_element_type=F32)
    accum_out[...] = listed_ref[TOUCH:, E:] + added[0:32, :]
    for b in range(ROWS_DEV // TILE):
        store(b).wait()


def update(plan, natural, table, listed, rows, chunks):
    return pl.pallas_call(
        update_kernel,
        out_shape=(jax.ShapeDtypeStruct((ROWS_DEV, E), F32), jax.ShapeDtypeStruct((32, LANES), F32)),
        in_specs=[SMEM, SMEM, HBM, HBM] + [VMEM] * 9,
        out_specs=(HBM, VMEM),
        scratch_shapes=[pltpu.VMEM((ROWS_DEV, E), F32), pltpu.VMEM((TOUCH + 32, E + LANES), F32),
                        pltpu.VMEM((TOUCH, E), F32),
                        pltpu.VMEM((TOUCH, LANES), F32), pltpu.VMEM((TOUCH, LANES), F32),
                        pltpu.SemaphoreType.DMA((ROWS_DEV // TILE + 1,)),
                        pltpu.SemaphoreType.DMA((ROWS_DEV // TILE,))],
        compiler_params=PARAMS,
        name="update",
    )(plan, natural, in_hbm(table), in_hbm(listed), rows, *chunks)


def z_pairs(k):
    return [(z * NX + x, ((z + k) % NZ) * NX + x) for z in range(NZ) for x in range(NX)]


def x_pairs(k):
    return [(z * NX + x, z * NX + (x + k) % NX) for z in range(NZ) for x in range(NX)]


def y_pairs(k):
    return [(y * NC + c, ((y + k) % NY) * NC + c) for y in range(NY) for c in range(NC)]


C_PAIRS = [(y * NC + c, y * NC + 1 - c) for y in range(NY) for c in range(NC)]


def body(table, accum, pooled_grad, row_ids, bag_ids, touched):
    grp = lax.axis_index("grp")
    me = lax.axis_index("shard")
    y, c = grp // NC, grp % NC
    z, x = me // NX, me % NX

    def ordered(listed):
        halves = listed.reshape(NC, NY, QUART)
        halves = jnp.where(c == 0, halves[::-1], halves)
        doubled = jnp.concatenate([halves, halves], axis=1)
        return lax.dynamic_slice(doubled, (0, y, 0), (NC, NY, QUART)).reshape(TOUCH)

    own_list = touched.reshape(TOUCH)
    next_list = lax.ppermute(own_list, "shard", x_pairs(-1))
    far_lists = lax.ppermute(jnp.stack([own_list, next_list]), "shard", x_pairs(-2))
    lists = {0: ordered(own_list), 1: ordered(next_list),
             2: ordered(far_lists[0]), 3: ordered(far_lists[1])}
    stacked = jnp.stack([lists[k][HALF:] for k in ORDER])[:, :, None]
    rows = jnp.broadcast_to(stacked, (NX, HALF, LANES))
    all_rows = jnp.broadcast_to(lists[0][:, None], (TOUCH, LANES))
    order = lists[0].reshape(8, LANES)
    bounds = jnp.sum((own_list[None, :] < TILE * jnp.arange(16, dtype=I32)[:, None]).astype(I32), axis=1)
    turn = (y + jnp.arange(NY, dtype=I32)) % NY
    plan = jnp.concatenate([bounds, (1 - c) * NY + turn, c * NY + turn])

    packet = pack(row_ids.reshape(32, LANES), bag_ids.reshape(32, LANES),
                  pooled_grad.reshape(B_DEV, E))

    def swap(packets):
        return [lax.ppermute(p, "grp", C_PAIRS) for p in packets]

    def gather_of(packets, split):
        return gather(z.reshape(1), packets, split)

    up = down = packet
    other = swap([packet])
    gathered = [gather_of([packet], 0)]
    for _ in range(1, 4):
        up = lax.ppermute(up, "shard", z_pairs(1))
        down = lax.ppermute(down, "shard", z_pairs(-1))
        gathered.append(gather_of([up, down] + other, 0))
        other = swap([up, down])
    up = lax.ppermute(up, "shard", z_pairs(1))
    gathered.append(gather_of(other, 0))
    at = jnp.concatenate([(x + jnp.array(ORDER, I32)) % NX, (NX * z).reshape(1)])
    most = sums(at, 0, 1, gathered, rows, [])
    gathered.append(gather_of([up], 0))
    gathered.append(gather_of(swap([up]), 0))

    listed = listed_values(order, all_rows, accum.reshape(32, LANES), table)
    both = {}
    for base, ks in ((0, (2,)), (1, (1, 3)), (3, (0,))):
        found = sums(at, base, len(ks), gathered[5:] if base == 0 else gathered, rows,
                     [most] if base == 0 else [])
        for n, k in enumerate(ks):
            both[k] = found[n]
            if k:
                both[k] = lax.ppermute(both[k], "shard", x_pairs(k))
    total = both[0] + both[2] + both[1] + both[3]
    part = total[0:QUART]
    for j in (2, 1, 3):
        part = part + lax.ppermute(total[j * QUART:(j + 1) * QUART], "grp", y_pairs(j))
    mine = [part] + [lax.ppermute(part, "grp", y_pairs(-j)) for j in range(1, NY)]
    other = [lax.ppermute(m, "grp", C_PAIRS) for m in mine]
    new_table, new_accum = update(plan, own_list, table, listed, all_rows, other + mine)
    return (new_table, new_accum.reshape(ROWS_DEV))


def solution(mesh):
    return jax.shard_map(
        body,
        mesh=mesh,
        in_specs=(
            P("shard", None),
            P("shard"),
            P("grp", "shard", None, None),
            P("grp", "shard", None),
            P("grp", "shard", None),
            P("shard", None),
        ),
        out_specs=(P("shard", None), P("shard")),
        check_vma=False,
    )
```

```python
import jax
import jax.numpy as jnp
from jax import lax
from jax.experimental import pallas as pl
from jax.experimental.pallas import tpu as pltpu
from jax.sharding import PartitionSpec as P


E = 256
ROWS_DEV = 4096
TOUCH = 1024
HALF = TOUCH // 2
QUART = TOUCH // 8
TILE = 512
LOOK = 4096
B_DEV = 512
LANES = 128
BLOCKS = 64
WIDTH = B_DEV + LANES
NZ, NX, NY, NC = 8, 4, 4, 2
F32 = jnp.float32
BF16 = jnp.bfloat16
I32 = jnp.int32
NT = (((1,), (1,)), ((), ()))
TN = (((0,), (0,)), ((), ()))
ORDER = (2, 1, 3, 0)
SMEM = pl.BlockSpec(memory_space=pltpu.SMEM)
VMEM = pl.BlockSpec(memory_space=pltpu.VMEM)
HBM = pl.BlockSpec(memory_space=pltpu.HBM)
PARAMS = pltpu.CompilerParams(vmem_limit_bytes=14 << 20)


def iota(shape, dim):
    return lax.broadcasted_iota(I32, shape, dim)


def one_hot(mask):
    return jnp.where(mask, 1.0, 0.0).astype(BF16)


def in_hbm(array):
    return pltpu.with_memory_space_constraint(array, pltpu.HBM)


def pack_kernel(ids_hbm, bags_hbm, g_hbm, out_ref, a_ref, b_ref, o_ref, ids_ref, bags_ref, g_ref, sem):
    loads = [pltpu.make_async_copy(src, dst, sem.at[n])
             for n, (src, dst) in enumerate(((ids_hbm, ids_ref), (bags_hbm, bags_ref), (g_hbm, g_ref)))]
    for load in loads:
        load.start()
    for load in loads:
        load.wait()
    groups = LOOK // LANES
    ids = ids_ref[...]
    owner = ids >> 12
    owners = iota((32, LANES), 0)
    running = jnp.zeros((32, LANES), F32)
    for i in range(groups):
        hit = jnp.where(owner[i:i + 1, :] == owners, 1.0, 0.0)
        o_ref[i * 32:(i + 1) * 32, 0:LANES] = hit.astype(BF16)
        o_ref[i * 32:(i + 1) * 32, LANES:2 * LANES] = running.astype(BF16)
        running = running + hit
    before = one_hot(iota((LANES, LANES), 0) < iota((LANES, LANES), 1))
    weights = jnp.concatenate([before, jnp.ones((LANES, LANES), BF16)], axis=0)
    prefix = jnp.dot(o_ref[...], weights, preferred_element_type=F32)
    totals = jnp.concatenate([running, jnp.zeros((LANES - 32, LANES), F32)], axis=0)
    count_row = lax.dot_general(jnp.ones((8, LANES), BF16), totals.astype(BF16), NT,
                                preferred_element_type=F32).astype(I32)
    blocks_row = (count_row + (LANES - 1)) >> 7
    start_row = jnp.dot(blocks_row.astype(F32).astype(BF16), before, preferred_element_type=F32)
    start_col = jnp.sum(
        jnp.where(iota((32, LANES), 1) < iota((32, LANES), 0),
                  jnp.broadcast_to(blocks_row[0:1, :].astype(F32), (32, LANES)), 0.0),
        axis=1, keepdims=True) * float(LANES)
    start_all = jnp.broadcast_to(start_col, (32, LANES))
    for i in range(groups):
        hit = owner[i:i + 1, :] == owners
        pos = jnp.sum(jnp.where(hit, prefix[i * 32:(i + 1) * 32, :] + start_all, 0.0),
                      axis=0, keepdims=True).astype(I32)
        key = (((ids[i:i + 1, :] & (ROWS_DEV - 1)) << 9) | bags_ref[i:i + 1, :]) + 1
        at_hi = (pos >> 7) == iota((BLOCKS, LANES), 0)
        for piece in range(3):
            part = ((key >> (8 * piece)) & 255).astype(F32)
            a_ref[piece * BLOCKS:(piece + 1) * BLOCKS, i * LANES:(i + 1) * LANES] = jnp.where(
                at_hi, part, 0.0).astype(BF16)
        b_ref[:, i * LANES:(i + 1) * LANES] = one_hot((pos & (LANES - 1)) == iota((LANES, LANES), 0))
    placed = lax.dot_general(a_ref[...], b_ref[...], NT, preferred_element_type=F32)
    out_ref[0:3 * BLOCKS, B_DEV:WIDTH] = placed.astype(BF16)
    meta = jnp.where(iota((16, LANES), 0) < 8,
                     jnp.concatenate([start_row, start_row], axis=0),
                     jnp.concatenate([blocks_row, blocks_row], axis=0).astype(F32))
    out_ref[3 * BLOCKS:3 * BLOCKS + 16, B_DEV:WIDTH] = meta.astype(BF16)
    out_ref[3 * BLOCKS + 16:E, B_DEV:WIDTH] = jnp.zeros((E - 3 * BLOCKS - 16, LANES), BF16)
    eye = one_hot(iota((E, E), 0) == iota((E, E), 1))
    out_ref[:, 0:B_DEV] = lax.dot_general(eye, g_ref[...], NT, preferred_element_type=F32).astype(BF16)


def pack(ids, bags, grads):
    return pl.pallas_call(
        pack_kernel,
        out_shape=jax.ShapeDtypeStruct((E, WIDTH), BF16),
        in_specs=[HBM] * 3,
        scratch_shapes=[pltpu.VMEM((3 * BLOCKS, LOOK), BF16),
                        pltpu.VMEM((LANES, LOOK), BF16),
                        pltpu.VMEM((TOUCH, 2 * LANES), BF16),
                        pltpu.VMEM((32, LANES), I32), pltpu.VMEM((32, LANES), I32),
                        pltpu.VMEM((B_DEV, E), BF16), pltpu.SemaphoreType.DMA((3,))],
        cost_estimate=cost(4),
        compiler_params=PARAMS,
        name="pack",
    )(*[in_hbm(a) for a in (ids, bags, grads)])


def gather_kernel(z_ref, *refs, count, split):
    packets = refs[0:count + split]
    x_ref, k_ref, m_ref, all_ref, scalar_ref, sem = refs[count + split:]
    copies = []
    for d in range(count):
        cut = 128 if split and d == count - 1 else 0
        tail = packets[-1] if cut else packets[d]
        side = tail[3 * BLOCKS - cut:3 * BLOCKS + 16 - cut, B_DEV:WIDTH].astype(F32).astype(I32)
        m_ref[d] = jnp.where(iota((8, LANES), 0) == 0, side[0:8], side[8:16])
        copies.append(pltpu.make_async_copy(m_ref.at[d], scalar_ref.at[d], sem.at[d]))
        copies[d].start()
    for d in range(count):
        cut = 128 if split and d == count - 1 else 0
        tail = packets[-1] if cut else packets[d]
        low = packets[d][0:2 * BLOCKS, B_DEV:WIDTH].astype(F32).astype(I32)
        top = tail[2 * BLOCKS - cut:3 * BLOCKS - cut, B_DEV:WIDTH].astype(F32).astype(I32)
        all_ref[d, 0:BLOCKS] = (low[0:BLOCKS] + (low[BLOCKS:2 * BLOCKS] << 8) + (top << 16)) - 1
        all_ref[d, BLOCKS:BLOCKS + 16] = jnp.zeros((16, LANES), I32)
    for copy in copies:
        copy.wait()
    for d in range(count):
        parts = packets[d:] if split and d == count - 1 else packets[d:d + 1]
        first = scalar_ref[d, 0, NX * z_ref[0]]
        last = scalar_ref[d, 0, NX * z_ref[0] + NX - 1] + scalar_ref[d, 1, NX * z_ref[0] + NX - 1]
        k_ref[d] = all_ref[d, pl.ds(first, 16), :] >> 9

        def pair(j, _, d=d, first=first, parts=parts):
            lines = [all_ref[d, pl.ds(first + 2 * j + i, 1), :] & (B_DEV - 1) for i in range(2)]
            picks = jnp.concatenate([one_hot(line == iota((B_DEV, LANES), 0)) for line in lines], axis=1)
            rows = E // len(parts)
            for n, part in enumerate(parts):
                got = jnp.dot(part[:, 0:B_DEV], picks, preferred_element_type=F32).astype(BF16)
                for i in range(2):
                    x_ref[d, 2 * j + i, n * rows:(n + 1) * rows] = got[:, i * LANES:(i + 1) * LANES]
            return 0

        lax.fori_loop(0, (last - first + 1) >> 1, pair, 0)


def gather(z, packets, split):
    count = len(packets) - split
    return pl.pallas_call(
        lambda *refs: gather_kernel(*refs, count=count, split=split),
        out_shape=(jax.ShapeDtypeStruct((count, 16, E, LANES), BF16),
                   jax.ShapeDtypeStruct((count, 16, LANES), I32),
                   jax.ShapeDtypeStruct((count, 8, LANES), I32)),
        in_specs=[SMEM] + [VMEM] * len(packets),
        scratch_shapes=[pltpu.VMEM((count, BLOCKS + 16, LANES), I32), pltpu.SMEM((count, 8, LANES), I32),
                        pltpu.SemaphoreType.DMA((count,))],
        cost_estimate=cost(2 + count),
        compiler_params=PARAMS,
    )(z, *packets)


def sums_kernel(at_ref, *refs, counts, base, many, fresh):
    groups = len(counts)
    metas, xs, keys = refs[0:groups], refs[groups:2 * groups], refs[2 * groups:3 * groups]
    rows_ref = refs[3 * groups]
    out_ref, all_ref, k_ref = refs[-3:]
    for m in range(many):
        column = at_ref[base + m]
        filled = jnp.int32(0)
        for n in range(groups):
            for d in range(counts[n]):
                found = metas[n][d, 1, at_ref[4] + column]
                first = metas[n][d, 0, at_ref[4] + column] - metas[n][d, 0, at_ref[4]]

                def move(j, _, n=n, d=d, filled=filled, first=first):
                    all_ref[filled + j] = xs[n][d, first + j]
                    k_ref[pl.ds(filled + j, 1), :] = keys[n][d, pl.ds(first + j, 1), :]
                    return 0

                lax.fori_loop(0, found, move, 0)
                filled = filled + found
        rounds = (filled + 7) >> 3

        def blank(j, _):
            all_ref[j] = jnp.zeros((E, LANES), BF16)
            k_ref[pl.ds(j, 1), :] = jnp.full((1, LANES), -1, I32)
            return 0

        lax.fori_loop(filled, rounds * 8, blank, 0)
        out_ref[m] = jnp.zeros((HALF, E), F32) if fresh else refs[3 * groups + 1][m]

        def accumulate(r, _, m=m):
            wide = jnp.concatenate([all_ref[8 * r + j] for j in range(8)], axis=1)
            lines = [k_ref[pl.ds(8 * r + j, 1), :] for j in range(8)]
            mine = rows_ref[base + m]
            hits = jnp.concatenate([one_hot(mine == line) for line in lines], axis=1)
            out_ref[m] += lax.dot_general(hits, wide, NT, preferred_element_type=F32)
            return 0

        lax.fori_loop(0, rounds, accumulate, 0)


def cost(us):
    return pl.CostEstimate(flops=int(us * 6e8), bytes_accessed=int(us * 3e6), transcendentals=0)


def sums(at, base, many, gathered, rows, old):
    counts = tuple(g[0].shape[0] for g in gathered)
    total = sum(counts)
    return pl.pallas_call(
        lambda *refs: sums_kernel(*refs, counts=counts, base=base, many=many, fresh=not old),
        in_specs=[SMEM] * (1 + len(counts)) + [VMEM] * (2 * len(counts) + 1 + len(old)),
        scratch_shapes=[pltpu.VMEM((4 * total, E, LANES), BF16), pltpu.VMEM((4 * total, LANES), I32)],
        out_shape=jax.ShapeDtypeStruct((many, HALF, E), F32),
        cost_estimate=cost(2 * many),
        compiler_params=PARAMS,
    )(at, *[g[2] for g in gathered], *[g[0] for g in gathered], *[g[1] for g in gathered], rows, *old)


def listed_kernel(list_ref, rows_ref, accum_ref, table_ref, out_ref):
    rows = rows_ref[...]
    hi = jnp.where((rows >> 7) == iota((TOUCH, LANES), 1), 1.0, 0.0)
    padded = jnp.concatenate([accum_ref[...], jnp.zeros((LANES - 32, LANES), F32)], axis=0)
    line = jnp.dot(hi, padded, precision=lax.Precision.HIGHEST, preferred_element_type=F32)
    mine = jnp.where((rows & (LANES - 1)) == iota((TOUCH, LANES), 1), line, 0.0)
    out_ref[0:TOUCH, E:] = jnp.broadcast_to(jnp.sum(mine, axis=1, keepdims=True), (TOUCH, LANES))
    out_ref[TOUCH:, E:] = accum_ref[...]
    out_ref[TOUCH:, 0:E] = jnp.zeros((32, E), F32)

    def step(i, _):
        for j in range(16):
            row = list_ref[i >> 3, (i & 7) * 16 + j]
            out_ref[pl.ds(i * 16 + j, 1), 0:E] = table_ref[pl.ds(row, 1), :]
        return 0

    lax.fori_loop(0, TOUCH // 16, step, 0)


def listed_values(order, rows, accum, table):
    return pl.pallas_call(
        listed_kernel,
        out_shape=jax.ShapeDtypeStruct((TOUCH + 32, E + LANES), F32),
        in_specs=[SMEM, VMEM, VMEM, VMEM],
        cost_estimate=cost(6),
        compiler_params=PARAMS,
        name="listed_values",
    )(order, rows, accum, table)


def update_kernel(*refs):
    plan_ref, list_ref, table_ref, listed_hbm, rows_ref = refs[0:5]
    chunks = refs[5:13]
    table_out, accum_out, new_ref, listed_ref, u_ref, lhs_ref, rhs_ref, load_sem, store_sem = refs[13:]
    tiles = ROWS_DEV // TILE
    listed_load = pltpu.make_async_copy(listed_hbm, listed_ref, load_sem.at[tiles])
    listed_load.start()

    def load(b):
        at = pl.ds(b * TILE if isinstance(b, int) else pl.multiple_of(b * TILE, TILE), TILE)
        return pltpu.make_async_copy(table_ref.at[at], new_ref.at[at], load_sem.at[b])

    for b in range(tiles):
        load(b).start()
    lane = iota((QUART, LANES), 1)
    means = []
    for n in range(8):
        at = slice(n * QUART, (n + 1) * QUART)
        g = chunks[n][...]
        means.append(jnp.sum(g * g, axis=1, keepdims=True) * (1.0 / E))
        rows = rows_ref[at, :]
        lhs_ref[at, :] = jnp.where((rows >> 7) == lane, means[n], 0.0)
        rhs_ref[at, :] = jnp.where((rows & (LANES - 1)) == lane, 1.0, 0.0)
    listed_load.wait()
    for n in range(8):
        at = slice(n * QUART, (n + 1) * QUART)
        now = listed_ref[at, E:E + 1] + means[n]
        u_ref[pl.ds(pl.multiple_of(plan_ref[16 + n] * QUART, QUART), QUART), :] = (
            listed_ref[at, 0:E] - 0.5 * chunks[n][...] / (jnp.sqrt(now) + 1e-08))

    def put(n):
        new_ref[pl.ds(list_ref[n], 1), :] = u_ref[pl.ds(n, 1), :]

    def store(b):
        at = pl.ds(b * TILE if isinstance(b, int) else pl.multiple_of(b * TILE, TILE), TILE)
        return pltpu.make_async_copy(new_ref.at[at], table_out.at[at], store_sem.at[b])

    def tile(b, _):
        first, last = plan_ref[b], plan_ref[b + 1]
        low, high = (first + 7) >> 3, last >> 3

        def step(i, _):
            block = u_ref[pl.ds(pl.multiple_of(i * 8, 8), 8), :]
            for j in range(8):
                new_ref[pl.ds(list_ref[i * 8 + j], 1), :] = block[j:j + 1, :]
            return 0

        load(b).wait()
        lax.fori_loop(first, jnp.minimum(low * 8, last), lambda n, _: (put(n), 0)[1], 0)
        lax.fori_loop(low, high, step, 0)
        lax.fori_loop(jnp.maximum(high, low) * 8, last, lambda n, _: (put(n), 0)[1], 0)
        store(b).start()
        return 0

    lax.fori_loop(0, ROWS_DEV // TILE, tile, 0)
    added = lax.dot_general(lhs_ref[...], rhs_ref[...], TN, precision=lax.Precision.HIGHEST,
                            preferred_element_type=F32)
    accum_out[...] = listed_ref[TOUCH:, E:] + added[0:32, :]
    for b in range(ROWS_DEV // TILE):
        store(b).wait()


def update(plan, natural, table, listed, rows, chunks):
    return pl.pallas_call(
        update_kernel,
        out_shape=(jax.ShapeDtypeStruct((ROWS_DEV, E), F32), jax.ShapeDtypeStruct((32, LANES), F32)),
        in_specs=[SMEM, SMEM, HBM, HBM] + [VMEM] * 9,
        out_specs=(HBM, VMEM),
        scratch_shapes=[pltpu.VMEM((ROWS_DEV, E), F32), pltpu.VMEM((TOUCH + 32, E + LANES), F32),
                        pltpu.VMEM((TOUCH, E), F32),
                        pltpu.VMEM((TOUCH, LANES), F32), pltpu.VMEM((TOUCH, LANES), F32),
                        pltpu.SemaphoreType.DMA((ROWS_DEV // TILE + 1,)),
                        pltpu.SemaphoreType.DMA((ROWS_DEV // TILE,))],
        compiler_params=PARAMS,
        name="update",
    )(plan, natural, in_hbm(table), in_hbm(listed), rows, *chunks)


def z_pairs(k):
    return [(z * NX + x, ((z + k) % NZ) * NX + x) for z in range(NZ) for x in range(NX)]


def x_pairs(k):
    return [(z * NX + x, z * NX + (x + k) % NX) for z in range(NZ) for x in range(NX)]


def y_pairs(k):
    return [(y * NC + c, ((y + k) % NY) * NC + c) for y in range(NY) for c in range(NC)]


C_PAIRS = [(y * NC + c, y * NC + 1 - c) for y in range(NY) for c in range(NC)]


def body(table, accum, pooled_grad, row_ids, bag_ids, touched):
    grp = lax.axis_index("grp")
    me = lax.axis_index("shard")
    y, c = grp // NC, grp % NC
    z, x = me // NX, me % NX

    def ordered(listed):
        halves = listed.reshape(NC, NY, QUART)
        halves = jnp.where(c == 0, halves[::-1], halves)
        doubled = jnp.concatenate([halves, halves], axis=1)
        return lax.dynamic_slice(doubled, (0, y, 0), (NC, NY, QUART)).reshape(TOUCH)

    own_list = touched.reshape(TOUCH)
    lists = {0: ordered(own_list)}
    for k in range(1, NX):
        lists[k] = ordered(lax.ppermute(own_list, "shard", x_pairs(-k)))
    stacked = jnp.stack([lists[k][HALF:] for k in ORDER])[:, :, None]
    rows = jnp.broadcast_to(stacked, (NX, HALF, LANES))
    all_rows = jnp.broadcast_to(lists[0][:, None], (TOUCH, LANES))
    order = lists[0].reshape(8, LANES)
    bounds = jnp.sum((own_list[None, :] < TILE * jnp.arange(16, dtype=I32)[:, None]).astype(I32), axis=1)
    turn = (y + jnp.arange(NY, dtype=I32)) % NY
    plan = jnp.concatenate([bounds, (1 - c) * NY + turn, c * NY + turn])

    packet = pack(row_ids.reshape(32, LANES), bag_ids.reshape(32, LANES),
                  pooled_grad.reshape(B_DEV, E))

    def swap(packets):
        return [lax.ppermute(p, "grp", C_PAIRS) for p in packets]

    def gather_of(packets, split):
        return gather(z.reshape(1), packets, split)

    up = down = packet
    other = swap([packet])
    gathered = [gather_of([packet], 0)]
    for _ in range(1, 4):
        up = lax.ppermute(up, "shard", z_pairs(1))
        down = lax.ppermute(down, "shard", z_pairs(-1))
        gathered.append(gather_of([up, down] + other, 0))
        other = swap([up, down])
    up = lax.ppermute(up, "shard", z_pairs(1))
    gathered.append(gather_of(other, 0))
    at = jnp.concatenate([(x + jnp.array(ORDER, I32)) % NX, (NX * z).reshape(1)])
    most = sums(at, 0, 1, gathered, rows, [])
    gathered.append(gather_of([up], 0))
    gathered.append(gather_of(swap([up]), 0))

    listed = listed_values(order, all_rows, accum.reshape(32, LANES), table)
    both = {}
    for base, ks in ((0, (2,)), (1, (1, 3)), (3, (0,))):
        found = sums(at, base, len(ks), gathered[5:] if base == 0 else gathered, rows,
                     [most] if base == 0 else [])
        for n, k in enumerate(ks):
            both[k] = found[n]
            if k:
                both[k] = lax.ppermute(both[k], "shard", x_pairs(k))
    total = both[0] + both[2] + both[1] + both[3]
    part = total[0:QUART]
    for j in (2, 1, 3):
        part = part + lax.ppermute(total[j * QUART:(j + 1) * QUART], "grp", y_pairs(j))
    mine = [part] + [lax.ppermute(part, "grp", y_pairs(-j)) for j in range(1, NY)]
    other = [lax.ppermute(m, "grp", C_PAIRS) for m in mine]
    new_table, new_accum = update(plan, own_list, table, listed, all_rows, other + mine)
    return (new_table, new_accum.reshape(ROWS_DEV))


def solution(mesh):
    return jax.shard_map(
        body,
        mesh=mesh,
        in_specs=(
            P("shard", None),
            P("shard"),
            P("grp", "shard", None, None),
            P("grp", "shard", None),
            P("grp", "shard", None),
            P("shard", None),
        ),
        out_specs=(P("shard", None), P("shard")),
        check_vma=False,
    )
```
